256 devices in a mesh: lat: 16 (over y, x), kpt: 16 (over z, core).
Axes of the slice: x: 4, y: 4, z: 8, core: 2. Of those that a mesh axis runs over, the one named last changes fastest.
Arguments:
- coarse: bfloat16 [2, 16, 256, 12288], P(None, 'lat', 'kpt'), may hold values from -0.1875 to 0.1875
- rp_vectors: int32 [16, 3], P('lat'), may hold values from -4 to 4
- rp_weights: int32 [16], P('lat'), may hold values from 1 to 3
- re_vectors: int32 [256, 3], replicated, may hold values from -4 to 4
- re_weights: int32 [256], replicated, may hold values from 1 to 3
- q_points: float32 [2, 3], replicated, may hold values from 0 to 1
- k_points: float32 [1024, 3], P('kpt'), may hold values from 0 to 1
- modes_rot: bfloat16 [2, 2, 48, 48], replicated, may hold values from -0.625 to 0.625
- u_k: bfloat16 [2, 1024, 16, 16], P(None, 'kpt'), may hold values from -1 to 1
- u_kq: bfloat16 [2, 2, 1024, 16, 16], P(None, None, 'kpt'), may hold values from -1 to 1
- mask_k: int32 [1024, 16], P('kpt'), may hold values 0 or 1
- mask_kq: int32 [2, 1024, 16], P(None, 'kpt'), may hold values 0 or 1
Outputs:
- coupling: bfloat16 [2, 1024, 2, 12288], P(None, 'kpt', None, 'lat')
The draws below stay inside these ranges and needn't reach their ends.
All inputs are finite; a program needn't handle non-finite values. No bound on the sum of `mask_k` or of `mask_kq` on one device may be relied on, other than what follows from the above.
Results may differ from the reference program's by a relative error of at most 0.017.
Values may be sent and summed in bfloat16 or wider, within the bound.
No kernel may reach another device: no remote copies, remote signals or barrier semaphores. Data moves between devices by JAX's collectives and lax.ppermute only.
A program may use at most 64 MiB of HBM per device.

```python
import jax
import jax.numpy as jnp
from jax import lax

W = 16
M = 48
NQ = 2
NK = 1024
NRP = 16
NRE = 256


def touch_ends(entries, stream_key, least, largest):
    index_at = [jax.random.randint(jax.random.fold_in(stream_key, axis), (), 0, length) for axis, length in enumerate(entries.shape)]
    longest = entries.shape.index(max(entries.shape))
    neighbour = index_at[:longest] + [(index_at[longest] + 1) % entries.shape[longest]] + index_at[longest + 1:]
    return entries.at[tuple(index_at)].set(least).at[tuple(neighbour)].set(largest)


def steps_of(key, extent, cuts, least, top_value):
    def one(dim, shards_of):
        steps = jax.random.uniform(jax.random.fold_in(jax.random.fold_in(key, 6), dim), (shards_of,), jnp.float32, least / len(cuts), top_value / len(cuts))
        return jnp.repeat(jnp.exp(steps), extent[dim] // shards_of).reshape((-1,) + (1,) * (len(extent) - dim - 1))

    gain = one(*cuts[0])
    for cut in cuts[1:]:
        gain = gain * one(*cut)
    return gain


def scatter_about(stream_key, shape, scale, reach, split=(), dtype=jnp.bfloat16):
    drawn = jax.random.normal(stream_key, shape, jnp.float32) * scale
    if len(split) > 0:
        drawn = steps_of(stream_key, shape, split, -0.22, 0.18) * drawn
    return jnp.clip(drawn, min=-reach, max=reach).astype(dtype)


def setup_inputs(seed: int = 0) -> dict:
    arg_keys = jax.random.split(jax.random.key(seed), 13)
    return {
        "coarse": scatter_about(arg_keys[0], (2, NRP, NRE, M * W * W), (NRP * NRE // 4) ** -0.5, 0.1875, ((1, 16), (2, 16))),
        "rp_vectors": touch_ends(jax.random.randint(arg_keys[1], (NRP, 3), -4, 5), jax.random.fold_in(arg_keys[1], 1), -4, 4).astype(jnp.int32),
        "rp_weights": touch_ends(jax.random.randint(arg_keys[2], (NRP,), 1, 4), jax.random.fold_in(arg_keys[2], 1), 1, 3).astype(jnp.int32),
        "re_vectors": touch_ends(jax.random.randint(arg_keys[3], (NRE, 3), -4, 5), jax.random.fold_in(arg_keys[3], 1), -4, 4).astype(jnp.int32),
        "re_weights": touch_ends(jax.random.randint(arg_keys[4], (NRE,), 1, 4), jax.random.fold_in(arg_keys[4], 1), 1, 3).astype(jnp.int32),
        "q_points": jnp.clip(jax.random.uniform(arg_keys[5], (NQ, 3), jnp.float32, 0.0, 1.0), 0.0, 1.0),
        "k_points": jnp.clip(1.0 * jax.random.uniform(arg_keys[6], (NK, 3), jnp.float32) ** steps_of(arg_keys[6], (NK, 3), ((0, 16),), -0.2, 0.2), 0.0, 1.0),
        "modes_rot": scatter_about(arg_keys[7], (2, NQ, M, M), (2 * M) ** -0.5, 0.625),
        "u_k": scatter_about(arg_keys[8], (2, NK, W, W), (2 * W) ** -0.5, 1.0, ((1, 16),)),
        "u_kq": scatter_about(arg_keys[9], (2, NQ, NK, W, W), (2 * W) ** -0.5, 1.0, ((2, 16),)),
        "mask_k": touch_ends((jax.random.randint(arg_keys[10], (NK, W), 0, 4) < 3).astype(jnp.int32), jax.random.fold_in(arg_keys[10], 1), 0, 1),
        "mask_kq": touch_ends((jax.random.randint(arg_keys[11], (NQ, NK, W), 0, 4) < 3).astype(jnp.int32), jax.random.fold_in(arg_keys[11], 1), 0, 1),
    }


two_pi = 6.283185307179586


def phases(points, vectors, weights):
    cells = vectors.astype(jnp.float32)
    argument = two_pi * (points[:, 0:1] * cells[None, :, 0] + points[:, 1:2] * cells[None, :, 1] + points[:, 2:3] * cells[None, :, 2])
    inverse = 1.0 / weights.astype(jnp.float32)
    return (jnp.cos(argument) * inverse).astype(jnp.bfloat16), (jnp.sin(argument) * inverse).astype(jnp.bfloat16)


def reference(coarse, rp_vectors, rp_weights, re_vectors, re_weights, q_points, k_points, modes_rot, u_k, u_kq, mask_k, mask_kq):
    high = lax.Precision.HIGHEST
    phase_real, phase_imag = phases(q_points, rp_vectors, rp_weights)
    flat_real = coarse[0].reshape(NRP, NRE * M * W * W)
    flat_imag = coarse[1].reshape(NRP, NRE * M * W * W)
    part_real = jnp.dot(phase_real, flat_real, preferred_element_type=jnp.float32) - jnp.dot(phase_imag, flat_imag, preferred_element_type=jnp.float32)
    part_imag = jnp.dot(phase_real, flat_imag, preferred_element_type=jnp.float32) + jnp.dot(phase_imag, flat_real, preferred_element_type=jnp.float32)
    on_q = jnp.stack([part_real, part_imag]).astype(jnp.bfloat16)
    values = lax.optimization_barrier(on_q).astype(jnp.float32).reshape(2, NQ, NRE, M, W * W)
    eigen = modes_rot.astype(jnp.float32)
    br = jnp.einsum("qmn,qrmx->qrnx", eigen[0], values[0], precision=high) - jnp.einsum("qmn,qrmx->qrnx", eigen[1], values[1], precision=high)
    bi = jnp.einsum("qmn,qrmx->qrnx", eigen[0], values[1], precision=high) + jnp.einsum("qmn,qrmx->qrnx", eigen[1], values[0], precision=high)
    branch = jnp.stack([br, bi]).reshape(2, NQ, NRE, M * W * W).astype(jnp.bfloat16)
    kreal, kimag = phases(k_points, re_vectors, re_weights)
    kreal = kreal.astype(jnp.float32)
    kimag = kimag.astype(jnp.float32)
    grid = lax.optimization_barrier(branch).astype(jnp.float32)
    er = jnp.einsum("kr,qrx->kqx", kreal, grid[0], precision=high) - jnp.einsum("kr,qrx->kqx", kimag, grid[1], precision=high)
    ei = jnp.einsum("kr,qrx->kqx", kreal, grid[1], precision=high) + jnp.einsum("kr,qrx->kqx", kimag, grid[0], precision=high)
    bloch = jnp.stack([er, ei]).astype(jnp.bfloat16)
    field = lax.optimization_barrier(bloch).astype(jnp.float32).reshape(2, NK, NQ, M, W, W)
    right = u_k.astype(jnp.float32)
    left = u_kq.astype(jnp.float32)
    tr = jnp.einsum("kqmab,kbn->kqman", field[0], right[0], precision=high) - jnp.einsum("kqmab,kbn->kqman", field[1], right[1], precision=high)
    ti = jnp.einsum("kqmab,kbn->kqman", field[0], right[1], precision=high) + jnp.einsum("kqmab,kbn->kqman", field[1], right[0], precision=high)
    half = lax.optimization_barrier(jnp.stack([tr, ti]).astype(jnp.bfloat16)).astype(jnp.float32)
    tr = half[0]
    ti = half[1]
    outr = jnp.einsum("qkac,kqman->kqmcn", left[0], tr, precision=high) + jnp.einsum("qkac,kqman->kqmcn", left[1], ti, precision=high)
    outi = jnp.einsum("qkac,kqman->kqmcn", left[0], ti, precision=high) - jnp.einsum("qkac,kqman->kqmcn", left[1], tr, precision=high)
    window = jnp.transpose(mask_kq.astype(jnp.float32), (1, 0, 2))[:, :, None, :, None] * mask_k.astype(jnp.float32)[:, None, None, None, :]
    result = jnp.stack([outr * window, outi * window])
    return result.reshape(2, NK, NQ, M * W * W).astype(jnp.bfloat16)
```

```python
import jax
import jax.numpy as jnp
from jax import lax
from jax.experimental import pallas as pl
from jax.experimental.pallas import tpu as pltpu
from jax.sharding import PartitionSpec as P

two_pi = 6.283185307179586
f32 = jnp.float32
bf16 = jnp.bfloat16

MODES = 48
BANDS = 16
CELLS = 16
LAT = 16
NQ = 2
KPTS = 64
PER = MODES // LAT
LANES = PER * BANDS * BANDS
STRIDE_S = 2 * MODES
ROWS = NQ * 2 * CELLS


def rotate_body(qp_ref, rv_ref, rw_ref, rot_ref, coarse_ref, out_ref, mat_ref, s_ref, o_ref):
    weight = 1.0 / jnp.full((8, 128), rw_ref[0], jnp.int32).astype(f32)
    for q in range(NQ):
        arg = two_pi * (
            qp_ref[q, 0] * rv_ref[0, 0].astype(f32)
            + qp_ref[q, 1] * rv_ref[0, 1].astype(f32)
            + qp_ref[q, 2] * rv_ref[0, 2].astype(f32)
        )
        angle = jnp.full((8, 128), arg, f32)
        pr = (jnp.cos(angle) * weight).astype(bf16).astype(f32)[0:1, 0:1]
        pi = (jnp.sin(angle) * weight).astype(bf16).astype(f32)[0:1, 0:1]
        rr = rot_ref[0, q].astype(f32)
        ri = rot_ref[1, q].astype(f32)
        cr = rr * pr - ri * pi
        ci = rr * pi + ri * pr
        top = jnp.concatenate([cr, -ci], axis=0)
        low = jnp.concatenate([ci, cr], axis=0)
        mat_ref[q * 96:q * 96 + 48, 0:96] = top.T
        mat_ref[q * 96 + 48:q * 96 + 96, 0:96] = low.T
    rows = []
    for g in range(2 * NQ):
        for j in range(PER):
            rows.append(mat_ref[pl.ds(g * 48 + j, LAT, stride=PER), :])
    mat = jnp.concatenate(rows, axis=0)[:, 0:96].astype(bf16)
    for part in range(2):
        for m in range(MODES):
            for h in range(2):
                at = (2 * m + h) * 128
                tile = coarse_ref[part, 0, :, at:at + 128].astype(f32)
                s_ref[h, pl.ds(part * MODES + m, CELLS, stride=STRIDE_S), :] = tile
    for e in range(CELLS):
        for h in range(2):
            block = s_ref[h, e * STRIDE_S:e * STRIDE_S + 96, :].astype(bf16)
            res = jnp.dot(mat, block, preferred_element_type=f32)
            for g in range(2 * NQ):
                for j in range(PER):
                    at = (g * PER + j) * LAT
                    o_ref[2 * j + h, pl.ds(g * CELLS + e, LAT, stride=ROWS), :] = res[at:at + LAT]
    for l in range(LAT):
        for t in range(2 * PER):
            out_ref[l, :, t * 128:(t + 1) * 128] = o_ref[t, l * ROWS:(l + 1) * ROWS, :].astype(bf16)


def sum_body(x_ref, out_ref):
    for r in range(0, ROWS, 16):
        acc = x_ref[0, r:r + 16, :].astype(f32)
        for p in range(1, LAT):
            acc = acc + x_ref[p, r:r + 16, :].astype(f32)
        out_ref[r:r + 16, :] = acc.astype(bf16)


def prep_body(at_ref, kp_ref, rv_ref, u_ref, uq_ref, mk_ref, mq_ref, ph_ref, uo_ref, lo_ref):
    z = at_ref[0]
    c = at_ref[1]
    lane = lax.broadcasted_iota(jnp.int32, (256, 512), 1)
    src = lax.broadcasted_iota(jnp.int32, (256, 512), 0)
    block = lane >> 5
    home = (((z - block) & 7) << 1) + (c ^ (block >> 3))
    cell = (home << 4) + (lane & 15)
    pick = jnp.where(src == cell, 1.0, 0.0).astype(bf16)
    vec = jnp.dot(rv_ref[...].astype(f32).astype(bf16), pick, preferred_element_type=f32)
    kp = kp_ref[...]
    arg = two_pi * (
        kp[:, 0:1] * vec[0:1, :] + kp[:, 1:2] * vec[1:2, :] + kp[:, 2:3] * vec[2:3, :]
    )
    inverse = 1.0 / vec[3:4, :]
    co = jnp.cos(arg) * inverse
    si = jnp.sin(arg) * inverse
    first = (lax.broadcasted_iota(jnp.int32, (KPTS, 512), 1) & 16) == 0
    ph_ref[0:KPTS, :] = jnp.where(first, co, -si).astype(bf16)
    ph_ref[KPTS:2 * KPTS, :] = jnp.where(first, si, co).astype(bf16)
    row = lax.broadcasted_iota(jnp.int32, (KPTS, 128), 0)
    col = lax.broadcasted_iota(jnp.int32, (KPTS, 128), 1)
    spread = jnp.where((col >> 1) == row, 1.0, 0.0).astype(bf16)
    row2 = lax.broadcasted_iota(jnp.int32, (128, 128), 0)
    col2 = lax.broadcasted_iota(jnp.int32, (128, 128), 1)
    place = jnp.where((((col2 & 1) << 6) + (col2 >> 1)) == row2, 1.0, 0.0).astype(bf16)
    dims = (((0,), (0,)), ((), ()))
    mk = lax.dot_general(mk_ref[...].astype(f32).astype(bf16), spread, dims, preferred_element_type=f32)
    mq = lax.dot_general(mq_ref[...].astype(f32).astype(bf16), place, dims, preferred_element_type=f32)
    for part in range(2):
        ut = lax.dot_general(u_ref[part], spread, dims, preferred_element_type=f32)
        lt = lax.dot_general(uq_ref[part], place, dims, preferred_element_type=f32)
        for b in range(BANDS):
            uo_ref[part, b] = ut[b * 16:(b + 1) * 16] * mk
            lo_ref[part, b] = lt[b * 16:(b + 1) * 16] * mq


def couple_body(*refs):
    xs = refs[:16]
    ph_ref, u_ref, l_ref, out_ref, y_ref, bl_ref, h_ref, r_ref = refs[16:]
    ph = ph_ref[...]
    for q in range(NQ):
        x = jnp.concatenate([r[q * 32:(q + 1) * 32, :] for r in xs], axis=0)
        t = jnp.dot(ph, x, preferred_element_type=f32)
        for part in range(2):
            for v in range(2 * PER):
                y_ref[part, v, pl.ds(q, KPTS, stride=2), :] = t[
                    part * KPTS:(part + 1) * KPTS, v * 128:(v + 1) * 128
                ]
    for part in range(2):
        for v in range(2 * PER):
            bl_ref[part, v * 128:(v + 1) * 128, :] = y_ref[part, v].T.astype(bf16).astype(f32)

    group = 4

    def first(i, _):
        base = i * group * BANDS
        accr = [jnp.zeros((16, 128), f32) for _ in range(group)]
        acci = [jnp.zeros((16, 128), f32) for _ in range(group)]
        for b in range(BANDS):
            ur = u_ref[0, b]
            ui = u_ref[1, b]
            for s in range(group):
                xr = bl_ref[0, pl.ds(base + s * BANDS + b, 1), :]
                xi = bl_ref[1, pl.ds(base + s * BANDS + b, 1), :]
                accr[s] = accr[s] + (xr * ur - xi * ui)
                acci[s] = acci[s] + (xr * ui + xi * ur)
        for s in range(group):
            h_ref[0, i * group + s] = accr[s].astype(bf16).astype(f32)
            h_ref[1, i * group + s] = acci[s].astype(bf16).astype(f32)
        return 0

    lax.fori_loop(0, PER * BANDS // group, first, 0)

    per = BANDS // group

    def second(i, _):
        n = i // per
        c0 = (i - n * per) * group
        accr = [jnp.zeros((16, 128), f32) for _ in range(group)]
        acci = [jnp.zeros((16, 128), f32) for _ in range(group)]
        for a in range(BANDS):
            hr = h_ref[0, n * BANDS + a]
            hi = h_ref[1, n * BANDS + a]
            for s in range(group):
                lr = l_ref[0, a, pl.ds(c0 + s, 1), :]
                li = l_ref[1, a, pl.ds(c0 + s, 1), :]
                accr[s] = accr[s] + (lr * hr + li * hi)
                acci[s] = acci[s] + (lr * hi - li * hr)
        for s in range(group):
            r_ref[0, i * group + s] = accr[s]
            r_ref[1, i * group + s] = acci[s]
        return 0

    lax.fori_loop(0, PER * per, second, 0)
    for part in range(2):
        for v in range(2 * PER):
            tile = r_ref[part, v * 8:(v + 1) * 8].reshape(128, 128).T
            out_ref[part, :, v * 128:(v + 1) * 128] = tile.astype(bf16)


def vmem():
    return pl.BlockSpec(memory_space=pltpu.VMEM)


def smem():
    return pl.BlockSpec(memory_space=pltpu.SMEM)


def params():
    return pltpu.CompilerParams(vmem_limit_bytes=40 << 20)


def per_device(
    coarse,
    rp_vectors,
    rp_weights,
    re_vectors,
    re_weights,
    q_points,
    k_points,
    modes_rot,
    u_k,
    u_kq,
    mask_k,
    mask_kq,
):
    rotated = pl.pallas_call(
        rotate_body,
        out_shape=jax.ShapeDtypeStruct((LAT, ROWS, LANES), bf16),
        in_specs=[smem(), smem(), smem(), vmem(), vmem()],
        out_specs=vmem(),
        scratch_shapes=[
            pltpu.VMEM((192, 128), f32),
            pltpu.VMEM((2, CELLS * STRIDE_S, 128), f32),
            pltpu.VMEM((2 * PER, LAT * ROWS, 128), f32),
        ],
        compiler_params=params(),
        name="rotate",
    )(q_points, rp_vectors, rp_weights, modes_rot, coarse)
    parts = lax.all_to_all(rotated, "lat", 0, 0, tiled=True)

    index = lax.axis_index("kpt")
    at = jnp.stack([index // 2, index % 2]).astype(jnp.int32)
    lattice = jnp.concatenate(
        [re_vectors.T, re_weights[None, :], jnp.zeros((4, re_weights.shape[0]), jnp.int32)], axis=0
    )
    phase, right, left = pl.pallas_call(
        prep_body,
        out_shape=(
            jax.ShapeDtypeStruct((2 * KPTS, 512), bf16),
            jax.ShapeDtypeStruct((2, BANDS, BANDS, 128), f32),
            jax.ShapeDtypeStruct((2, BANDS, BANDS, 128), f32),
        ),
        in_specs=[smem()] + [vmem()] * 6,
        out_specs=(vmem(),) * 3,
        compiler_params=params(),
        name="prep",
    )(
        at,
        k_points,
        lattice,
        u_k.reshape(2, KPTS, BANDS * BANDS),
        u_kq.reshape(2, NQ * KPTS, BANDS * BANDS),
        mask_k,
        mask_kq.reshape(NQ * KPTS, BANDS),
    )

    own = pl.pallas_call(
        sum_body,
        out_shape=jax.ShapeDtypeStruct((ROWS, LANES), bf16),
        in_specs=[vmem()],
        out_specs=vmem(),
        compiler_params=params(),
        name="add_up",
    )(parts)

    def shift(x, step):
        return lax.ppermute(x, "kpt", [(i, (i + 2 * step) % 16) for i in range(16)])

    def swap(x):
        return lax.ppermute(x, "kpt", [(i, i ^ 1) for i in range(16)])

    up = shift(own, 3)
    down = shift(own, -3)
    blocks = {0: own, 3: up, 5: down}
    blocks[1] = shift(own, 1)
    blocks[7] = shift(own, -1)
    blocks[4] = shift(up, 1)
    blocks[2] = shift(up, -1)
    blocks[6] = shift(down, 1)
    near = [blocks[i] for i in range(8)]
    far = [swap(x) for x in near]

    result = pl.pallas_call(
        couple_body,
        out_shape=jax.ShapeDtypeStruct((2, 2 * KPTS, LANES), bf16),
        in_specs=[vmem()] * 19,
        out_specs=vmem(),
        scratch_shapes=[
            pltpu.VMEM((2, 2 * PER, 128, 128), f32),
            pltpu.VMEM((2, LANES, 128), f32),
            pltpu.VMEM((2, PER * BANDS, BANDS, 128), f32),
            pltpu.VMEM((2, PER * BANDS, BANDS, 128), f32),
        ],
        compiler_params=params(),
        name="couple",
    )(*near, *far, phase, right, left)
    return result.reshape(2, KPTS, NQ, LANES)


def solution(mesh):
    placed = (
        P(None, "lat", "kpt", None),
        P("lat", None),
        P("lat"),
        P(),
        P(),
        P(),
        P("kpt", None),
        P(),
        P(None, "kpt", None, None),
        P(None, None, "kpt", None, None),
        P("kpt", None),
        P(None, "kpt", None),
    )
    return jax.shard_map(
        per_device,
        mesh=mesh,
        in_specs=placed,
        out_specs=P(None, "kpt", None, "lat"),
        check_vma=False,
    )
```

```python
import jax
import jax.numpy as jnp
from jax import lax
from jax.experimental import pallas as pl
from jax.experimental.pallas import tpu as pltpu
from jax.sharding import PartitionSpec as P

two_pi = 6.283185307179586
f32 = jnp.float32
bf16 = jnp.bfloat16

MODES = 48
BANDS = 16
CELLS = 16
LAT = 16
NQ = 2
KPTS = 64
PER = MODES // LAT
LANES = PER * BANDS * BANDS
STRIDE_S = 2 * MODES
ROWS = NQ * 2 * CELLS
CHUNKS = 4
CHUNK = MODES * BANDS * BANDS // CHUNKS


def rotate_body(
    qp_hbm, rv_hbm, rw_hbm, rot_hbm, coarse_hbm, out_ref,
    qp_ref, rv_ref, rw_ref, rot_ref, coarse_ref, mat_ref, s_ref, o_ref, sems,
):
    small = [
        pltpu.make_async_copy(src, dst, sems.at[i])
        for i, (src, dst) in enumerate(
            [(qp_hbm, qp_ref), (rv_hbm, rv_ref), (rw_hbm, rw_ref), (rot_hbm, rot_ref)]
        )
    ]
    large = []
    for part in range(2):
        for i in range(CHUNKS):
            lanes = pl.ds(i * CHUNK, CHUNK)
            large.append(
                pltpu.make_async_copy(
                    coarse_hbm.at[part, 0, :, lanes],
                    coarse_ref.at[part, :, lanes],
                    sems.at[4 + part * CHUNKS + i],
                )
            )
    for copy in small + large:
        copy.start()
    for copy in small:
        copy.wait()
    weight = 1.0 / jnp.full((8, 128), rw_ref[0, 0], jnp.int32).astype(f32)
    for q in range(NQ):
        arg = two_pi * (
            qp_ref[q, 0] * rv_ref[0, 0].astype(f32)
            + qp_ref[q, 1] * rv_ref[0, 1].astype(f32)
            + qp_ref[q, 2] * rv_ref[0, 2].astype(f32)
        )
        angle = jnp.full((8, 128), arg, f32)
        pr = (jnp.cos(angle) * weight).astype(bf16).astype(f32)[0:1, 0:1]
        pi = (jnp.sin(angle) * weight).astype(bf16).astype(f32)[0:1, 0:1]
        rr = rot_ref[0, q].astype(f32)
        ri = rot_ref[1, q].astype(f32)
        cr = rr * pr - ri * pi
        ci = rr * pi + ri * pr
        top = jnp.concatenate([cr, -ci], axis=0)
        low = jnp.concatenate([ci, cr], axis=0)
        mat_ref[q * 96:q * 96 + 48, 0:96] = top.T
        mat_ref[q * 96 + 48:q * 96 + 96, 0:96] = low.T
    rows = []
    for g in range(2 * NQ):
        for j in range(PER):
            rows.append(mat_ref[pl.ds(g * 48 + j, LAT, stride=PER), :])
    mat = jnp.concatenate(rows, axis=0)[:, 0:96].astype(bf16)
    for part in range(2):
        for m in range(MODES):
            if m * 256 % CHUNK == 0:
                large[part * CHUNKS + m * 256 // CHUNK].wait()
            for h in range(2):
                at = (2 * m + h) * 128
                tile = coarse_ref[part, :, at:at + 128].astype(f32)
                s_ref[h, pl.ds(part * MODES + m, CELLS, stride=STRIDE_S), :] = tile
    for e in range(CELLS):
        for h in range(2):
            block = s_ref[h, e * STRIDE_S:e * STRIDE_S + 96, :].astype(bf16)
            res = jnp.dot(mat, block, preferred_element_type=f32)
            for g in range(2 * NQ):
                for j in range(PER):
                    at = (g * PER + j) * LAT
                    o_ref[2 * j + h, pl.ds(g * CELLS + e, LAT, stride=ROWS), :] = res[at:at + LAT]
    for l in range(LAT):
        for t in range(2 * PER):
            out_ref[l, :, t * 128:(t + 1) * 128] = o_ref[t, l * ROWS:(l + 1) * ROWS, :].astype(bf16)


def sum_body(x_ref, out_ref):
    for r in range(0, ROWS, 16):
        acc = x_ref[0, r:r + 16, :].astype(f32)
        for p in range(1, LAT):
            acc = acc + x_ref[p, r:r + 16, :].astype(f32)
        out_ref[r:r + 16, :] = acc.astype(bf16)


def prep_body(at_ref, kp_ref, rv_ref, u_ref, uq_ref, mk_ref, mq_ref, ph_ref, uo_ref, lo_ref):
    z = at_ref[0]
    c = at_ref[1]
    lane = lax.broadcasted_iota(jnp.int32, (256, 512), 1)
    src = lax.broadcasted_iota(jnp.int32, (256, 512), 0)
    block = lane >> 5
    home = (((z - block) & 7) << 1) + (c ^ (block >> 3))
    cell = (home << 4) + (lane & 15)
    pick = jnp.where(src == cell, 1.0, 0.0).astype(bf16)
    vec = jnp.dot(rv_ref[...].astype(f32).astype(bf16), pick, preferred_element_type=f32)
    kp = kp_ref[...]
    arg = two_pi * (
        kp[:, 0:1] * vec[0:1, :] + kp[:, 1:2] * vec[1:2, :] + kp[:, 2:3] * vec[2:3, :]
    )
    inverse = 1.0 / vec[3:4, :]
    co = jnp.cos(arg) * inverse
    si = jnp.sin(arg) * inverse
    first = (lax.broadcasted_iota(jnp.int32, (KPTS, 512), 1) & 16) == 0
    ph_ref[0:KPTS, :] = jnp.where(first, co, -si).astype(bf16)
    ph_ref[KPTS:2 * KPTS, :] = jnp.where(first, si, co).astype(bf16)
    row = lax.broadcasted_iota(jnp.int32, (KPTS, 128), 0)
    col = lax.broadcasted_iota(jnp.int32, (KPTS, 128), 1)
    spread = jnp.where((col >> 1) == row, 1.0, 0.0).astype(bf16)
    row2 = lax.broadcasted_iota(jnp.int32, (128, 128), 0)
    col2 = lax.broadcasted_iota(jnp.int32, (128, 128), 1)
    place = jnp.where((((col2 & 1) << 6) + (col2 >> 1)) == row2, 1.0, 0.0).astype(bf16)
    dims = (((0,), (0,)), ((), ()))
    mk = lax.dot_general(mk_ref[...].astype(f32).astype(bf16), spread, dims, preferred_element_type=f32)
    mq = lax.dot_general(mq_ref[...].astype(f32).astype(bf16), place, dims, preferred_element_type=f32)
    for part in range(2):
        ut = lax.dot_general(u_ref[part], spread, dims, preferred_element_type=f32)
        lt = lax.dot_general(uq_ref[part], place, dims, preferred_element_type=f32)
        for b in range(BANDS):
            uo_ref[part, b] = ut[b * 16:(b + 1) * 16] * mk
            lo_ref[part, b] = lt[b * 16:(b + 1) * 16] * mq


def pack_body(own_ref, up_ref, down_ref, order_ref, three_ref, two_ref):
    for i, ref in enumerate((own_ref, up_ref, down_ref)):
        value = ref[...]
        three_ref[i * ROWS:(i + 1) * ROWS, :] = value
        if i < 2:
            two_ref[i * ROWS:(i + 1) * ROWS, :] = value


PLACE = ((0, 0), (1, 0), (2, 1), (0, 1), (1, 1), (0, 2), (1, 2), (2, 0))


def couple_body(*refs):
    ph_ref, u_ref, l_ref, out_ref, y_ref, bl_ref, h_ref, r_ref = refs[6:]
    ph = ph_ref[...]
    for q in range(NQ):
        x = jnp.concatenate(
            [
                refs[side * 3 + i][j * ROWS + q * 32:j * ROWS + (q + 1) * 32, :]
                for side in range(2)
                for i, j in PLACE
            ],
            axis=0,
        )
        t = jnp.dot(ph, x, preferred_element_type=f32)
        for part in range(2):
            for v in range(2 * PER):
                y_ref[part, v, pl.ds(q, KPTS, stride=2), :] = t[
                    part * KPTS:(part + 1) * KPTS, v * 128:(v + 1) * 128
                ]
    for part in range(2):
        for v in range(2 * PER):
            bl_ref[part, v * 128:(v + 1) * 128, :] = y_ref[part, v].T.astype(bf16).astype(f32)

    group = 4

    def first(i, _):
        base = i * group * BANDS
        accr = [jnp.zeros((16, 128), f32) for _ in range(group)]
        acci = [jnp.zeros((16, 128), f32) for _ in range(group)]
        for b in range(BANDS):
            ur = u_ref[0, b]
            ui = u_ref[1, b]
            for s in range(group):
                xr = bl_ref[0, pl.ds(base + s * BANDS + b, 1), :]
                xi = bl_ref[1, pl.ds(base + s * BANDS + b, 1), :]
                accr[s] = accr[s] + (xr * ur - xi * ui)
                acci[s] = acci[s] + (xr * ui + xi * ur)
        for s in range(group):
            h_ref[0, i * group + s] = accr[s].astype(bf16).astype(f32)
            h_ref[1, i * group + s] = acci[s].astype(bf16).astype(f32)
        return 0

    lax.fori_loop(0, PER * BANDS // group, first, 0)

    per = BANDS // group

    def second(i, _):
        n = i // per
        c0 = (i - n * per) * group
        accr = [jnp.zeros((16, 128), f32) for _ in range(group)]
        acci = [jnp.zeros((16, 128), f32) for _ in range(group)]
        for a in range(BANDS):
            hr = h_ref[0, n * BANDS + a]
            hi = h_ref[1, n * BANDS + a]
            for s in range(group):
                lr = l_ref[0, a, pl.ds(c0 + s, 1), :]
                li = l_ref[1, a, pl.ds(c0 + s, 1), :]
                accr[s] = accr[s] + (lr * hr + li * hi)
                acci[s] = acci[s] + (lr * hi - li * hr)
        for s in range(group):
            r_ref[0, i * group + s] = accr[s]
            r_ref[1, i * group + s] = acci[s]
        return 0

    lax.fori_loop(0, PER * per, second, 0)
    for part in range(2):
        for v in range(2 * PER):
            tile = r_ref[part, v * 8:(v + 1) * 8].reshape(128, 128).T
            out_ref[part, :, v * 128:(v + 1) * 128] = tile.astype(bf16)


def vmem():
    return pl.BlockSpec(memory_space=pltpu.VMEM)


def hbm():
    return pl.BlockSpec(memory_space=pltpu.HBM)


def smem():
    return pl.BlockSpec(memory_space=pltpu.SMEM)


def params():
    return pltpu.CompilerParams(vmem_limit_bytes=40 << 20)


def per_device(
    coarse,
    rp_vectors,
    rp_weights,
    re_vectors,
    re_weights,
    q_points,
    k_points,
    modes_rot,
    u_k,
    u_kq,
    mask_k,
    mask_kq,
):
    rotated = pl.pallas_call(
        rotate_body,
        out_shape=jax.ShapeDtypeStruct((LAT, ROWS, LANES), bf16),
        in_specs=[hbm()] * 5,
        out_specs=vmem(),
        scratch_shapes=[
            pltpu.SMEM((NQ, 3), f32),
            pltpu.SMEM((1, 3), jnp.int32),
            pltpu.SMEM((1, 1), jnp.int32),
            pltpu.VMEM((2, NQ, MODES, MODES), bf16),
            pltpu.VMEM((2, CELLS, MODES * BANDS * BANDS), bf16),
            pltpu.VMEM((192, 128), f32),
            pltpu.VMEM((2, CELLS * STRIDE_S, 128), f32),
            pltpu.VMEM((2 * PER, LAT * ROWS, 128), f32),
            pltpu.SemaphoreType.DMA((4 + 2 * CHUNKS,)),
        ],
        compiler_params=pltpu.CompilerParams(vmem_limit_bytes=63 << 20),
        name="rotate",
    )(q_points, rp_vectors, rp_weights[None, :], modes_rot, coarse)
    parts = lax.all_to_all(rotated, "lat", 0, 0, tiled=True)

    index = lax.axis_index("kpt")
    at = jnp.stack([index // 2, index % 2]).astype(jnp.int32)
    lattice = jnp.concatenate(
        [re_vectors.T, re_weights[None, :], jnp.zeros((4, re_weights.shape[0]), jnp.int32)], axis=0
    )
    phase, right, left = pl.pallas_call(
        prep_body,
        out_shape=(
            jax.ShapeDtypeStruct((2 * KPTS, 512), bf16),
            jax.ShapeDtypeStruct((2, BANDS, BANDS, 128), f32),
            jax.ShapeDtypeStruct((2, BANDS, BANDS, 128), f32),
        ),
        in_specs=[smem()] + [vmem()] * 6,
        out_specs=(vmem(),) * 3,
        compiler_params=params(),
        name="prep",
    )(
        at,
        k_points,
        lattice,
        u_k.reshape(2, KPTS, BANDS * BANDS),
        u_kq.reshape(2, NQ * KPTS, BANDS * BANDS),
        mask_k,
        mask_kq.reshape(NQ * KPTS, BANDS),
    )

    own = pl.pallas_call(
        sum_body,
        out_shape=jax.ShapeDtypeStruct((ROWS, LANES), bf16),
        in_specs=[vmem()],
        out_specs=vmem(),
        compiler_params=params(),
        name="add_up",
    )(parts)

    def shift(x, step):
        return lax.ppermute(x, "kpt", [(i, (i + 2 * step) % 16) for i in range(16)])

    def swap(x):
        return lax.ppermute(x, "kpt", [(i, i ^ 1) for i in range(16)])

    up = shift(own, 3)
    down = shift(own, -3)
    packed, pair = pl.pallas_call(
        pack_body,
        out_shape=(
            jax.ShapeDtypeStruct((3 * ROWS, LANES), bf16),
            jax.ShapeDtypeStruct((2 * ROWS, LANES), bf16),
        ),
        in_specs=[vmem()] * 3 + [pl.BlockSpec(memory_space=pl.ANY)],
        out_specs=(vmem(), vmem()),
        compiler_params=params(),
        name="pack",
    )(own, up, down, phase)
    plus = shift(packed, 1)
    minus = shift(pair, -1)
    near = [packed, plus, minus]
    far = [swap(x) for x in near]

    result = pl.pallas_call(
        couple_body,
        out_shape=jax.ShapeDtypeStruct((2, 2 * KPTS, LANES), bf16),
        in_specs=[vmem()] * 9,
        out_specs=vmem(),
        scratch_shapes=[
            pltpu.VMEM((2, 2 * PER, 128, 128), f32),
            pltpu.VMEM((2, LANES, 128), f32),
            pltpu.VMEM((2, PER * BANDS, BANDS, 128), f32),
            pltpu.VMEM((2, PER * BANDS, BANDS, 128), f32),
        ],
        compiler_params=params(),
        name="couple",
    )(*near, *far, phase, right, left)
    return result.reshape(2, KPTS, NQ, LANES)


def solution(mesh):
    placed = (
        P(None, "lat", "kpt", None),
        P("lat", None),
        P("lat"),
        P(),
        P(),
        P(),
        P("kpt", None),
        P(),
        P(None, "kpt", None, None),
        P(None, None, "kpt", None, None),
        P("kpt", None),
        P(None, "kpt", None),
    )
    return jax.shard_map(
        per_device,
        mesh=mesh,
        in_specs=placed,
        out_specs=P(None, "kpt", None, "lat"),
        check_vma=False,
    )
```

```python
import functools

import jax
import jax.numpy as jnp
from jax import lax
from jax.experimental import pallas as pl
from jax.experimental.pallas import tpu as pltpu
from jax.sharding import PartitionSpec as P

two_pi = 6.283185307179586
f32 = jnp.float32
bf16 = jnp.bfloat16

MODES = 48
BANDS = 16
CELLS = 16
LAT = 16
NQ = 2
KPTS = 64
PER = MODES // LAT
LANES = PER * BANDS * BANDS
STRIDE_S = 2 * MODES
ROWS = 2 * CELLS
CHUNKS = 4
CHUNK = MODES * BANDS * BANDS // CHUNKS


def rotate_body(
    qp_hbm, rv_hbm, rw_hbm, rot_hbm, coarse_hbm, order_ref, out_ref,
    qp_ref, rv_ref, rw_ref, rot_ref, coarse_ref, mat_ref, s_ref, o_ref, sems, *, q,
):
    small = [
        pltpu.make_async_copy(src, dst, sems.at[i])
        for i, (src, dst) in enumerate(
            [(qp_hbm, qp_ref), (rv_hbm, rv_ref), (rw_hbm, rw_ref), (rot_hbm, rot_ref)]
        )
    ]
    large = []
    for part in range(2):
        for i in range(CHUNKS):
            lanes = pl.ds(i * CHUNK, CHUNK)
            large.append(
                pltpu.make_async_copy(
                    coarse_hbm.at[part, 0, :, lanes],
                    coarse_ref.at[part, :, lanes],
                    sems.at[4 + part * CHUNKS + i],
                )
            )
    for copy in small + large:
        copy.start()
    for copy in small:
        copy.wait()
    weight = 1.0 / jnp.full((8, 128), rw_ref[0, 0], jnp.int32).astype(f32)
    arg = two_pi * (
        qp_ref[q, 0] * rv_ref[0, 0].astype(f32)
        + qp_ref[q, 1] * rv_ref[0, 1].astype(f32)
        + qp_ref[q, 2] * rv_ref[0, 2].astype(f32)
    )
    angle = jnp.full((8, 128), arg, f32)
    pr = (jnp.cos(angle) * weight).astype(bf16).astype(f32)[0:1, 0:1]
    pi = (jnp.sin(angle) * weight).astype(bf16).astype(f32)[0:1, 0:1]
    rr = rot_ref[0, q].astype(f32)
    ri = rot_ref[1, q].astype(f32)
    cr = rr * pr - ri * pi
    ci = rr * pi + ri * pr
    mat_ref[0:48, 0:96] = jnp.concatenate([cr, -ci], axis=0).T
    mat_ref[48:96, 0:96] = jnp.concatenate([ci, cr], axis=0).T
    rows = []
    for g in range(2):
        for j in range(PER):
            rows.append(mat_ref[pl.ds(g * 48 + j, LAT, stride=PER), :])
    mat = jnp.concatenate(rows, axis=0)[:, 0:96].astype(bf16)
    for part in range(2):
        for m in range(MODES):
            if m * 256 % CHUNK == 0:
                large[part * CHUNKS + m * 256 // CHUNK].wait()
            for h in range(2):
                at = (2 * m + h) * 128
                tile = coarse_ref[part, :, at:at + 128].astype(f32)
                s_ref[h, pl.ds(part * MODES + m, CELLS, stride=STRIDE_S), :] = tile
    for e in range(CELLS):
        for h in range(2):
            block = s_ref[h, e * STRIDE_S:e * STRIDE_S + 96, :].astype(bf16)
            res = jnp.dot(mat, block, preferred_element_type=f32)
            for g in range(2):
                for j in range(PER):
                    at = (g * PER + j) * LAT
                    o_ref[2 * j + h, pl.ds(g * CELLS + e, LAT, stride=ROWS), :] = res[at:at + LAT]
    for l in range(LAT):
        for t in range(2 * PER):
            out_ref[l, :, t * 128:(t + 1) * 128] = o_ref[t, l * ROWS:(l + 1) * ROWS, :].astype(bf16)


def sum_body(x_ref, *refs):
    out_ref = refs[-1]
    for r in range(0, ROWS, 16):
        acc = x_ref[0, r:r + 16, :].astype(f32)
        for p in range(1, LAT):
            acc = acc + x_ref[p, r:r + 16, :].astype(f32)
        out_ref[r:r + 16, :] = acc.astype(bf16)


def prep_body(at_ref, kp_ref, rv_ref, u_ref, uq_ref, mk_ref, mq_ref, ph_ref, uo_ref, lo_ref):
    z = at_ref[0]
    c = at_ref[1]
    lane = lax.broadcasted_iota(jnp.int32, (256, 512), 1)
    src = lax.broadcasted_iota(jnp.int32, (256, 512), 0)
    block = lane >> 5
    home = (((z - block) & 7) << 1) + (c ^ (block >> 3))
    cell = (home << 4) + (lane & 15)
    pick = jnp.where(src == cell, 1.0, 0.0).astype(bf16)
    vec = jnp.dot(rv_ref[...].astype(f32).astype(bf16), pick, preferred_element_type=f32)
    kp = kp_ref[...]
    arg = two_pi * (
        kp[:, 0:1] * vec[0:1, :] + kp[:, 1:2] * vec[1:2, :] + kp[:, 2:3] * vec[2:3, :]
    )
    inverse = 1.0 / vec[3:4, :]
    co = jnp.cos(arg) * inverse
    si = jnp.sin(arg) * inverse
    first = (lax.broadcasted_iota(jnp.int32, (KPTS, 512), 1) & 16) == 0
    ph_ref[0:KPTS, :] = jnp.where(first, co, -si).astype(bf16)
    ph_ref[KPTS:2 * KPTS, :] = jnp.where(first, si, co).astype(bf16)
    row = lax.broadcasted_iota(jnp.int32, (KPTS, 128), 0)
    col = lax.broadcasted_iota(jnp.int32, (KPTS, 128), 1)
    spread = jnp.where((col >> 1) == row, 1.0, 0.0).astype(bf16)
    row2 = lax.broadcasted_iota(jnp.int32, (128, 128), 0)
    col2 = lax.broadcasted_iota(jnp.int32, (128, 128), 1)
    place = jnp.where((((col2 & 1) << 6) + (col2 >> 1)) == row2, 1.0, 0.0).astype(bf16)
    dims = (((0,), (0,)), ((), ()))
    mk = lax.dot_general(mk_ref[...].astype(f32).astype(bf16), spread, dims, preferred_element_type=f32)
    mq = lax.dot_general(mq_ref[...].astype(f32).astype(bf16), place, dims, preferred_element_type=f32)
    for part in range(2):
        ut = lax.dot_general(u_ref[part], spread, dims, preferred_element_type=f32)
        lt = lax.dot_general(uq_ref[part], place, dims, preferred_element_type=f32)
        for b in range(BANDS):
            uo_ref[part, b] = ut[b * 16:(b + 1) * 16] * mk
            lo_ref[part, b] = lt[b * 16:(b + 1) * 16] * mq


def pack_body(own_ref, up_ref, down_ref, order_ref, three_ref, two_ref):
    for i, ref in enumerate((own_ref, up_ref, down_ref)):
        value = ref[...]
        three_ref[i * ROWS:(i + 1) * ROWS, :] = value
        if i < 2:
            two_ref[i * ROWS:(i + 1) * ROWS, :] = value


PLACE = ((0, 0), (1, 0), (2, 1), (0, 1), (1, 1), (0, 2), (1, 2), (2, 0))


def couple_body(*refs):
    ph_ref, u_ref, l_ref, out_ref, y_ref, bl_ref, h_ref, r_ref = refs[12:]
    ph = ph_ref[...]
    for q in range(NQ):
        x = jnp.concatenate(
            [
                refs[q * 6 + side * 3 + i][j * ROWS:(j + 1) * ROWS, :]
                for side in range(2)
                for i, j in PLACE
            ],
            axis=0,
        )
        t = jnp.dot(ph, x, preferred_element_type=f32)
        for part in range(2):
            for v in range(2 * PER):
                y_ref[part, v, pl.ds(q, KPTS, stride=2), :] = t[
                    part * KPTS:(part + 1) * KPTS, v * 128:(v + 1) * 128
                ]
    for part in range(2):
        for v in range(2 * PER):
            bl_ref[part, v * 128:(v + 1) * 128, :] = y_ref[part, v].T.astype(bf16).astype(f32)

    group = 4

    def first(i, _):
        base = i * group * BANDS
        accr = [jnp.zeros((16, 128), f32) for _ in range(group)]
        acci = [jnp.zeros((16, 128), f32) for _ in range(group)]
        for b in range(BANDS):
            ur = u_ref[0, b]
            ui = u_ref[1, b]
            for s in range(group):
                xr = bl_ref[0, pl.ds(base + s * BANDS + b, 1), :]
                xi = bl_ref[1, pl.ds(base + s * BANDS + b, 1), :]
                accr[s] = accr[s] + (xr * ur - xi * ui)
                acci[s] = acci[s] + (xr * ui + xi * ur)
        for s in range(group):
            h_ref[0, i * group + s] = accr[s].astype(bf16).astype(f32)
            h_ref[1, i * group + s] = acci[s].astype(bf16).astype(f32)
        return 0

    lax.fori_loop(0, PER * BANDS // group, first, 0)

    per = BANDS // group

    def second(i, _):
        n = i // per
        c0 = (i - n * per) * group
        accr = [jnp.zeros((16, 128), f32) for _ in range(group)]
        acci = [jnp.zeros((16, 128), f32) for _ in range(group)]
        for a in range(BANDS):
            hr = h_ref[0, n * BANDS + a]
            hi = h_ref[1, n * BANDS + a]
            for s in range(group):
                lr = l_ref[0, a, pl.ds(c0 + s, 1), :]
                li = l_ref[1, a, pl.ds(c0 + s, 1), :]
                accr[s] = accr[s] + (lr * hr + li * hi)
                acci[s] = acci[s] + (lr * hi - li * hr)
        for s in range(group):
            r_ref[0, i * group + s] = accr[s]
            r_ref[1, i * group + s] = acci[s]
        return 0

    lax.fori_loop(0, PER * per, second, 0)
    for part in range(2):
        for v in range(2 * PER):
            tile = r_ref[part, v * 8:(v + 1) * 8].reshape(128, 128).T
            out_ref[part, :, v * 128:(v + 1) * 128] = tile.astype(bf16)


def vmem():
    return pl.BlockSpec(memory_space=pltpu.VMEM)


def hbm():
    return pl.BlockSpec(memory_space=pltpu.HBM)


def smem():
    return pl.BlockSpec(memory_space=pltpu.SMEM)


def params():
    return pltpu.CompilerParams(vmem_limit_bytes=40 << 20)


def rotate(q, *args):
    return pl.pallas_call(
        functools.partial(rotate_body, q=q),
        out_shape=jax.ShapeDtypeStruct((LAT, ROWS, LANES), bf16),
        in_specs=[hbm()] * 5 + [pl.BlockSpec(memory_space=pl.ANY)],
        out_specs=vmem(),
        scratch_shapes=[
            pltpu.SMEM((NQ, 3), f32),
            pltpu.SMEM((1, 3), jnp.int32),
            pltpu.SMEM((1, 1), jnp.int32),
            pltpu.VMEM((2, NQ, MODES, MODES), bf16),
            pltpu.VMEM((2, CELLS, MODES * BANDS * BANDS), bf16),
            pltpu.VMEM((96, 128), f32),
            pltpu.VMEM((2, CELLS * STRIDE_S, 128), f32),
            pltpu.VMEM((2 * PER, LAT * ROWS, 128), f32),
            pltpu.SemaphoreType.DMA((4 + 2 * CHUNKS,)),
        ],
        compiler_params=pltpu.CompilerParams(vmem_limit_bytes=(63 if q == 0 else 40) << 20),
        name=f"rotate{q}",
    )(*args)


def add_up(parts, order):
    return pl.pallas_call(
        sum_body,
        out_shape=jax.ShapeDtypeStruct((ROWS, LANES), bf16),
        in_specs=[vmem()] + [pl.BlockSpec(memory_space=pl.ANY)] * len(order),
        out_specs=vmem(),
        compiler_params=params(),
        name="add_up",
    )(parts, *order)


def shift(x, step):
    return lax.ppermute(x, "kpt", [(i, (i + 2 * step) % 16) for i in range(16)])


def swap(x):
    return lax.ppermute(x, "kpt", [(i, i ^ 1) for i in range(16)])


def gather(own, order):
    packed, pair = pl.pallas_call(
        pack_body,
        out_shape=(
            jax.ShapeDtypeStruct((3 * ROWS, LANES), bf16),
            jax.ShapeDtypeStruct((2 * ROWS, LANES), bf16),
        ),
        in_specs=[vmem()] * 3 + [pl.BlockSpec(memory_space=pl.ANY)],
        out_specs=(vmem(), vmem()),
        compiler_params=params(),
        name="pack",
    )(own, shift(own, 3), shift(own, -3), order)
    near = [packed, shift(packed, 1), shift(pair, -1)]
    return near + [swap(x) for x in near]


def per_device(
    coarse,
    rp_vectors,
    rp_weights,
    re_vectors,
    re_weights,
    q_points,
    k_points,
    modes_rot,
    u_k,
    u_kq,
    mask_k,
    mask_kq,
):
    small = (q_points, rp_vectors, rp_weights[None, :], modes_rot)
    parts = []
    order = q_points
    for q in range(NQ):
        order = rotate(q, *small, coarse, order)
        parts.append(lax.all_to_all(order, "lat", 0, 0, tiled=True))

    index = lax.axis_index("kpt")
    at = jnp.stack([index // 2, index % 2]).astype(jnp.int32)
    lattice = jnp.concatenate(
        [re_vectors.T, re_weights[None, :], jnp.zeros((4, re_weights.shape[0]), jnp.int32)], axis=0
    )
    phase, right, left = pl.pallas_call(
        prep_body,
        out_shape=(
            jax.ShapeDtypeStruct((2 * KPTS, 512), bf16),
            jax.ShapeDtypeStruct((2, BANDS, BANDS, 128), f32),
            jax.ShapeDtypeStruct((2, BANDS, BANDS, 128), f32),
        ),
        in_specs=[smem()] + [vmem()] * 6,
        out_specs=(vmem(),) * 3,
        compiler_params=params(),
        name="prep",
    )(
        at,
        k_points,
        lattice,
        u_k.reshape(2, KPTS, BANDS * BANDS),
        u_kq.reshape(2, NQ * KPTS, BANDS * BANDS),
        mask_k,
        mask_kq.reshape(NQ * KPTS, BANDS),
    )

    spread = []
    for q in range(NQ):
        spread += gather(add_up(parts[q], spread), phase)

    result = pl.pallas_call(
        couple_body,
        out_shape=jax.ShapeDtypeStruct((2, 2 * KPTS, LANES), bf16),
        in_specs=[vmem()] * 15,
        out_specs=vmem(),
        scratch_shapes=[
            pltpu.VMEM((2, 2 * PER, 128, 128), f32),
            pltpu.VMEM((2, LANES, 128), f32),
            pltpu.VMEM((2, PER * BANDS, BANDS, 128), f32),
            pltpu.VMEM((2, PER * BANDS, BANDS, 128), f32),
        ],
        compiler_params=params(),
        name="couple",
    )(*spread, phase, right, left)
    return result.reshape(2, KPTS, NQ, LANES)


def solution(mesh):
    placed = (
        P(None, "lat", "kpt", None),
        P("lat", None),
        P("lat"),
        P(),
        P(),
        P(),
        P("kpt", None),
        P(),
        P(None, "kpt", None, None),
        P(None, None, "kpt", None, None),
        P("kpt", None),
        P(None, "kpt", None),
    )
    return jax.shard_map(
        per_device,
        mesh=mesh,
        in_specs=placed,
        out_specs=P(None, "kpt", None, "lat"),
        check_vma=False,
    )
```

```python
import jax
import jax.numpy as jnp
from jax import lax
from jax.experimental import pallas as pl
from jax.experimental.pallas import tpu as pltpu
from jax.sharding import PartitionSpec as P

two_pi = 6.283185307179586
f32 = jnp.float32
bf16 = jnp.bfloat16

MODES = 48
BANDS = 16
CELLS = 16
LAT = 16
ZED = 8
NQ = 2
KPTS = 64
PER = MODES // LAT
LANES = PER * BANDS * BANDS
STRIDE_S = 2 * MODES
SENT = 2 * MODES + 8
CHUNKS = 4
CHUNK = MODES * BANDS * BANDS // CHUNKS
SOURCES = ZED * LAT
WIDTH = PER * 128


def split_body(
    qp_hbm, rv_hbm, rw_hbm, coarse_hbm, out_ref, qp_ref, rv_ref, rw_ref, coarse_ref, s_ref, sems
):
    small = [
        pltpu.make_async_copy(src, dst, sems.at[i])
        for i, (src, dst) in enumerate([(qp_hbm, qp_ref), (rv_hbm, rv_ref), (rw_hbm, rw_ref)])
    ]
    large = []
    for part in range(2):
        for i in range(CHUNKS):
            lanes = pl.ds(i * CHUNK, CHUNK)
            large.append(
                pltpu.make_async_copy(
                    coarse_hbm.at[part, 0, :, lanes],
                    coarse_ref.at[part, :, lanes],
                    sems.at[3 + part * CHUNKS + i],
                )
            )
    for copy in large + small:
        copy.start()
    for part in range(2):
        for m in range(MODES):
            if m * 256 % CHUNK == 0:
                large[part * CHUNKS + m * 256 // CHUNK].wait()
            for h in range(2):
                at = (2 * m + h) * 128
                tile = coarse_ref[part, :, at:at + 128].astype(f32)
                s_ref[h, pl.ds(part * MODES + m, CELLS, stride=STRIDE_S), :] = tile
    for copy in small:
        copy.wait()
    weight = 1.0 / jnp.full((8, 128), rw_ref[0, 0], jnp.int32).astype(f32)
    rows = []
    for q in range(NQ):
        arg = two_pi * (
            qp_ref[q, 0] * rv_ref[0, 0].astype(f32)
            + qp_ref[q, 1] * rv_ref[0, 1].astype(f32)
            + qp_ref[q, 2] * rv_ref[0, 2].astype(f32)
        )
        angle = jnp.full((8, 128), arg, f32)
        rows += [jnp.cos(angle) * weight, jnp.sin(angle) * weight]
    line = lax.broadcasted_iota(jnp.int32, (8, 128), 0)
    phase = rows[3]
    for i in range(3):
        phase = jnp.where(line == i, rows[i], phase)
    phase = phase.astype(bf16)
    for e in range(CELLS):
        for h in range(2):
            lanes = slice(h * 128, (h + 1) * 128)
            out_ref[e, 0:96, lanes] = s_ref[h, e * STRIDE_S:e * STRIDE_S + 96, :].astype(bf16)
            out_ref[e, 96:SENT, lanes] = phase


def turn_body(rot_ref, mat_ref, t_ref):
    for q in range(NQ):
        rr = rot_ref[0, q].astype(f32)
        ri = rot_ref[1, q].astype(f32)
        t_ref[0:48, 0:96] = jnp.concatenate([rr, -ri], axis=0).T
        t_ref[48:96, 0:96] = jnp.concatenate([ri, rr], axis=0).T
        rows = []
        for g in range(2):
            for j in range(PER):
                rows.append(t_ref[pl.ds(g * 48 + j, LAT, stride=PER), :])
        mat_ref[q] = jnp.concatenate(rows, axis=0)[:, 0:96].astype(bf16)


def branch_body(x_ref, mat_ref, order_ref, out_ref, o_ref):
    for h in range(2):
        lanes = slice(h * 128, (h + 1) * 128)
        sums = [jnp.zeros((MODES, 128), f32) for _ in range(2 * NQ)]
        for p in range(LAT):
            xr = x_ref[p, 0:MODES, lanes].astype(f32)
            xi = x_ref[p, MODES:2 * MODES, lanes].astype(f32)
            phase = x_ref[p, 96:SENT, lanes].astype(f32)
            for q in range(NQ):
                pr = phase[2 * q:2 * q + 1]
                pi = phase[2 * q + 1:2 * q + 2]
                sums[2 * q] = sums[2 * q] + (pr * xr - pi * xi)
                sums[2 * q + 1] = sums[2 * q + 1] + (pr * xi + pi * xr)
        for q in range(NQ):
            on_q = jnp.concatenate([sums[2 * q], sums[2 * q + 1]], axis=0).astype(bf16)
            res = jnp.dot(mat_ref[q], on_q, preferred_element_type=f32)
            for g in range(2):
                for j in range(PER):
                    at = (g * PER + j) * LAT
                    o_ref[j, pl.ds(q * 4 + g * 2 + h, LAT, stride=8), :] = res[at:at + LAT]
    for j in range(PER):
        value = o_ref[j].reshape(LAT, 8, 128).astype(bf16)
        for z in range(ZED):
            out_ref[z * LAT:(z + 1) * LAT, :, j * 128:(j + 1) * 128] = value


def prep_body(core_ref, kp_ref, rv_ref, u_ref, uq_ref, mk_ref, mq_ref, ph_ref, uo_ref, lo_ref):
    c = core_ref[0]
    lane = lax.broadcasted_iota(jnp.int32, (256, 256), 1)
    src = lax.broadcasted_iota(jnp.int32, (256, 256), 0)
    home = (((lane >> 4) & 7) << 1) + (c ^ (lane >> 7))
    cell = (home << 4) + (lane & 15)
    pick = jnp.where(src == cell, 1.0, 0.0).astype(bf16)
    vec = jnp.dot(rv_ref[...].astype(f32).astype(bf16), pick, preferred_element_type=f32)
    kp = kp_ref[...]
    arg = two_pi * (
        kp[:, 0:1] * vec[0:1, :] + kp[:, 1:2] * vec[1:2, :] + kp[:, 2:3] * vec[2:3, :]
    )
    inverse = 1.0 / vec[3:4, :]
    both = jnp.concatenate([jnp.cos(arg) * inverse, jnp.sin(arg) * inverse], axis=0).astype(bf16)
    for piece in range(4):
        wide = lax.broadcasted_iota(jnp.int32, (256, 512), 1) + piece * 512
        deep = lax.broadcasted_iota(jnp.int32, (256, 512), 0)
        spread8 = jnp.where((wide >> 3) == deep, 1.0, 0.0).astype(bf16)
        grown = jnp.dot(both, spread8, preferred_element_type=f32)
        co = grown[0:KPTS]
        si = grown[KPTS:2 * KPTS]
        kind = lax.broadcasted_iota(jnp.int32, (KPTS, 512), 1) & 7
        real = (kind & 2) == 0
        values = (jnp.where(real, co, -si), jnp.where(real, si, co))
        for q in range(NQ):
            for h in range(2):
                mine = (kind & 5) == q * 4 + h
                for part in range(2):
                    at = ((q * 2 + h) * 2 + part) * KPTS
                    ph_ref[at:at + KPTS, piece * 512:(piece + 1) * 512] = jnp.where(
                        mine, values[part], 0.0
                    ).astype(bf16)
    row = lax.broadcasted_iota(jnp.int32, (KPTS, 128), 0)
    col = lax.broadcasted_iota(jnp.int32, (KPTS, 128), 1)
    spread = jnp.where((col >> 1) == row, 1.0, 0.0).astype(bf16)
    row2 = lax.broadcasted_iota(jnp.int32, (128, 128), 0)
    col2 = lax.broadcasted_iota(jnp.int32, (128, 128), 1)
    place = jnp.where((((col2 & 1) << 6) + (col2 >> 1)) == row2, 1.0, 0.0).astype(bf16)
    dims = (((0,), (0,)), ((), ()))
    mk = lax.dot_general(mk_ref[...].astype(f32).astype(bf16), spread, dims, preferred_element_type=f32)
    mq = lax.dot_general(mq_ref[...].astype(f32).astype(bf16), place, dims, preferred_element_type=f32)
    for part in range(2):
        ut = lax.dot_general(u_ref[part], spread, dims, preferred_element_type=f32)
        lt = lax.dot_general(uq_ref[part], place, dims, preferred_element_type=f32)
        for b in range(BANDS):
            uo_ref[part, b] = ut[b * 16:(b + 1) * 16] * mk
            lo_ref[part, b] = lt[b * 16:(b + 1) * 16] * mq


def couple_body(near_ref, far_ref, ph_ref, u_ref, l_ref, out_ref, y_ref, bl_ref, h_ref, r_ref):
    half = SOURCES * 8
    t = jnp.dot(
        ph_ref[:, 0:half], near_ref[...].reshape(half, WIDTH), preferred_element_type=f32
    ) + jnp.dot(
        ph_ref[:, half:2 * half], far_ref[...].reshape(half, WIDTH), preferred_element_type=f32
    )
    for q in range(NQ):
        for h in range(2):
            for part in range(2):
                at = ((q * 2 + h) * 2 + part) * KPTS
                for j in range(PER):
                    y_ref[part, 2 * j + h, pl.ds(q, KPTS, stride=2), :] = t[
                        at:at + KPTS, j * 128:(j + 1) * 128
                    ]
    for part in range(2):
        for v in range(2 * PER):
            bl_ref[part, v * 128:(v + 1) * 128, :] = y_ref[part, v].T.astype(bf16).astype(f32)

    group = 4

    def first(i, _):
        base = i * group * BANDS
        accr = [jnp.zeros((16, 128), f32) for _ in range(group)]
        acci = [jnp.zeros((16, 128), f32) for _ in range(group)]
        for b in range(BANDS):
            ur = u_ref[0, b]
            ui = u_ref[1, b]
            for s in range(group):
                xr = bl_ref[0, pl.ds(base + s * BANDS + b, 1), :]
                xi = bl_ref[1, pl.ds(base + s * BANDS + b, 1), :]
                accr[s] = accr[s] + (xr * ur - xi * ui)
                acci[s] = acci[s] + (xr * ui + xi * ur)
        for s in range(group):
            h_ref[0, i * group + s] = accr[s].astype(bf16).astype(f32)
            h_ref[1, i * group + s] = acci[s].astype(bf16).astype(f32)
        return 0

    lax.fori_loop(0, PER * BANDS // group, first, 0)

    per = BANDS // group

    def second(i, _):
        n = i // per
        c0 = (i - n * per) * group
        accr = [jnp.zeros((16, 128), f32) for _ in range(group)]
        acci = [jnp.zeros((16, 128), f32) for _ in range(group)]
        for a in range(BANDS):
            hr = h_ref[0, n * BANDS + a]
            hi = h_ref[1, n * BANDS + a]
            for s in range(group):
                lr = l_ref[0, a, pl.ds(c0 + s, 1), :]
                li = l_ref[1, a, pl.ds(c0 + s, 1), :]
                accr[s] = accr[s] + (lr * hr + li * hi)
                acci[s] = acci[s] + (lr * hi - li * hr)
        for s in range(group):
            r_ref[0, i * group + s] = accr[s]
            r_ref[1, i * group + s] = acci[s]
        return 0

    lax.fori_loop(0, PER * per, second, 0)
    for part in range(2):
        for v in range(2 * PER):
            tile = r_ref[part, v * 8:(v + 1) * 8].reshape(128, 128).T
            out_ref[part, :, v * 128:(v + 1) * 128] = tile.astype(bf16)


def vmem():
    return pl.BlockSpec(memory_space=pltpu.VMEM)


def hbm():
    return pl.BlockSpec(memory_space=pltpu.HBM)


def smem():
    return pl.BlockSpec(memory_space=pltpu.SMEM)


def params(mib=40):
    return pltpu.CompilerParams(vmem_limit_bytes=mib << 20)


def per_device(
    coarse,
    rp_vectors,
    rp_weights,
    re_vectors,
    re_weights,
    q_points,
    k_points,
    modes_rot,
    u_k,
    u_kq,
    mask_k,
    mask_kq,
):
    cells = pl.pallas_call(
        split_body,
        out_shape=jax.ShapeDtypeStruct((CELLS, SENT, 256), bf16),
        in_specs=[hbm()] * 4,
        out_specs=vmem(),
        scratch_shapes=[
            pltpu.SMEM((NQ, 3), f32),
            pltpu.SMEM((1, 3), jnp.int32),
            pltpu.SMEM((1, 1), jnp.int32),
            pltpu.VMEM((2, CELLS, MODES * BANDS * BANDS), bf16),
            pltpu.VMEM((2, CELLS * STRIDE_S, 128), f32),
            pltpu.SemaphoreType.DMA((3 + 2 * CHUNKS,)),
        ],
        compiler_params=params(63),
        name="split",
    )(q_points, rp_vectors, rp_weights[None, :], coarse)
    parts = lax.all_to_all(cells, "lat", 0, 0, tiled=True)

    turn = pl.pallas_call(
        turn_body,
        out_shape=jax.ShapeDtypeStruct((NQ, 2 * MODES, 2 * MODES), bf16),
        in_specs=[vmem()],
        out_specs=vmem(),
        scratch_shapes=[pltpu.VMEM((2 * MODES, 128), f32)],
        compiler_params=params(),
        name="turn",
    )(modes_rot)
    core = (lax.axis_index("kpt") & 1).astype(jnp.int32).reshape(1)
    lattice = jnp.concatenate(
        [re_vectors.T, re_weights[None, :], jnp.zeros((4, re_weights.shape[0]), jnp.int32)], axis=0
    )
    phase, right, left = pl.pallas_call(
        prep_body,
        out_shape=(
            jax.ShapeDtypeStruct((8 * KPTS, 2 * SOURCES * 8), bf16),
            jax.ShapeDtypeStruct((2, BANDS, BANDS, 128), f32),
            jax.ShapeDtypeStruct((2, BANDS, BANDS, 128), f32),
        ),
        in_specs=[smem()] + [vmem()] * 6,
        out_specs=(vmem(),) * 3,
        compiler_params=params(),
        name="prep",
    )(
        core,
        k_points,
        lattice,
        u_k.reshape(2, KPTS, BANDS * BANDS),
        u_kq.reshape(2, NQ * KPTS, BANDS * BANDS),
        mask_k,
        mask_kq.reshape(NQ * KPTS, BANDS),
    )

    branch = pl.pallas_call(
        branch_body,
        out_shape=jax.ShapeDtypeStruct((SOURCES, 8, WIDTH), bf16),
        in_specs=[vmem()] * 2 + [pl.BlockSpec(memory_space=pl.ANY)],
        out_specs=vmem(),
        scratch_shapes=[pltpu.VMEM((PER, LAT * 8, 128), f32)],
        compiler_params=params(),
        name="branch",
    )(parts, turn, phase)
    same_core = [[l * 16 + 2 * z + c for z in range(ZED) for l in range(LAT)] for c in range(2)]
    near = lax.all_to_all(
        branch, ("lat", "kpt"), 0, 0, tiled=True, axis_index_groups=same_core
    )
    far = lax.ppermute(near, "kpt", [(i, i ^ 1) for i in range(16)])

    result = pl.pallas_call(
        couple_body,
        out_shape=jax.ShapeDtypeStruct((2, 2 * KPTS, LANES), bf16),
        in_specs=[vmem()] * 5,
        out_specs=vmem(),
        scratch_shapes=[
            pltpu.VMEM((2, 2 * PER, 128, 128), f32),
            pltpu.VMEM((2, LANES, 128), f32),
            pltpu.VMEM((2, PER * BANDS, BANDS, 128), f32),
            pltpu.VMEM((2, PER * BANDS, BANDS, 128), f32),
        ],
        compiler_params=params(),
        name="couple",
    )(near, far, phase, right, left)
    return result.reshape(2, KPTS, NQ, LANES)


def solution(mesh):
    placed = (
        P(None, "lat", "kpt", None),
        P("lat", None),
        P("lat"),
        P(),
        P(),
        P(),
        P("kpt", None),
        P(),
        P(None, "kpt", None, None),
        P(None, None, "kpt", None, None),
        P("kpt", None),
        P(None, "kpt", None),
    )
    return jax.shard_map(
        per_device,
        mesh=mesh,
        in_specs=placed,
        out_specs=P(None, "kpt", None, "lat"),
        check_vma=False,
    )
```

```python
import jax
import jax.numpy as jnp
from jax import lax
from jax.experimental import pallas as pl
from jax.experimental.pallas import tpu as pltpu
from jax.sharding import PartitionSpec as P

two_pi = 6.283185307179586
f32 = jnp.float32
bf16 = jnp.bfloat16

MODES = 48
BANDS = 16
CELLS = 16
LAT = 16
NQ = 2
KPTS = 64
PER = MODES // LAT
LANES = PER * BANDS * BANDS
STRIDE_S = 2 * MODES + 1
ROWS = NQ * 2 * CELLS
STRIDE_O = ROWS + 1
CHUNKS = 4
CHUNK = MODES * BANDS * BANDS // CHUNKS


def rotate_body(
    qp_hbm, rv_hbm, rw_hbm, rot_hbm, coarse_hbm, out_ref,
    qp_ref, rv_ref, rw_ref, rot_ref, coarse_ref, mat_ref, s_ref, o_ref, sems,
):
    small = [
        pltpu.make_async_copy(src, dst, sems.at[i])
        for i, (src, dst) in enumerate(
            [(qp_hbm, qp_ref), (rv_hbm, rv_ref), (rw_hbm, rw_ref), (rot_hbm, rot_ref)]
        )
    ]
    large = []
    for part in range(2):
        for i in range(CHUNKS):
            lanes = pl.ds(i * CHUNK, CHUNK)
            large.append(
                pltpu.make_async_copy(
                    coarse_hbm.at[part, 0, :, lanes],
                    coarse_ref.at[part, :, lanes],
                    sems.at[4 + part * CHUNKS + i],
                )
            )
    for copy in small + large:
        copy.start()
    for copy in small:
        copy.wait()
    weight = 1.0 / jnp.full((8, 128), rw_ref[0, 0], jnp.int32).astype(f32)
    for q in range(NQ):
        arg = two_pi * (
            qp_ref[q, 0] * rv_ref[0, 0].astype(f32)
            + qp_ref[q, 1] * rv_ref[0, 1].astype(f32)
            + qp_ref[q, 2] * rv_ref[0, 2].astype(f32)
        )
        angle = jnp.full((8, 128), arg, f32)
        pr = (jnp.cos(angle) * weight).astype(bf16).astype(f32)[0:1, 0:1]
        pi = (jnp.sin(angle) * weight).astype(bf16).astype(f32)[0:1, 0:1]
        rr = rot_ref[0, q].astype(f32)
        ri = rot_ref[1, q].astype(f32)
        cr = rr * pr - ri * pi
        ci = rr * pi + ri * pr
        top = jnp.concatenate([cr, -ci], axis=0)
        low = jnp.concatenate([ci, cr], axis=0)
        mat_ref[q * 96:q * 96 + 48, 0:96] = top.T
        mat_ref[q * 96 + 48:q * 96 + 96, 0:96] = low.T
    rows = []
    for g in range(2 * NQ):
        for j in range(PER):
            rows.append(mat_ref[pl.ds(g * 48 + j, LAT, stride=PER), :])
    mat = jnp.concatenate(rows, axis=0)[:, 0:96].astype(bf16)
    for part in range(2):
        for m in range(MODES):
            if m * 256 % CHUNK == 0:
                large[part * CHUNKS + m * 256 // CHUNK].wait()
            for h in range(2):
                at = (2 * m + h) * 128
                tile = coarse_ref[part, :, at:at + 128].astype(f32)
                s_ref[h, pl.ds(part * MODES + m, CELLS, stride=STRIDE_S), :] = tile
    for e in range(CELLS):
        block = jnp.concatenate(
            [s_ref[h, e * STRIDE_S:e * STRIDE_S + 96, :].astype(bf16) for h in range(2)], axis=1
        )
        both = jnp.dot(mat, block, preferred_element_type=f32)
        for h in range(2):
            res = both[:, h * 128:(h + 1) * 128]
            for g in range(2 * NQ):
                for j in range(PER):
                    at = (g * PER + j) * LAT
                    o_ref[2 * j + h, pl.ds(g * CELLS + e, LAT, stride=STRIDE_O), :] = res[at:at + LAT]
    for l in range(LAT):
        for t in range(2 * PER):
            out_ref[l, :, t * 128:(t + 1) * 128] = o_ref[t, l * STRIDE_O:l * STRIDE_O + ROWS, :].astype(bf16)


def sum_body(x_ref, out_ref):
    for r in range(0, ROWS, 16):
        acc = x_ref[0, r:r + 16, :].astype(f32)
        for p in range(1, LAT):
            acc = acc + x_ref[p, r:r + 16, :].astype(f32)
        out_ref[r:r + 16, :] = acc.astype(bf16)


def prep_body(at_ref, kp_ref, rv_ref, u_ref, uq_ref, mk_ref, mq_ref, ph_ref, uo_ref, lo_ref):
    z = at_ref[0]
    c = at_ref[1]
    lane = lax.broadcasted_iota(jnp.int32, (256, 512), 1)
    src = lax.broadcasted_iota(jnp.int32, (256, 512), 0)
    block = lane >> 5
    home = (((z - block) & 7) << 1) + (c ^ (block >> 3))
    cell = (home << 4) + (lane & 15)
    pick = jnp.where(src == cell, 1.0, 0.0).astype(bf16)
    vec = jnp.dot(rv_ref[...].astype(f32).astype(bf16), pick, preferred_element_type=f32)
    kp = kp_ref[...]
    arg = two_pi * (
        kp[:, 0:1] * vec[0:1, :] + kp[:, 1:2] * vec[1:2, :] + kp[:, 2:3] * vec[2:3, :]
    )
    inverse = 1.0 / vec[3:4, :]
    co = jnp.cos(arg) * inverse
    si = jnp.sin(arg) * inverse
    first = (lax.broadcasted_iota(jnp.int32, (KPTS, 512), 1) & 16) == 0
    ph_ref[0:KPTS, :] = jnp.where(first, co, -si).astype(bf16)
    ph_ref[KPTS:2 * KPTS, :] = jnp.where(first, si, co).astype(bf16)
    row = lax.broadcasted_iota(jnp.int32, (KPTS, 128), 0)
    col = lax.broadcasted_iota(jnp.int32, (KPTS, 128), 1)
    spread = jnp.where((col >> 1) == row, 1.0, 0.0).astype(bf16)
    row2 = lax.broadcasted_iota(jnp.int32, (128, 128), 0)
    col2 = lax.broadcasted_iota(jnp.int32, (128, 128), 1)
    place = jnp.where((((col2 & 1) << 6) + (col2 >> 1)) == row2, 1.0, 0.0).astype(bf16)
    dims = (((0,), (0,)), ((), ()))
    mk = lax.dot_general(mk_ref[...].astype(f32).astype(bf16), spread, dims, preferred_element_type=f32)
    mq = lax.dot_general(mq_ref[...].astype(f32).astype(bf16), place, dims, preferred_element_type=f32)
    for part in range(2):
        ut = lax.dot_general(u_ref[part], spread, dims, preferred_element_type=f32)
        lt = lax.dot_general(uq_ref[part], place, dims, preferred_element_type=f32)
        for b in range(BANDS):
            uo_ref[part, b] = ut[b * 16:(b + 1) * 16] * mk
            lo_ref[part, b] = lt[b * 16:(b + 1) * 16] * mq


def pack_body(own_ref, up_ref, down_ref, order_ref, three_ref, two_ref):
    for i, ref in enumerate((own_ref, up_ref, down_ref)):
        value = ref[...]
        three_ref[i * ROWS:(i + 1) * ROWS, :] = value
        if i < 2:
            two_ref[i * ROWS:(i + 1) * ROWS, :] = value


PLACE = ((0, 0), (1, 0), (2, 1), (0, 1), (1, 1), (0, 2), (1, 2), (2, 0))


def couple_body(*refs):
    ph_ref, u_ref, l_ref, out_ref, y_ref, bl_ref, h_ref, r_ref = refs[6:]
    ph = ph_ref[...]
    for q in range(NQ):
        x = jnp.concatenate(
            [
                refs[side * 3 + i][j * ROWS + q * 32:j * ROWS + (q + 1) * 32, :]
                for side in range(2)
                for i, j in PLACE
            ],
            axis=0,
        )
        t = jnp.dot(ph, x, preferred_element_type=f32)
        for part in range(2):
            for v in range(2 * PER):
                y_ref[part, v, pl.ds(q, KPTS, stride=2), :] = t[
                    part * KPTS:(part + 1) * KPTS, v * 128:(v + 1) * 128
                ]
    for part in range(2):
        for v in range(2 * PER):
            bl_ref[part, v * 128:(v + 1) * 128, :] = y_ref[part, v].T.astype(bf16).astype(f32)

    group = 4

    def first(i, _):
        base = i * group * BANDS
        accr = [jnp.zeros((16, 128), f32) for _ in range(group)]
        acci = [jnp.zeros((16, 128), f32) for _ in range(group)]
        for b in range(BANDS):
            ur = u_ref[0, b]
            ui = u_ref[1, b]
            for s in range(group):
                xr = bl_ref[0, pl.ds(base + s * BANDS + b, 1), :]
                xi = bl_ref[1, pl.ds(base + s * BANDS + b, 1), :]
                accr[s] = accr[s] + (xr * ur - xi * ui)
                acci[s] = acci[s] + (xr * ui + xi * ur)
        for s in range(group):
            h_ref[0, i * group + s] = accr[s].astype(bf16).astype(f32)
            h_ref[1, i * group + s] = acci[s].astype(bf16).astype(f32)
        return 0

    lax.fori_loop(0, PER * BANDS // group, first, 0)

    per = BANDS // group

    def second(i, _):
        n = i // per
        c0 = (i - n * per) * group
        accr = [jnp.zeros((16, 128), f32) for _ in range(group)]
        acci = [jnp.zeros((16, 128), f32) for _ in range(group)]
        for a in range(BANDS):
            hr = h_ref[0, n * BANDS + a]
            hi = h_ref[1, n * BANDS + a]
            for s in range(group):
                lr = l_ref[0, a, pl.ds(c0 + s, 1), :]
                li = l_ref[1, a, pl.ds(c0 + s, 1), :]
                accr[s] = accr[s] + (lr * hr + li * hi)
                acci[s] = acci[s] + (lr * hi - li * hr)
        for s in range(group):
            r_ref[0, i * group + s] = accr[s]
            r_ref[1, i * group + s] = acci[s]
        return 0

    lax.fori_loop(0, PER * per, second, 0)
    for part in range(2):
        for v in range(2 * PER):
            tile = r_ref[part, v * 8:(v + 1) * 8].reshape(128, 128).T
            out_ref[part, :, :, v * 128:(v + 1) * 128] = tile.reshape(KPTS, NQ, 128).astype(bf16)


def vmem():
    return pl.BlockSpec(memory_space=pltpu.VMEM)


def hbm():
    return pl.BlockSpec(memory_space=pltpu.HBM)


def smem():
    return pl.BlockSpec(memory_space=pltpu.SMEM)


def params():
    return pltpu.CompilerParams(vmem_limit_bytes=40 << 20)


def per_device(
    coarse,
    rp_vectors,
    rp_weights,
    re_vectors,
    re_weights,
    q_points,
    k_points,
    modes_rot,
    u_k,
    u_kq,
    mask_k,
    mask_kq,
):
    rotated = pl.pallas_call(
        rotate_body,
        out_shape=jax.ShapeDtypeStruct((LAT, ROWS, LANES), bf16),
        in_specs=[hbm()] * 5,
        out_specs=vmem(),
        scratch_shapes=[
            pltpu.SMEM((NQ, 3), f32),
            pltpu.SMEM((1, 3), jnp.int32),
            pltpu.SMEM((1, 1), jnp.int32),
            pltpu.VMEM((2, NQ, MODES, MODES), bf16),
            pltpu.VMEM((2, CELLS, MODES * BANDS * BANDS), bf16),
            pltpu.VMEM((192, 128), f32),
            pltpu.VMEM((2, CELLS * STRIDE_S, 128), f32),
            pltpu.VMEM((2 * PER, LAT * STRIDE_O, 128), f32),
            pltpu.SemaphoreType.DMA((4 + 2 * CHUNKS,)),
        ],
        compiler_params=pltpu.CompilerParams(vmem_limit_bytes=63 << 20),
        name="rotate",
    )(q_points, rp_vectors, rp_weights[None, :], modes_rot, coarse)
    parts = lax.all_to_all(rotated, "lat", 0, 0, tiled=True)

    index = lax.axis_index("kpt")
    at = jnp.stack([index // 2, index % 2]).astype(jnp.int32)
    lattice = jnp.concatenate(
        [re_vectors.T, re_weights[None, :], jnp.zeros((4, re_weights.shape[0]), jnp.int32)], axis=0
    )
    phase, right, left = pl.pallas_call(
        prep_body,
        out_shape=(
            jax.ShapeDtypeStruct((2 * KPTS, 512), bf16),
            jax.ShapeDtypeStruct((2, BANDS, BANDS, 128), f32),
            jax.ShapeDtypeStruct((2, BANDS, BANDS, 128), f32),
        ),
        in_specs=[smem()] + [vmem()] * 6,
        out_specs=(vmem(),) * 3,
        compiler_params=params(),
        name="prep",
    )(
        at,
        k_points,
        lattice,
        u_k.reshape(2, KPTS, BANDS * BANDS),
        u_kq.reshape(2, NQ * KPTS, BANDS * BANDS),
        mask_k,
        mask_kq.reshape(NQ * KPTS, BANDS),
    )

    own = pl.pallas_call(
        sum_body,
        out_shape=jax.ShapeDtypeStruct((ROWS, LANES), bf16),
        in_specs=[vmem()],
        out_specs=vmem(),
        compiler_params=params(),
        name="add_up",
    )(parts)

    def shift(x, step):
        return lax.ppermute(x, "kpt", [(i, (i + 2 * step) % 16) for i in range(16)])

    def swap(x):
        return lax.ppermute(x, "kpt", [(i, i ^ 1) for i in range(16)])

    up = shift(own, 3)
    down = shift(own, -3)
    packed, pair = pl.pallas_call(
        pack_body,
        out_shape=(
            jax.ShapeDtypeStruct((3 * ROWS, LANES), bf16),
            jax.ShapeDtypeStruct((2 * ROWS, LANES), bf16),
        ),
        in_specs=[vmem()] * 3 + [pl.BlockSpec(memory_space=pl.ANY)],
        out_specs=(vmem(), vmem()),
        compiler_params=params(),
        name="pack",
    )(own, up, down, phase)
    plus = shift(packed, 1)
    minus = shift(pair, -1)
    near = [packed, plus, minus]
    far = [swap(x) for x in near]

    result = pl.pallas_call(
        couple_body,
        out_shape=jax.ShapeDtypeStruct((2, KPTS, NQ, LANES), bf16),
        in_specs=[vmem()] * 9,
        out_specs=vmem(),
        scratch_shapes=[
            pltpu.VMEM((2, 2 * PER, 128, 128), f32),
            pltpu.VMEM((2, LANES, 128), f32),
            pltpu.VMEM((2, PER * BANDS, BANDS, 128), f32),
            pltpu.VMEM((2, PER * BANDS, BANDS, 128), f32),
        ],
        compiler_params=params(),
        name="couple",
    )(*near, *far, phase, right, left)
    return result


def solution(mesh):
    placed = (
        P(None, "lat", "kpt", None),
        P("lat", None),
        P("lat"),
        P(),
        P(),
        P(),
        P("kpt", None),
        P(),
        P(None, "kpt", None, None),
        P(None, None, "kpt", None, None),
        P("kpt", None),
        P(None, "kpt", None),
    )
    return jax.shard_map(
        per_device,
        mesh=mesh,
        in_specs=placed,
        out_specs=P(None, "kpt", None, "lat"),
        check_vma=False,
    )
```

```python
import jax
import jax.numpy as jnp
from jax import lax
from jax.experimental import pallas as pl
from jax.experimental.pallas import tpu as pltpu
from jax.sharding import PartitionSpec as P

two_pi = 6.283185307179586
f32 = jnp.float32
bf16 = jnp.bfloat16

MODES = 48
BANDS = 16
CELLS = 16
LAT = 16
NQ = 2
KPTS = 64
PER = MODES // LAT
LANES = PER * BANDS * BANDS
STRIDE_S = 2 * MODES + 1
ROWS = NQ * 2 * CELLS
STRIDE_O = ROWS + 1
CHUNKS = 4
CHUNK = MODES * BANDS * BANDS // CHUNKS


def rotate_body(
    qp_hbm, rv_hbm, rw_hbm, rot_hbm, coarse_hbm, out_ref,
    qp_ref, rv_ref, rw_ref, rot_ref, coarse_ref, mat_ref, s_ref, o_ref, sems,
):
    small = [
        pltpu.make_async_copy(src, dst, sems.at[i])
        for i, (src, dst) in enumerate(
            [(qp_hbm, qp_ref), (rv_hbm, rv_ref), (rw_hbm, rw_ref), (rot_hbm, rot_ref)]
        )
    ]
    large = []
    for part in range(2):
        for i in range(CHUNKS):
            lanes = pl.ds(i * CHUNK, CHUNK)
            large.append(
                pltpu.make_async_copy(
                    coarse_hbm.at[part, 0, :, lanes],
                    coarse_ref.at[part, :, lanes],
                    sems.at[4 + part * CHUNKS + i],
                )
            )
    for copy in small + large:
        copy.start()
    for copy in small:
        copy.wait()
    weight = 1.0 / jnp.full((8, 128), rw_ref[0, 0], jnp.int32).astype(f32)
    for q in range(NQ):
        arg = two_pi * (
            qp_ref[q, 0] * rv_ref[0, 0].astype(f32)
            + qp_ref[q, 1] * rv_ref[0, 1].astype(f32)
            + qp_ref[q, 2] * rv_ref[0, 2].astype(f32)
        )
        angle = jnp.full((8, 128), arg, f32)
        pr = (jnp.cos(angle) * weight).astype(bf16).astype(f32)[0:1, 0:1]
        pi = (jnp.sin(angle) * weight).astype(bf16).astype(f32)[0:1, 0:1]
        rr = rot_ref[0, q].astype(f32)
        ri = rot_ref[1, q].astype(f32)
        cr = rr * pr - ri * pi
        ci = rr * pi + ri * pr
        top = jnp.concatenate([cr, -ci], axis=0)
        low = jnp.concatenate([ci, cr], axis=0)
        mat_ref[q * 96:q * 96 + 48, 0:96] = top.T
        mat_ref[q * 96 + 48:q * 96 + 96, 0:96] = low.T
    rows = []
    for g in range(2 * NQ):
        for j in range(PER):
            rows.append(mat_ref[pl.ds(g * 48 + j, LAT, stride=PER), :])
    mat = jnp.concatenate(rows, axis=0)[:, 0:96].astype(bf16)
    for part in range(2):
        for m in range(MODES):
            if m * 256 % CHUNK == 0:
                large[part * CHUNKS + m * 256 // CHUNK].wait()
            for h in range(2):
                at = (2 * m + h) * 128
                tile = coarse_ref[part, :, at:at + 128].astype(f32)
                s_ref[h, pl.ds(part * MODES + m, CELLS, stride=STRIDE_S), :] = tile
    for e in range(CELLS):
        block = jnp.concatenate(
            [s_ref[h, e * STRIDE_S:e * STRIDE_S + 96, :].astype(bf16) for h in range(2)], axis=1
        )
        both = jnp.dot(mat, block, preferred_element_type=f32)
        for h in range(2):
            res = both[:, h * 128:(h + 1) * 128]
            for g in range(2 * NQ):
                for j in range(PER):
                    at = (g * PER + j) * LAT
                    o_ref[2 * j + h, pl.ds(g * CELLS + e, LAT, stride=STRIDE_O), :] = res[at:at + LAT]
    for l in range(LAT):
        for t in range(2 * PER):
            out_ref[l, :, t * 128:(t + 1) * 128] = o_ref[t, l * STRIDE_O:l * STRIDE_O + ROWS, :].astype(bf16)


def sum_body(x_ref, out_ref):
    for r in range(0, ROWS, 16):
        acc = x_ref[0, r:r + 16, :].astype(f32)
        for p in range(1, LAT):
            acc = acc + x_ref[p, r:r + 16, :].astype(f32)
        out_ref[r:r + 16, :] = acc.astype(bf16)


def prep_body(at_ref, kp_ref, rv_ref, u_ref, uq_ref, mk_ref, mq_ref, ph_ref, uo_ref, lo_ref):
    z = at_ref[0]
    c = at_ref[1]
    lane = lax.broadcasted_iota(jnp.int32, (256, 512), 1)
    src = lax.broadcasted_iota(jnp.int32, (256, 512), 0)
    block = lane >> 5
    home = (((z - block) & 7) << 1) + (c ^ (block >> 3))
    cell = (home << 4) + (lane & 15)
    pick = jnp.where(src == cell, 1.0, 0.0).astype(bf16)
    vec = jnp.dot(rv_ref[...].astype(f32).astype(bf16), pick, preferred_element_type=f32)
    kp = kp_ref[...]
    arg = two_pi * (
        kp[:, 0:1] * vec[0:1, :] + kp[:, 1:2] * vec[1:2, :] + kp[:, 2:3] * vec[2:3, :]
    )
    inverse = 1.0 / vec[3:4, :]
    co = jnp.cos(arg) * inverse
    si = jnp.sin(arg) * inverse
    first = (lax.broadcasted_iota(jnp.int32, (KPTS, 512), 1) & 16) == 0
    ph_ref[0:KPTS, :] = jnp.where(first, co, -si).astype(bf16)
    ph_ref[KPTS:2 * KPTS, :] = jnp.where(first, si, co).astype(bf16)
    row = lax.broadcasted_iota(jnp.int32, (KPTS, 128), 0)
    col = lax.broadcasted_iota(jnp.int32, (KPTS, 128), 1)
    spread = jnp.where((col >> 1) == row, 1.0, 0.0).astype(bf16)
    row2 = lax.broadcasted_iota(jnp.int32, (128, 128), 0)
    col2 = lax.broadcasted_iota(jnp.int32, (128, 128), 1)
    place = jnp.where((((col2 & 1) << 6) + (col2 >> 1)) == row2, 1.0, 0.0).astype(bf16)
    dims = (((0,), (0,)), ((), ()))
    mk = lax.dot_general(mk_ref[...].astype(f32).astype(bf16), spread, dims, preferred_element_type=f32)
    mq = lax.dot_general(mq_ref[...].astype(f32).astype(bf16), place, dims, preferred_element_type=f32)
    ur, ui = (
        lax.dot_general(u_ref[part], spread, dims, preferred_element_type=f32) for part in range(2)
    )
    lr, li = (
        lax.dot_general(uq_ref[part], place, dims, preferred_element_type=f32) for part in range(2)
    )
    for i, (u, left) in enumerate(((ur, lr), (ui - ur, -(li + lr)), (ur + ui, lr - li))):
        for b in range(BANDS):
            uo_ref[i, b] = u[b * 16:(b + 1) * 16] * mk
            lo_ref[i, b] = left[b * 16:(b + 1) * 16] * mq


def pack_body(own_ref, across_ref, order_ref, out_ref):
    out_ref[0:ROWS, :] = own_ref[...]
    out_ref[ROWS:2 * ROWS, :] = across_ref[...]


PLACE = ((0, 0), (3, 0), (1, 0), (4, 1), (0, 1), (3, 1), (2, 0), (4, 0))


def couple_body(*refs):
    ph_ref, u_ref, l_ref, out_ref, y_ref, bl_ref, h_ref, r_ref = refs[10:]
    ph = ph_ref[...]
    for q in range(NQ):
        x = jnp.concatenate(
            [
                refs[side * 5 + i][j * ROWS + q * 32:j * ROWS + (q + 1) * 32, :]
                for side in range(2)
                for i, j in PLACE
            ],
            axis=0,
        )
        t = jnp.dot(ph, x, preferred_element_type=f32)
        for part in range(2):
            for v in range(2 * PER):
                y_ref[part, v, pl.ds(q, KPTS, stride=2), :] = t[
                    part * KPTS:(part + 1) * KPTS, v * 128:(v + 1) * 128
                ]
    for v in range(2 * PER):
        rows = slice(v * 128, (v + 1) * 128)
        xr, xi = (y_ref[part, v].T.astype(bf16).astype(f32) for part in range(2))
        bl_ref[0, rows, :] = xr + xi
        bl_ref[1, rows, :] = xr
        bl_ref[2, rows, :] = xi

    group = 4

    def first(i, _):
        base = i * group * BANDS
        acc = [[jnp.zeros((16, 128), f32) for _ in range(3)] for _ in range(group)]
        for b in range(BANDS):
            us = [u_ref[t, b] for t in range(3)]
            for s in range(group):
                for t in range(3):
                    acc[s][t] = acc[s][t] + bl_ref[t, pl.ds(base + s * BANDS + b, 1), :] * us[t]
        for s in range(group):
            hr = (acc[s][0] - acc[s][2]).astype(bf16).astype(f32)
            hi = (acc[s][0] + acc[s][1]).astype(bf16).astype(f32)
            h_ref[0, i * group + s] = hr + hi
            h_ref[1, i * group + s] = hr
            h_ref[2, i * group + s] = hi
        return 0

    lax.fori_loop(0, PER * BANDS // group, first, 0)

    per = BANDS // group

    def second(i, _):
        n = i // per
        c0 = (i - n * per) * group
        acc = [[jnp.zeros((16, 128), f32) for _ in range(3)] for _ in range(group)]
        for a in range(BANDS):
            hs = [h_ref[t, n * BANDS + a] for t in range(3)]
            for s in range(group):
                for t in range(3):
                    acc[s][t] = acc[s][t] + l_ref[t, a, pl.ds(c0 + s, 1), :] * hs[t]
        for s in range(group):
            r_ref[0, i * group + s] = acc[s][0] - acc[s][2]
            r_ref[1, i * group + s] = acc[s][0] + acc[s][1]
        return 0

    lax.fori_loop(0, PER * per, second, 0)
    for part in range(2):
        for v in range(2 * PER):
            tile = r_ref[part, v * 8:(v + 1) * 8].reshape(128, 128).T
            out_ref[part, :, :, v * 128:(v + 1) * 128] = tile.reshape(KPTS, NQ, 128).astype(bf16)


def vmem():
    return pl.BlockSpec(memory_space=pltpu.VMEM)


def hbm():
    return pl.BlockSpec(memory_space=pltpu.HBM)


def smem():
    return pl.BlockSpec(memory_space=pltpu.SMEM)


def params():
    return pltpu.CompilerParams(vmem_limit_bytes=40 << 20)


def per_device(
    coarse,
    rp_vectors,
    rp_weights,
    re_vectors,
    re_weights,
    q_points,
    k_points,
    modes_rot,
    u_k,
    u_kq,
    mask_k,
    mask_kq,
):
    rotated = pl.pallas_call(
        rotate_body,
        out_shape=jax.ShapeDtypeStruct((LAT, ROWS, LANES), bf16),
        in_specs=[hbm()] * 5,
        out_specs=vmem(),
        scratch_shapes=[
            pltpu.SMEM((NQ, 3), f32),
            pltpu.SMEM((1, 3), jnp.int32),
            pltpu.SMEM((1, 1), jnp.int32),
            pltpu.VMEM((2, NQ, MODES, MODES), bf16),
            pltpu.VMEM((2, CELLS, MODES * BANDS * BANDS), bf16),
            pltpu.VMEM((192, 128), f32),
            pltpu.VMEM((2, CELLS * STRIDE_S, 128), f32),
            pltpu.VMEM((2 * PER, LAT * STRIDE_O, 128), f32),
            pltpu.SemaphoreType.DMA((4 + 2 * CHUNKS,)),
        ],
        compiler_params=pltpu.CompilerParams(vmem_limit_bytes=63 << 20),
        name="rotate",
    )(q_points, rp_vectors, rp_weights[None, :], modes_rot, coarse)
    parts = lax.all_to_all(rotated, "lat", 0, 0, tiled=True)

    index = lax.axis_index("kpt")
    at = jnp.stack([index // 2, index % 2]).astype(jnp.int32)
    lattice = jnp.concatenate(
        [re_vectors.T, re_weights[None, :], jnp.zeros((4, re_weights.shape[0]), jnp.int32)], axis=0
    )
    phase, right, left = pl.pallas_call(
        prep_body,
        out_shape=(
            jax.ShapeDtypeStruct((2 * KPTS, 512), bf16),
            jax.ShapeDtypeStruct((3, BANDS, BANDS, 128), f32),
            jax.ShapeDtypeStruct((3, BANDS, BANDS, 128), f32),
        ),
        in_specs=[smem()] + [vmem()] * 6,
        out_specs=(vmem(),) * 3,
        compiler_params=params(),
        name="prep",
    )(
        at,
        k_points,
        lattice,
        u_k.reshape(2, KPTS, BANDS * BANDS),
        u_kq.reshape(2, NQ * KPTS, BANDS * BANDS),
        mask_k,
        mask_kq.reshape(NQ * KPTS, BANDS),
    )

    own = pl.pallas_call(
        sum_body,
        out_shape=jax.ShapeDtypeStruct((ROWS, LANES), bf16),
        in_specs=[vmem()],
        out_specs=vmem(),
        compiler_params=params(),
        name="add_up",
    )(parts)

    def shift(x, step):
        return lax.ppermute(x, "kpt", [(i, (i + 2 * step) % 16) for i in range(16)])

    def swap(x):
        return lax.ppermute(x, "kpt", [(i, i ^ 1) for i in range(16)])

    across = shift(own, 4)
    packed = pl.pallas_call(
        pack_body,
        out_shape=jax.ShapeDtypeStruct((2 * ROWS, LANES), bf16),
        in_specs=[vmem()] * 2 + [pl.BlockSpec(memory_space=pl.ANY)],
        out_specs=vmem(),
        compiler_params=params(),
        name="pack",
    )(own, across, phase)
    near = [packed, shift(own, 2), shift(own, -2), shift(packed, 1), shift(packed, -1)]
    far = [swap(x) for x in near]

    result = pl.pallas_call(
        couple_body,
        out_shape=jax.ShapeDtypeStruct((2, KPTS, NQ, LANES), bf16),
        in_specs=[vmem()] * 13,
        out_specs=vmem(),
        scratch_shapes=[
            pltpu.VMEM((2, 2 * PER, 128, 128), f32),
            pltpu.VMEM((3, LANES, 128), f32),
            pltpu.VMEM((3, PER * BANDS, BANDS, 128), f32),
            pltpu.VMEM((2, PER * BANDS, BANDS, 128), f32),
        ],
        compiler_params=params(),
        name="couple",
    )(*near, *far, phase, right, left)
    return result


def solution(mesh):
    placed = (
        P(None, "lat", "kpt", None),
        P("lat", None),
        P("lat"),
        P(),
        P(),
        P(),
        P("kpt", None),
        P(),
        P(None, "kpt", None, None),
        P(None, None, "kpt", None, None),
        P("kpt", None),
        P(None, "kpt", None),
    )
    return jax.shard_map(
        per_device,
        mesh=mesh,
        in_specs=placed,
        out_specs=P(None, "kpt", None, "lat"),
        check_vma=False,
    )
```

```python
import jax
import jax.numpy as jnp
from jax import lax
from jax.experimental import pallas as pl
from jax.experimental.pallas import tpu as pltpu
from jax.sharding import PartitionSpec as P

two_pi = 6.283185307179586
f32 = jnp.float32
bf16 = jnp.bfloat16

MODES = 48
BANDS = 16
CELLS = 16
LAT = 16
NQ = 2
KPTS = 64
PER = MODES // LAT
LANES = PER * BANDS * BANDS
STRIDE_S = 2 * MODES + 1
ROWS = NQ * 2 * CELLS
STRIDE_O = ROWS + 1
CHUNKS = 4
SENDS = 4
CHUNK = MODES * BANDS * BANDS // CHUNKS


def rotate_body(
    qp_hbm, rv_hbm, rw_hbm, rot_hbm, coarse_hbm, out_hbm,
    qp_ref, rv_ref, rw_ref, rot_ref, coarse_ref, mat_ref, s_ref, o_ref, send_ref, sems,
):
    small = [
        pltpu.make_async_copy(src, dst, sems.at[i])
        for i, (src, dst) in enumerate(
            [(qp_hbm, qp_ref), (rv_hbm, rv_ref), (rw_hbm, rw_ref), (rot_hbm, rot_ref)]
        )
    ]
    large = []
    for part in range(2):
        for i in range(CHUNKS):
            lanes = pl.ds(i * CHUNK, CHUNK)
            large.append(
                pltpu.make_async_copy(
                    coarse_hbm.at[part, 0, :, lanes],
                    coarse_ref.at[part, :, lanes],
                    sems.at[4 + part * CHUNKS + i],
                )
            )
    for copy in large + small:
        copy.start()
    for part in range(2):
        for m in range(MODES):
            if m * 256 % CHUNK == 0:
                large[part * CHUNKS + m * 256 // CHUNK].wait()
            for h in range(2):
                at = (2 * m + h) * 128
                tile = coarse_ref[part, :, at:at + 128].astype(f32)
                s_ref[h, pl.ds(part * MODES + m, CELLS, stride=STRIDE_S), :] = tile
    for copy in small:
        copy.wait()
    weight = 1.0 / jnp.full((8, 128), rw_ref[0, 0], jnp.int32).astype(f32)
    for q in range(NQ):
        arg = two_pi * (
            qp_ref[q, 0] * rv_ref[0, 0].astype(f32)
            + qp_ref[q, 1] * rv_ref[0, 1].astype(f32)
            + qp_ref[q, 2] * rv_ref[0, 2].astype(f32)
        )
        angle = jnp.full((8, 128), arg, f32)
        pr = (jnp.cos(angle) * weight).astype(bf16).astype(f32)[0:1, 0:1]
        pi = (jnp.sin(angle) * weight).astype(bf16).astype(f32)[0:1, 0:1]
        rr = rot_ref[0, q].astype(f32)
        ri = rot_ref[1, q].astype(f32)
        cr = rr * pr - ri * pi
        ci = rr * pi + ri * pr
        top = jnp.concatenate([cr, -ci], axis=0)
        low = jnp.concatenate([ci, cr], axis=0)
        mat_ref[q * 96:q * 96 + 48, 0:96] = top.T
        mat_ref[q * 96 + 48:q * 96 + 96, 0:96] = low.T
    rows = []
    for g in range(2 * NQ):
        for j in range(PER):
            rows.append(mat_ref[pl.ds(g * 48 + j, LAT, stride=PER), :])
    mat = jnp.concatenate(rows, axis=0)[:, 0:96].astype(bf16)
    for e in range(CELLS):
        block = jnp.concatenate(
            [s_ref[h, e * STRIDE_S:e * STRIDE_S + 96, :].astype(bf16) for h in range(2)], axis=1
        )
        both = jnp.dot(mat, block, preferred_element_type=f32)
        for h in range(2):
            res = both[:, h * 128:(h + 1) * 128]
            for g in range(2 * NQ):
                for j in range(PER):
                    at = (g * PER + j) * LAT
                    o_ref[2 * j + h, pl.ds(g * CELLS + e, LAT, stride=STRIDE_O), :] = res[at:at + LAT]
    sends = []
    for l in range(LAT):
        for t in range(2 * PER):
            send_ref[l, :, t * 128:(t + 1) * 128] = o_ref[
                t, l * STRIDE_O:l * STRIDE_O + ROWS, :
            ].astype(bf16)
        if l % SENDS == SENDS - 1:
            part = pl.ds(l + 1 - SENDS, SENDS)
            sends.append(
                pltpu.make_async_copy(
                    send_ref.at[part], out_hbm.at[part], sems.at[4 + 2 * CHUNKS + l // SENDS]
                )
            )
            sends[-1].start()
    for copy in sends:
        copy.wait()


def sum_body(x_ref, out_ref):
    for r in range(0, ROWS, 16):
        acc = x_ref[0, r:r + 16, :].astype(f32)
        for p in range(1, LAT):
            acc = acc + x_ref[p, r:r + 16, :].astype(f32)
        out_ref[r:r + 16, :] = acc.astype(bf16)


def prep_body(at_ref, kp_ref, rv_ref, u_ref, uq_ref, mk_ref, mq_ref, ph_ref, uo_ref, lo_ref):
    z = at_ref[0]
    c = at_ref[1]
    lane = lax.broadcasted_iota(jnp.int32, (256, 512), 1)
    src = lax.broadcasted_iota(jnp.int32, (256, 512), 0)
    block = lane >> 5
    home = (((z - block) & 7) << 1) + (c ^ (block >> 3))
    cell = (home << 4) + (lane & 15)
    pick = jnp.where(src == cell, 1.0, 0.0).astype(bf16)
    vec = jnp.dot(rv_ref[...].astype(f32).astype(bf16), pick, preferred_element_type=f32)
    kp = kp_ref[...]
    arg = two_pi * (
        kp[:, 0:1] * vec[0:1, :] + kp[:, 1:2] * vec[1:2, :] + kp[:, 2:3] * vec[2:3, :]
    )
    inverse = 1.0 / vec[3:4, :]
    co = jnp.cos(arg) * inverse
    si = jnp.sin(arg) * inverse
    first = (lax.broadcasted_iota(jnp.int32, (KPTS, 512), 1) & 16) == 0
    ph_ref[0:KPTS, :] = jnp.where(first, co, -si).astype(bf16)
    ph_ref[KPTS:2 * KPTS, :] = jnp.where(first, si, co).astype(bf16)
    row = lax.broadcasted_iota(jnp.int32, (KPTS, 128), 0)
    col = lax.broadcasted_iota(jnp.int32, (KPTS, 128), 1)
    spread = jnp.where((col >> 1) == row, 1.0, 0.0).astype(bf16)
    row2 = lax.broadcasted_iota(jnp.int32, (128, 128), 0)
    col2 = lax.broadcasted_iota(jnp.int32, (128, 128), 1)
    place = jnp.where((((col2 & 1) << 6) + (col2 >> 1)) == row2, 1.0, 0.0).astype(bf16)
    dims = (((0,), (0,)), ((), ()))
    mk = lax.dot_general(mk_ref[...].astype(f32).astype(bf16), spread, dims, preferred_element_type=f32)
    mq = lax.dot_general(mq_ref[...].astype(f32).astype(bf16), place, dims, preferred_element_type=f32)
    ur, ui = (
        lax.dot_general(u_ref[part], spread, dims, preferred_element_type=f32) for part in range(2)
    )
    lr, li = (
        lax.dot_general(uq_ref[part], place, dims, preferred_element_type=f32) for part in range(2)
    )
    for i, (u, left) in enumerate(((ur, lr), (ui - ur, -(li + lr)), (ur + ui, lr - li))):
        for b in range(BANDS):
            uo_ref[i, b] = u[b * 16:(b + 1) * 16] * mk
            lo_ref[i, b] = left[b * 16:(b + 1) * 16] * mq


def pack_body(own_ref, up_ref, down_ref, order_ref, three_ref, two_ref):
    for i, ref in enumerate((own_ref, up_ref, down_ref)):
        value = ref[...]
        three_ref[i * ROWS:(i + 1) * ROWS, :] = value
        if i < 2:
            two_ref[i * ROWS:(i + 1) * ROWS, :] = value


PLACE = ((0, 0), (1, 0), (2, 1), (0, 1), (1, 1), (0, 2), (1, 2), (2, 0))


def couple_body(*refs):
    ph_ref, u_ref, l_ref, out_hbm, y_ref, bl_ref, h_ref, r_ref, out_ref, sems = refs[6:]
    ph = ph_ref[...]
    for q in range(NQ):
        x = jnp.concatenate(
            [
                refs[side * 3 + i][j * ROWS + q * 32:j * ROWS + (q + 1) * 32, :]
                for side in range(2)
                for i, j in PLACE
            ],
            axis=0,
        )
        t = jnp.dot(ph, x, preferred_element_type=f32)
        for part in range(2):
            for v in range(2 * PER):
                y_ref[part, v, pl.ds(q, KPTS, stride=2), :] = t[
                    part * KPTS:(part + 1) * KPTS, v * 128:(v + 1) * 128
                ]
    for v in range(2 * PER):
        rows = slice(v * 128, (v + 1) * 128)
        xr, xi = (y_ref[part, v].T.astype(bf16).astype(f32) for part in range(2))
        bl_ref[0, rows, :] = xr + xi
        bl_ref[1, rows, :] = xr
        bl_ref[2, rows, :] = xi

    group = 4

    def first(i, _):
        base = i * group * BANDS
        acc = [[jnp.zeros((16, 128), f32) for _ in range(3)] for _ in range(group)]
        for b in range(BANDS):
            us = [u_ref[t, b] for t in range(3)]
            for s in range(group):
                for t in range(3):
                    acc[s][t] = acc[s][t] + bl_ref[t, pl.ds(base + s * BANDS + b, 1), :] * us[t]
        for s in range(group):
            hr = (acc[s][0] - acc[s][2]).astype(bf16).astype(f32)
            hi = (acc[s][0] + acc[s][1]).astype(bf16).astype(f32)
            h_ref[0, i * group + s] = hr + hi
            h_ref[1, i * group + s] = hr
            h_ref[2, i * group + s] = hi
        return 0

    lax.fori_loop(0, PER * BANDS // group, first, 0)

    copies = []
    for n in range(PER):

        def second(i, _):
            acc = [[jnp.zeros((16, 128), f32) for _ in range(3)] for _ in range(group)]
            for a in range(BANDS):
                hs = [h_ref[t, n * BANDS + a] for t in range(3)]
                for s in range(group):
                    for t in range(3):
                        row = l_ref[t, a, pl.ds(i * group + s, 1), :]
                        acc[s][t] = acc[s][t] + row * hs[t]
            for s in range(group):
                r_ref[0, i * group + s] = acc[s][0] - acc[s][2]
                r_ref[1, i * group + s] = acc[s][0] + acc[s][1]
            return 0

        lax.fori_loop(0, BANDS // group, second, 0)
        for part in range(2):
            for h in range(2):
                tile = r_ref[part, h * 8:(h + 1) * 8].reshape(128, 128).T
                at = (2 * n + h) * 128
                out_ref[part, :, :, at:at + 128] = tile.reshape(KPTS, NQ, 128).astype(bf16)
        lanes = pl.ds(n * 256, 256)
        copies.append(
            pltpu.make_async_copy(
                out_ref.at[:, :, :, lanes], out_hbm.at[:, :, :, lanes], sems.at[n]
            )
        )
        copies[-1].start()
    for copy in copies:
        copy.wait()


def vmem():
    return pl.BlockSpec(memory_space=pltpu.VMEM)


def hbm():
    return pl.BlockSpec(memory_space=pltpu.HBM)


def smem():
    return pl.BlockSpec(memory_space=pltpu.SMEM)


def params():
    return pltpu.CompilerParams(vmem_limit_bytes=40 << 20)


def per_device(
    coarse,
    rp_vectors,
    rp_weights,
    re_vectors,
    re_weights,
    q_points,
    k_points,
    modes_rot,
    u_k,
    u_kq,
    mask_k,
    mask_kq,
):
    rotated = pl.pallas_call(
        rotate_body,
        out_shape=jax.ShapeDtypeStruct((LAT, ROWS, LANES), bf16),
        in_specs=[hbm()] * 5,
        out_specs=hbm(),
        scratch_shapes=[
            pltpu.SMEM((NQ, 3), f32),
            pltpu.SMEM((1, 3), jnp.int32),
            pltpu.SMEM((1, 1), jnp.int32),
            pltpu.VMEM((2, NQ, MODES, MODES), bf16),
            pltpu.VMEM((2, CELLS, MODES * BANDS * BANDS), bf16),
            pltpu.VMEM((192, 128), f32),
            pltpu.VMEM((2, CELLS * STRIDE_S, 128), f32),
            pltpu.VMEM((2 * PER, LAT * STRIDE_O, 128), f32),
            pltpu.VMEM((LAT, ROWS, LANES), bf16),
            pltpu.SemaphoreType.DMA((4 + 2 * CHUNKS + LAT // SENDS,)),
        ],
        compiler_params=pltpu.CompilerParams(vmem_limit_bytes=63 << 20),
        name="rotate",
    )(q_points, rp_vectors, rp_weights[None, :], modes_rot, coarse)
    parts = lax.all_to_all(rotated, "lat", 0, 0, tiled=True)

    index = lax.axis_index("kpt")
    at = jnp.stack([index // 2, index % 2]).astype(jnp.int32)
    lattice = jnp.concatenate(
        [re_vectors.T, re_weights[None, :], jnp.zeros((4, re_weights.shape[0]), jnp.int32)], axis=0
    )
    phase, right, left = pl.pallas_call(
        prep_body,
        out_shape=(
            jax.ShapeDtypeStruct((2 * KPTS, 512), bf16),
            jax.ShapeDtypeStruct((3, BANDS, BANDS, 128), f32),
            jax.ShapeDtypeStruct((3, BANDS, BANDS, 128), f32),
        ),
        in_specs=[smem()] + [vmem()] * 6,
        out_specs=(vmem(),) * 3,
        compiler_params=params(),
        name="prep",
    )(
        at,
        k_points,
        lattice,
        u_k.reshape(2, KPTS, BANDS * BANDS),
        u_kq.reshape(2, NQ * KPTS, BANDS * BANDS),
        mask_k,
        mask_kq.reshape(NQ * KPTS, BANDS),
    )

    own = pl.pallas_call(
        sum_body,
        out_shape=jax.ShapeDtypeStruct((ROWS, LANES), bf16),
        in_specs=[vmem()],
        out_specs=vmem(),
        compiler_params=params(),
        name="add_up",
    )(parts)

    def shift(x, step):
        return lax.ppermute(x, "kpt", [(i, (i + 2 * step) % 16) for i in range(16)])

    def swap(x):
        return lax.ppermute(x, "kpt", [(i, i ^ 1) for i in range(16)])

    up = shift(own, 3)
    down = shift(own, -3)
    packed, pair = pl.pallas_call(
        pack_body,
        out_shape=(
            jax.ShapeDtypeStruct((3 * ROWS, LANES), bf16),
            jax.ShapeDtypeStruct((2 * ROWS, LANES), bf16),
        ),
        in_specs=[vmem()] * 3 + [pl.BlockSpec(memory_space=pl.ANY)],
        out_specs=(vmem(), vmem()),
        compiler_params=params(),
        name="pack",
    )(own, up, down, phase)
    plus = shift(packed, 1)
    minus = shift(pair, -1)
    near = [packed, plus, minus]
    far = [swap(x) for x in near]

    result = pl.pallas_call(
        couple_body,
        out_shape=jax.ShapeDtypeStruct((2, KPTS, NQ, LANES), bf16),
        in_specs=[vmem()] * 9,
        out_specs=hbm(),
        scratch_shapes=[
            pltpu.VMEM((2, 2 * PER, 128, 128), f32),
            pltpu.VMEM((3, LANES, 128), f32),
            pltpu.VMEM((3, PER * BANDS, BANDS, 128), f32),
            pltpu.VMEM((2, BANDS, BANDS, 128), f32),
            pltpu.VMEM((2, KPTS, NQ, LANES), bf16),
            pltpu.SemaphoreType.DMA((PER,)),
        ],
        compiler_params=params(),
        name="couple",
    )(*near, *far, phase, right, left)
    return result


def solution(mesh):
    placed = (
        P(None, "lat", "kpt", None),
        P("lat", None),
        P("lat"),
        P(),
        P(),
        P(),
        P("kpt", None),
        P(),
        P(None, "kpt", None, None),
        P(None, None, "kpt", None, None),
        P("kpt", None),
        P(None, "kpt", None),
    )
    return jax.shard_map(
        per_device,
        mesh=mesh,
        in_specs=placed,
        out_specs=P(None, "kpt", None, "lat"),
        check_vma=False,
    )
```

```python
import jax
import jax.numpy as jnp
from jax import lax
from jax.experimental import pallas as pl
from jax.experimental.pallas import tpu as pltpu
from jax.sharding import PartitionSpec as P

two_pi = 6.283185307179586
f32 = jnp.float32
bf16 = jnp.bfloat16

MODES = 48
BANDS = 16
CELLS = 16
LAT = 16
NQ = 2
KPTS = 64
PER = MODES // LAT
LANES = PER * BANDS * BANDS
STRIDE_S = 2 * MODES + 1
ROWS = NQ * 2 * CELLS
STRIDE_O = ROWS + 1
CHUNKS = 4
CHUNK = MODES * BANDS * BANDS // CHUNKS


def rotate_body(
    qp_hbm, rv_hbm, rw_hbm, rot_hbm, coarse_hbm, out_ref,
    qp_ref, rv_ref, rw_ref, rot_ref, coarse_ref, mat_ref, s_ref, o_ref, sems,
):
    small = [
        pltpu.make_async_copy(src, dst, sems.at[i])
        for i, (src, dst) in enumerate(
            [(qp_hbm, qp_ref), (rv_hbm, rv_ref), (rw_hbm, rw_ref), (rot_hbm, rot_ref)]
        )
    ]
    large = []
    for part in range(2):
        for i in range(CHUNKS):
            lanes = pl.ds(i * CHUNK, CHUNK)
            large.append(
                pltpu.make_async_copy(
                    coarse_hbm.at[part, 0, :, lanes],
                    coarse_ref.at[part, :, lanes],
                    sems.at[4 + part * CHUNKS + i],
                )
            )
    for copy in small + large:
        copy.start()
    for copy in small:
        copy.wait()
    weight = 1.0 / jnp.full((8, 128), rw_ref[0, 0], jnp.int32).astype(f32)
    for q in range(NQ):
        arg = two_pi * (
            qp_ref[q, 0] * rv_ref[0, 0].astype(f32)
            + qp_ref[q, 1] * rv_ref[0, 1].astype(f32)
            + qp_ref[q, 2] * rv_ref[0, 2].astype(f32)
        )
        angle = jnp.full((8, 128), arg, f32)
        pr = (jnp.cos(angle) * weight).astype(bf16).astype(f32)[0:1, 0:1]
        pi = (jnp.sin(angle) * weight).astype(bf16).astype(f32)[0:1, 0:1]
        rr = rot_ref[0, q].astype(f32)
        ri = rot_ref[1, q].astype(f32)
        cr = rr * pr - ri * pi
        ci = rr * pi + ri * pr
        top = jnp.concatenate([cr, -ci], axis=0)
        low = jnp.concatenate([ci, cr], axis=0)
        mat_ref[q * 96:q * 96 + 48, 0:96] = top.T
        mat_ref[q * 96 + 48:q * 96 + 96, 0:96] = low.T
    rows = []
    for g in range(2 * NQ):
        for j in range(PER):
            rows.append(mat_ref[pl.ds(g * 48 + j, LAT, stride=PER), :])
    mat = jnp.concatenate(rows, axis=0)[:, 0:96].astype(bf16)
    for part in range(2):
        for m in range(MODES):
            if m * 256 % CHUNK == 0:
                large[part * CHUNKS + m * 256 // CHUNK].wait()
            for h in range(2):
                at = (2 * m + h) * 128
                tile = coarse_ref[part, :, at:at + 128].astype(f32)
                s_ref[h, pl.ds(part * MODES + m, CELLS, stride=STRIDE_S), :] = tile
    for e in range(CELLS):
        block = jnp.concatenate(
            [s_ref[h, e * STRIDE_S:e * STRIDE_S + 96, :].astype(bf16) for h in range(2)], axis=1
        )
        both = jnp.dot(mat, block, preferred_element_type=f32)
        for h in range(2):
            res = both[:, h * 128:(h + 1) * 128]
            for g in range(2 * NQ):
                for j in range(PER):
                    at = (g * PER + j) * LAT
                    o_ref[2 * j + h, pl.ds(g * CELLS + e, LAT, stride=STRIDE_O), :] = res[at:at + LAT]
    for l in range(LAT):
        for t in range(2 * PER):
            out_ref[l, :, t * 128:(t + 1) * 128] = o_ref[t, l * STRIDE_O:l * STRIDE_O + ROWS, :].astype(bf16)


def sum_body(x_ref, out_ref):
    for r in range(0, ROWS, 16):
        acc = x_ref[0, r:r + 16, :].astype(f32)
        for p in range(1, LAT):
            acc = acc + x_ref[p, r:r + 16, :].astype(f32)
        out_ref[r:r + 16, :] = acc.astype(bf16)


def prep_body(at_ref, kp_ref, rv_ref, u_ref, uq_ref, mk_ref, mq_ref, ph_ref, uo_ref, lo_ref):
    z = at_ref[0]
    c = at_ref[1]
    lane = lax.broadcasted_iota(jnp.int32, (256, 512), 1)
    src = lax.broadcasted_iota(jnp.int32, (256, 512), 0)
    block = lane >> 5
    home = (((z - block) & 7) << 1) + (c ^ (block >> 3))
    cell = (home << 4) + (lane & 15)
    pick = jnp.where(src == cell, 1.0, 0.0).astype(bf16)
    vec = jnp.dot(rv_ref[...].astype(f32).astype(bf16), pick, preferred_element_type=f32)
    kp = kp_ref[...]
    arg = two_pi * (
        kp[:, 0:1] * vec[0:1, :] + kp[:, 1:2] * vec[1:2, :] + kp[:, 2:3] * vec[2:3, :]
    )
    inverse = 1.0 / vec[3:4, :]
    co = jnp.cos(arg) * inverse
    si = jnp.sin(arg) * inverse
    first = (lax.broadcasted_iota(jnp.int32, (KPTS, 512), 1) & 16) == 0
    ph_ref[0:KPTS, :] = jnp.where(first, co, -si).astype(bf16)
    ph_ref[KPTS:2 * KPTS, :] = jnp.where(first, si, co).astype(bf16)
    row = lax.broadcasted_iota(jnp.int32, (KPTS, 128), 0)
    col = lax.broadcasted_iota(jnp.int32, (KPTS, 128), 1)
    spread = jnp.where((col >> 1) == row, 1.0, 0.0).astype(bf16)
    row2 = lax.broadcasted_iota(jnp.int32, (128, 128), 0)
    col2 = lax.broadcasted_iota(jnp.int32, (128, 128), 1)
    place = jnp.where((((col2 & 1) << 6) + (col2 >> 1)) == row2, 1.0, 0.0).astype(bf16)
    dims = (((0,), (0,)), ((), ()))
    mk = lax.dot_general(mk_ref[...].astype(f32).astype(bf16), spread, dims, preferred_element_type=f32)
    mq = lax.dot_general(mq_ref[...].astype(f32).astype(bf16), place, dims, preferred_element_type=f32)
    ur, ui = (
        lax.dot_general(u_ref[part], spread, dims, preferred_element_type=f32) for part in range(2)
    )
    lr, li = (
        lax.dot_general(uq_ref[part], place, dims, preferred_element_type=f32) for part in range(2)
    )
    for i, (u, left) in enumerate(((ur, lr), (ui - ur, -(li + lr)), (ur + ui, lr - li))):
        for b in range(BANDS):
            uo_ref[i, b] = u[b * 16:(b + 1) * 16] * mk
            lo_ref[i, b] = left[b * 16:(b + 1) * 16] * mq


def pack_body(own_ref, back_ref, out_ref):
    out_ref[0:ROWS, :] = own_ref[...]
    out_ref[ROWS:2 * ROWS, :] = back_ref[...]


def pack_all_body(own_ref, back_ref, ahead_ref, across_ref, order_ref, pair_ref, out_ref):
    pair_ref[0:ROWS, :] = own_ref[...]
    pair_ref[ROWS:2 * ROWS, :] = ahead_ref[...]
    for i, ref in enumerate((own_ref, back_ref, ahead_ref, across_ref)):
        out_ref[i * ROWS:(i + 1) * ROWS, :] = ref[...]


PLACE = ((0, 0), (1, 0), (0, 1), (1, 1), (0, 3), (2, 1), (0, 2), (2, 0))


def couple_body(*refs):
    ph_ref, u_ref, l_ref, out_ref, y_ref, bl_ref, h_ref, r_ref = refs[6:]
    ph = ph_ref[...]
    for q in range(NQ):
        x = jnp.concatenate(
            [
                refs[side * 3 + i][j * ROWS + q * 32:j * ROWS + (q + 1) * 32, :]
                for side in range(2)
                for i, j in PLACE
            ],
            axis=0,
        )
        t = jnp.dot(ph, x, preferred_element_type=f32)
        for part in range(2):
            for v in range(2 * PER):
                y_ref[part, v, pl.ds(q, KPTS, stride=2), :] = t[
                    part * KPTS:(part + 1) * KPTS, v * 128:(v + 1) * 128
                ]
    for v in range(2 * PER):
        rows = slice(v * 128, (v + 1) * 128)
        xr, xi = (y_ref[part, v].T.astype(bf16).astype(f32) for part in range(2))
        bl_ref[0, rows, :] = xr + xi
        bl_ref[1, rows, :] = xr
        bl_ref[2, rows, :] = xi

    group = 4

    def first(i, _):
        base = i * group * BANDS
        acc = [[jnp.zeros((16, 128), f32) for _ in range(3)] for _ in range(group)]
        for b in range(BANDS):
            us = [u_ref[t, b] for t in range(3)]
            for s in range(group):
                for t in range(3):
                    acc[s][t] = acc[s][t] + bl_ref[t, pl.ds(base + s * BANDS + b, 1), :] * us[t]
        for s in range(group):
            hr = (acc[s][0] - acc[s][2]).astype(bf16).astype(f32)
            hi = (acc[s][0] + acc[s][1]).astype(bf16).astype(f32)
            h_ref[0, i * group + s] = hr + hi
            h_ref[1, i * group + s] = hr
            h_ref[2, i * group + s] = hi
        return 0

    lax.fori_loop(0, PER * BANDS // group, first, 0)

    per = BANDS // group

    def second(i, _):
        n = i // per
        c0 = (i - n * per) * group
        acc = [[jnp.zeros((16, 128), f32) for _ in range(3)] for _ in range(group)]
        for a in range(BANDS):
            hs = [h_ref[t, n * BANDS + a] for t in range(3)]
            for s in range(group):
                for t in range(3):
                    acc[s][t] = acc[s][t] + l_ref[t, a, pl.ds(c0 + s, 1), :] * hs[t]
        for s in range(group):
            r_ref[0, i * group + s] = acc[s][0] - acc[s][2]
            r_ref[1, i * group + s] = acc[s][0] + acc[s][1]
        return 0

    lax.fori_loop(0, PER * per, second, 0)
    for part in range(2):
        for v in range(2 * PER):
            tile = r_ref[part, v * 8:(v + 1) * 8].reshape(128, 128).T
            out_ref[part, :, :, v * 128:(v + 1) * 128] = tile.reshape(KPTS, NQ, 128).astype(bf16)


def vmem():
    return pl.BlockSpec(memory_space=pltpu.VMEM)


def hbm():
    return pl.BlockSpec(memory_space=pltpu.HBM)


def smem():
    return pl.BlockSpec(memory_space=pltpu.SMEM)


def params():
    return pltpu.CompilerParams(vmem_limit_bytes=40 << 20)


def per_device(
    coarse,
    rp_vectors,
    rp_weights,
    re_vectors,
    re_weights,
    q_points,
    k_points,
    modes_rot,
    u_k,
    u_kq,
    mask_k,
    mask_kq,
):
    rotated = pl.pallas_call(
        rotate_body,
        out_shape=jax.ShapeDtypeStruct((LAT, ROWS, LANES), bf16),
        in_specs=[hbm()] * 5,
        out_specs=vmem(),
        scratch_shapes=[
            pltpu.SMEM((NQ, 3), f32),
            pltpu.SMEM((1, 3), jnp.int32),
            pltpu.SMEM((1, 1), jnp.int32),
            pltpu.VMEM((2, NQ, MODES, MODES), bf16),
            pltpu.VMEM((2, CELLS, MODES * BANDS * BANDS), bf16),
            pltpu.VMEM((192, 128), f32),
            pltpu.VMEM((2, CELLS * STRIDE_S, 128), f32),
            pltpu.VMEM((2 * PER, LAT * STRIDE_O, 128), f32),
            pltpu.SemaphoreType.DMA((4 + 2 * CHUNKS,)),
        ],
        compiler_params=pltpu.CompilerParams(vmem_limit_bytes=63 << 20),
        name="rotate",
    )(q_points, rp_vectors, rp_weights[None, :], modes_rot, coarse)
    parts = lax.all_to_all(rotated, "lat", 0, 0, tiled=True)

    index = lax.axis_index("kpt")
    at = jnp.stack([index // 2, index % 2]).astype(jnp.int32)
    lattice = jnp.concatenate(
        [re_vectors.T, re_weights[None, :], jnp.zeros((4, re_weights.shape[0]), jnp.int32)], axis=0
    )
    phase, right, left = pl.pallas_call(
        prep_body,
        out_shape=(
            jax.ShapeDtypeStruct((2 * KPTS, 512), bf16),
            jax.ShapeDtypeStruct((3, BANDS, BANDS, 128), f32),
            jax.ShapeDtypeStruct((3, BANDS, BANDS, 128), f32),
        ),
        in_specs=[smem()] + [vmem()] * 6,
        out_specs=(vmem(),) * 3,
        compiler_params=params(),
        name="prep",
    )(
        at,
        k_points,
        lattice,
        u_k.reshape(2, KPTS, BANDS * BANDS),
        u_kq.reshape(2, NQ * KPTS, BANDS * BANDS),
        mask_k,
        mask_kq.reshape(NQ * KPTS, BANDS),
    )

    own = pl.pallas_call(
        sum_body,
        out_shape=jax.ShapeDtypeStruct((ROWS, LANES), bf16),
        in_specs=[vmem()],
        out_specs=vmem(),
        compiler_params=params(),
        name="add_up",
    )(parts)

    def shift(x, step):
        return lax.ppermute(x, "kpt", [(i, (i + 2 * step) % 16) for i in range(16)])

    def swap(x):
        return lax.ppermute(x, "kpt", [(i, i ^ 1) for i in range(16)])

    back = shift(own, 2)
    ahead = shift(own, -2)
    across = shift(own, 4)
    pair = pl.pallas_call(
        pack_body,
        out_shape=jax.ShapeDtypeStruct((2 * ROWS, LANES), bf16),
        in_specs=[vmem()] * 2,
        out_specs=vmem(),
        compiler_params=params(),
        name="pack",
    )(own, back)
    other, packed = pl.pallas_call(
        pack_all_body,
        out_shape=(
            jax.ShapeDtypeStruct((2 * ROWS, LANES), bf16),
            jax.ShapeDtypeStruct((4 * ROWS, LANES), bf16),
        ),
        in_specs=[vmem()] * 4 + [pl.BlockSpec(memory_space=pl.ANY)],
        out_specs=(vmem(), vmem()),
        compiler_params=params(),
        name="pack_all",
    )(own, back, ahead, across, phase)
    near = [packed, shift(pair, 1), shift(other, -1)]
    far = [swap(x) for x in near]

    result = pl.pallas_call(
        couple_body,
        out_shape=jax.ShapeDtypeStruct((2, KPTS, NQ, LANES), bf16),
        in_specs=[vmem()] * 9,
        out_specs=vmem(),
        scratch_shapes=[
            pltpu.VMEM((2, 2 * PER, 128, 128), f32),
            pltpu.VMEM((3, LANES, 128), f32),
            pltpu.VMEM((3, PER * BANDS, BANDS, 128), f32),
            pltpu.VMEM((2, PER * BANDS, BANDS, 128), f32),
        ],
        compiler_params=params(),
        name="couple",
    )(*near, *far, phase, right, left)
    return result


def solution(mesh):
    placed = (
        P(None, "lat", "kpt", None),
        P("lat", None),
        P("lat"),
        P(),
        P(),
        P(),
        P("kpt", None),
        P(),
        P(None, "kpt", None, None),
        P(None, None, "kpt", None, None),
        P("kpt", None),
        P(None, "kpt", None),
    )
    return jax.shard_map(
        per_device,
        mesh=mesh,
        in_specs=placed,
        out_specs=P(None, "kpt", None, "lat"),
        check_vma=False,
    )
```

```python
import jax
import jax.numpy as jnp
from jax import lax
from jax.experimental import pallas as pl
from jax.experimental.pallas import tpu as pltpu
from jax.sharding import PartitionSpec as P

two_pi = 6.283185307179586
f32 = jnp.float32
bf16 = jnp.bfloat16

MODES = 48
BANDS = 16
CELLS = 16
LAT = 16
NQ = 2
KPTS = 64
PER = MODES // LAT
LANES = PER * BANDS * BANDS
STRIDE_S = 2 * MODES + 1
ROWS = NQ * 2 * CELLS
STRIDE_O = ROWS + 1
CHUNKS = 4
CHUNK = MODES * BANDS * BANDS // CHUNKS


def rotate_body(
    qp_hbm, rv_hbm, rw_hbm, rot_hbm, coarse_hbm, out_ref,
    qp_ref, rv_ref, rw_ref, rot_ref, coarse_ref, mat_ref, s_ref, o_ref, sems,
):
    small = [
        pltpu.make_async_copy(src, dst, sems.at[i])
        for i, (src, dst) in enumerate(
            [(qp_hbm, qp_ref), (rv_hbm, rv_ref), (rw_hbm, rw_ref), (rot_hbm, rot_ref)]
        )
    ]
    large = []
    for part in range(2):
        for i in range(CHUNKS):
            lanes = pl.ds(i * CHUNK, CHUNK)
            large.append(
                pltpu.make_async_copy(
                    coarse_hbm.at[part, 0, :, lanes],
                    coarse_ref.at[part, :, lanes],
                    sems.at[4 + part * CHUNKS + i],
                )
            )
    for copy in small + large:
        copy.start()
    for copy in small:
        copy.wait()
    weight = 1.0 / jnp.full((8, 128), rw_ref[0, 0], jnp.int32).astype(f32)
    for q in range(NQ):
        arg = two_pi * (
            qp_ref[q, 0] * rv_ref[0, 0].astype(f32)
            + qp_ref[q, 1] * rv_ref[0, 1].astype(f32)
            + qp_ref[q, 2] * rv_ref[0, 2].astype(f32)
        )
        angle = jnp.full((8, 128), arg, f32)
        pr = (jnp.cos(angle) * weight).astype(bf16).astype(f32)[0:1, 0:1]
        pi = (jnp.sin(angle) * weight).astype(bf16).astype(f32)[0:1, 0:1]
        rr = rot_ref[0, q].astype(f32)
        ri = rot_ref[1, q].astype(f32)
        cr = rr * pr - ri * pi
        ci = rr * pi + ri * pr
        top = jnp.concatenate([cr, -ci], axis=0)
        low = jnp.concatenate([ci, cr], axis=0)
        mat_ref[q * 96:q * 96 + 48, 0:96] = top.T
        mat_ref[q * 96 + 48:q * 96 + 96, 0:96] = low.T
    rows = []
    for g in range(2 * NQ):
        for j in range(PER):
            rows.append(mat_ref[pl.ds(g * 48 + j, LAT, stride=PER), :])
    mat = jnp.concatenate(rows, axis=0)[:, 0:96].astype(bf16)
    for part in range(2):
        for m in range(MODES):
            if m * 256 % CHUNK == 0:
                large[part * CHUNKS + m * 256 // CHUNK].wait()
            for h in range(2):
                at = (2 * m + h) * 128
                tile = coarse_ref[part, :, at:at + 128].astype(f32)
                s_ref[h, pl.ds(part * MODES + m, CELLS, stride=STRIDE_S), :] = tile
    for e in range(CELLS):
        block = jnp.concatenate(
            [s_ref[h, e * STRIDE_S:e * STRIDE_S + 96, :].astype(bf16) for h in range(2)], axis=1
        )
        both = jnp.dot(mat, block, preferred_element_type=f32)
        for h in range(2):
            res = both[:, h * 128:(h + 1) * 128]
            for g in range(2 * NQ):
                for j in range(PER):
                    at = (g * PER + j) * LAT
                    o_ref[2 * j + h, pl.ds(g * CELLS + e, LAT, stride=STRIDE_O), :] = res[at:at + LAT]
    for l in range(LAT):
        for t in range(2 * PER):
            out_ref[l, :, t * 128:(t + 1) * 128] = o_ref[t, l * STRIDE_O:l * STRIDE_O + ROWS, :].astype(bf16)


def sum_body(x_ref, out_ref):
    for r in range(0, ROWS, 16):
        acc = x_ref[0, r:r + 16, :].astype(f32)
        for p in range(1, LAT):
            acc = acc + x_ref[p, r:r + 16, :].astype(f32)
        out_ref[r:r + 16, :] = acc.astype(bf16)


def prep_body(at_ref, kp_ref, rv_ref, u_ref, uq_ref, mk_ref, mq_ref, ph_ref, uo_ref, lo_ref):
    z = at_ref[0]
    c = at_ref[1]
    lane = lax.broadcasted_iota(jnp.int32, (256, 512), 1)
    src = lax.broadcasted_iota(jnp.int32, (256, 512), 0)
    block = lane >> 5
    home = (((z - block) & 7) << 1) + (c ^ (block >> 3))
    cell = (home << 4) + (lane & 15)
    pick = jnp.where(src == cell, 1.0, 0.0).astype(bf16)
    vec = jnp.dot(rv_ref[...].astype(f32).astype(bf16), pick, preferred_element_type=f32)
    kp = kp_ref[...]
    arg = two_pi * (
        kp[:, 0:1] * vec[0:1, :] + kp[:, 1:2] * vec[1:2, :] + kp[:, 2:3] * vec[2:3, :]
    )
    inverse = 1.0 / vec[3:4, :]
    co = jnp.cos(arg) * inverse
    si = jnp.sin(arg) * inverse
    first = (lax.broadcasted_iota(jnp.int32, (KPTS, 512), 1) & 16) == 0
    ph_ref[0:KPTS, :] = jnp.where(first, co, -si).astype(bf16)
    ph_ref[KPTS:2 * KPTS, :] = jnp.where(first, si, co).astype(bf16)
    row = lax.broadcasted_iota(jnp.int32, (KPTS, 128), 0)
    col = lax.broadcasted_iota(jnp.int32, (KPTS, 128), 1)
    spread = jnp.where((col >> 1) == row, 1.0, 0.0).astype(bf16)
    row2 = lax.broadcasted_iota(jnp.int32, (128, 128), 0)
    col2 = lax.broadcasted_iota(jnp.int32, (128, 128), 1)
    place = jnp.where((((col2 & 1) << 6) + (col2 >> 1)) == row2, 1.0, 0.0).astype(bf16)
    dims = (((0,), (0,)), ((), ()))
    mk = lax.dot_general(mk_ref[...].astype(f32).astype(bf16), spread, dims, preferred_element_type=f32)
    mq = lax.dot_general(mq_ref[...].astype(f32).astype(bf16), place, dims, preferred_element_type=f32)
    ur, ui = (
        lax.dot_general(u_ref[part], spread, dims, preferred_element_type=f32) for part in range(2)
    )
    lr, li = (
        lax.dot_general(uq_ref[part], place, dims, preferred_element_type=f32) for part in range(2)
    )
    for i, (u, left) in enumerate(((ur, lr), (ui - ur, -(li + lr)), (ur + ui, lr - li))):
        for b in range(BANDS):
            uo_ref[i, b] = u[b * 16:(b + 1) * 16] * mk
            lo_ref[i, b] = left[b * 16:(b + 1) * 16] * mq


def pack_body(own_ref, back_ref, ahead_ref, order_ref, three_ref, two_ref):
    for i, ref in enumerate((own_ref, back_ref, ahead_ref)):
        value = ref[...]
        three_ref[i * ROWS:(i + 1) * ROWS, :] = value
        if i > 0:
            two_ref[(i - 1) * ROWS:i * ROWS, :] = value


PLACE = ((0, 0), (1, 0), (2, 0), (0, 1), (1, 1), (2, 1), (0, 2), (1, 2))


def couple_body(*refs):
    ph_ref, u_ref, l_ref, out_ref, y_ref, bl_ref, h_ref, r_ref = refs[6:]
    ph = ph_ref[...]
    for q in range(NQ):
        x = jnp.concatenate(
            [
                refs[side * 3 + i][j * ROWS + q * 32:j * ROWS + (q + 1) * 32, :]
                for side in range(2)
                for i, j in PLACE
            ],
            axis=0,
        )
        t = jnp.dot(ph, x, preferred_element_type=f32)
        for part in range(2):
            for v in range(2 * PER):
                y_ref[part, v, pl.ds(q, KPTS, stride=2), :] = t[
                    part * KPTS:(part + 1) * KPTS, v * 128:(v + 1) * 128
                ]
    for v in range(2 * PER):
        rows = slice(v * 128, (v + 1) * 128)
        xr, xi = (y_ref[part, v].T.astype(bf16).astype(f32) for part in range(2))
        bl_ref[0, rows, :] = xr + xi
        bl_ref[1, rows, :] = xr
        bl_ref[2, rows, :] = xi

    group = 4

    def first(i, _):
        base = i * group * BANDS
        acc = [[jnp.zeros((16, 128), f32) for _ in range(3)] for _ in range(group)]
        for b in range(BANDS):
            us = [u_ref[t, b] for t in range(3)]
            for s in range(group):
                for t in range(3):
                    acc[s][t] = acc[s][t] + bl_ref[t, pl.ds(base + s * BANDS + b, 1), :] * us[t]
        for s in range(group):
            hr = (acc[s][0] - acc[s][2]).astype(bf16).astype(f32)
            hi = (acc[s][0] + acc[s][1]).astype(bf16).astype(f32)
            h_ref[0, i * group + s] = hr + hi
            h_ref[1, i * group + s] = hr
            h_ref[2, i * group + s] = hi
        return 0

    lax.fori_loop(0, PER * BANDS // group, first, 0)

    per = BANDS // group

    def second(i, _):
        n = i // per
        c0 = (i - n * per) * group
        acc = [[jnp.zeros((16, 128), f32) for _ in range(3)] for _ in range(group)]
        for a in range(BANDS):
            hs = [h_ref[t, n * BANDS + a] for t in range(3)]
            for s in range(group):
                for t in range(3):
                    acc[s][t] = acc[s][t] + l_ref[t, a, pl.ds(c0 + s, 1), :] * hs[t]
        for s in range(group):
            r_ref[0, i * group + s] = acc[s][0] - acc[s][2]
            r_ref[1, i * group + s] = acc[s][0] + acc[s][1]
        return 0

    lax.fori_loop(0, PER * per, second, 0)
    for part in range(2):
        for v in range(2 * PER):
            tile = r_ref[part, v * 8:(v + 1) * 8].reshape(128, 128).T
            out_ref[part, :, :, v * 128:(v + 1) * 128] = tile.reshape(KPTS, NQ, 128).astype(bf16)


def vmem():
    return pl.BlockSpec(memory_space=pltpu.VMEM)


def hbm():
    return pl.BlockSpec(memory_space=pltpu.HBM)


def smem():
    return pl.BlockSpec(memory_space=pltpu.SMEM)


def params():
    return pltpu.CompilerParams(vmem_limit_bytes=40 << 20)


def per_device(
    coarse,
    rp_vectors,
    rp_weights,
    re_vectors,
    re_weights,
    q_points,
    k_points,
    modes_rot,
    u_k,
    u_kq,
    mask_k,
    mask_kq,
):
    rotated = pl.pallas_call(
        rotate_body,
        out_shape=jax.ShapeDtypeStruct((LAT, ROWS, LANES), bf16),
        in_specs=[hbm()] * 5,
        out_specs=vmem(),
        scratch_shapes=[
            pltpu.SMEM((NQ, 3), f32),
            pltpu.SMEM((1, 3), jnp.int32),
            pltpu.SMEM((1, 1), jnp.int32),
            pltpu.VMEM((2, NQ, MODES, MODES), bf16),
            pltpu.VMEM((2, CELLS, MODES * BANDS * BANDS), bf16),
            pltpu.VMEM((192, 128), f32),
            pltpu.VMEM((2, CELLS * STRIDE_S, 128), f32),
            pltpu.VMEM((2 * PER, LAT * STRIDE_O, 128), f32),
            pltpu.SemaphoreType.DMA((4 + 2 * CHUNKS,)),
        ],
        compiler_params=pltpu.CompilerParams(vmem_limit_bytes=63 << 20),
        name="rotate",
    )(q_points, rp_vectors, rp_weights[None, :], modes_rot, coarse)
    parts = lax.all_to_all(rotated, "lat", 0, 0, tiled=True)

    index = lax.axis_index("kpt")
    at = jnp.stack([index // 2, index % 2]).astype(jnp.int32)
    lattice = jnp.concatenate(
        [re_vectors.T, re_weights[None, :], jnp.zeros((4, re_weights.shape[0]), jnp.int32)], axis=0
    )
    phase, right, left = pl.pallas_call(
        prep_body,
        out_shape=(
            jax.ShapeDtypeStruct((2 * KPTS, 512), bf16),
            jax.ShapeDtypeStruct((3, BANDS, BANDS, 128), f32),
            jax.ShapeDtypeStruct((3, BANDS, BANDS, 128), f32),
        ),
        in_specs=[smem()] + [vmem()] * 6,
        out_specs=(vmem(),) * 3,
        compiler_params=params(),
        name="prep",
    )(
        at,
        k_points,
        lattice,
        u_k.reshape(2, KPTS, BANDS * BANDS),
        u_kq.reshape(2, NQ * KPTS, BANDS * BANDS),
        mask_k,
        mask_kq.reshape(NQ * KPTS, BANDS),
    )

    own = pl.pallas_call(
        sum_body,
        out_shape=jax.ShapeDtypeStruct((ROWS, LANES), bf16),
        in_specs=[vmem()],
        out_specs=vmem(),
        compiler_params=params(),
        name="add_up",
    )(parts)

    def shift(x, step):
        return lax.ppermute(x, "kpt", [(i, (i + 2 * step) % 16) for i in range(16)])

    def swap(x):
        return lax.ppermute(x, "kpt", [(i, i ^ 1) for i in range(16)])

    back = shift(own, 3)
    ahead = shift(own, -2)
    packed, pair = pl.pallas_call(
        pack_body,
        out_shape=(
            jax.ShapeDtypeStruct((3 * ROWS, LANES), bf16),
            jax.ShapeDtypeStruct((2 * ROWS, LANES), bf16),
        ),
        in_specs=[vmem()] * 3 + [pl.BlockSpec(memory_space=pl.ANY)],
        out_specs=(vmem(), vmem()),
        compiler_params=params(),
        name="pack",
    )(own, back, ahead, phase)
    plus = shift(packed, 1)
    minus = shift(pair, -1)
    near = [packed, plus, minus]
    far = [swap(x) for x in near]

    result = pl.pallas_call(
        couple_body,
        out_shape=jax.ShapeDtypeStruct((2, KPTS, NQ, LANES), bf16),
        in_specs=[vmem()] * 9,
        out_specs=vmem(),
        scratch_shapes=[
            pltpu.VMEM((2, 2 * PER, 128, 128), f32),
            pltpu.VMEM((3, LANES, 128), f32),
            pltpu.VMEM((3, PER * BANDS, BANDS, 128), f32),
            pltpu.VMEM((2, PER * BANDS, BANDS, 128), f32),
        ],
        compiler_params=params(),
        name="couple",
    )(*near, *far, phase, right, left)
    return result


def solution(mesh):
    placed = (
        P(None, "lat", "kpt", None),
        P("lat", None),
        P("lat"),
        P(),
        P(),
        P(),
        P("kpt", None),
        P(),
        P(None, "kpt", None, None),
        P(None, None, "kpt", None, None),
        P("kpt", None),
        P(None, "kpt", None),
    )
    return jax.shard_map(
        per_device,
        mesh=mesh,
        in_specs=placed,
        out_specs=P(None, "kpt", None, "lat"),
        check_vma=False,
    )
```

```python
import jax
import jax.numpy as jnp
from jax import lax
from jax.experimental import pallas as pl
from jax.experimental.pallas import tpu as pltpu
from jax.sharding import PartitionSpec as P

two_pi = 6.283185307179586
f32 = jnp.float32
bf16 = jnp.bfloat16

MODES = 48
BANDS = 16
CELLS = 16
LAT = 16
NQ = 2
KPTS = 64
PER = MODES // LAT
LANES = PER * BANDS * BANDS
STRIDE_S = 2 * MODES + 1
ROWS = NQ * 2 * CELLS
STRIDE_O = ROWS + 1
CHUNKS = 4
CHUNK = MODES * BANDS * BANDS // CHUNKS


def rotate_body(
    qp_hbm, rv_hbm, rw_hbm, rot_hbm, coarse_hbm, out_ref,
    qp_ref, rv_ref, rw_ref, rot_ref, coarse_ref, mat_ref, s_ref, o_ref, sems,
):
    small = [
        pltpu.make_async_copy(src, dst, sems.at[i])
        for i, (src, dst) in enumerate(
            [(qp_hbm, qp_ref), (rv_hbm, rv_ref), (rw_hbm, rw_ref), (rot_hbm, rot_ref)]
        )
    ]
    large = []
    for part in range(2):
        for i in range(CHUNKS):
            lanes = pl.ds(i * CHUNK, CHUNK)
            large.append(
                pltpu.make_async_copy(
                    coarse_hbm.at[part, 0, :, lanes],
                    coarse_ref.at[part, :, lanes],
                    sems.at[4 + part * CHUNKS + i],
                )
            )
    for copy in small + large:
        copy.start()
    for copy in small:
        copy.wait()
    weight = 1.0 / jnp.full((8, 128), rw_ref[0, 0], jnp.int32).astype(f32)
    for q in range(NQ):
        arg = two_pi * (
            qp_ref[q, 0] * rv_ref[0, 0].astype(f32)
            + qp_ref[q, 1] * rv_ref[0, 1].astype(f32)
            + qp_ref[q, 2] * rv_ref[0, 2].astype(f32)
        )
        angle = jnp.full((8, 128), arg, f32)
        pr = (jnp.cos(angle) * weight).astype(bf16).astype(f32)[0:1, 0:1]
        pi = (jnp.sin(angle) * weight).astype(bf16).astype(f32)[0:1, 0:1]
        rr = rot_ref[0, q].astype(f32)
        ri = rot_ref[1, q].astype(f32)
        cr = rr * pr - ri * pi
        ci = rr * pi + ri * pr
        top = jnp.concatenate([cr, -ci], axis=0)
        low = jnp.concatenate([ci, cr], axis=0)
        mat_ref[q * 96:q * 96 + 48, 0:96] = top.T
        mat_ref[q * 96 + 48:q * 96 + 96, 0:96] = low.T
    rows = []
    for g in range(2 * NQ):
        for j in range(PER):
            rows.append(mat_ref[pl.ds(g * 48 + j, LAT, stride=PER), :])
    mat = jnp.concatenate(rows, axis=0)[:, 0:96].astype(bf16)
    for part in range(2):
        for m in range(MODES):
            if m * 256 % CHUNK == 0:
                large[part * CHUNKS + m * 256 // CHUNK].wait()
            for h in range(2):
                at = (2 * m + h) * 128
                tile = coarse_ref[part, :, at:at + 128].astype(f32)
                s_ref[h, pl.ds(part * MODES + m, CELLS, stride=STRIDE_S), :] = tile
    for e in range(CELLS):
        block = jnp.concatenate(
            [s_ref[h, e * STRIDE_S:e * STRIDE_S + 96, :].astype(bf16) for h in range(2)], axis=1
        )
        both = jnp.dot(mat, block, preferred_element_type=f32)
        for h in range(2):
            res = both[:, h * 128:(h + 1) * 128]
            for g in range(2 * NQ):
                for j in range(PER):
                    at = (g * PER + j) * LAT
                    o_ref[2 * j + h, pl.ds(g * CELLS + e, LAT, stride=STRIDE_O), :] = res[at:at + LAT]
    for l in range(LAT):
        for t in range(2 * PER):
            out_ref[l, :, t * 128:(t + 1) * 128] = o_ref[t, l * STRIDE_O:l * STRIDE_O + ROWS, :].astype(bf16)


def sum_body(x_ref, out_ref):
    for r in range(0, ROWS, 16):
        acc = x_ref[0, r:r + 16, :].astype(f32)
        for p in range(1, LAT):
            acc = acc + x_ref[p, r:r + 16, :].astype(f32)
        out_ref[r:r + 16, :] = acc.astype(bf16)


def prep_body(at_ref, kp_ref, rv_ref, u_ref, uq_ref, mk_ref, mq_ref, ph_ref, uo_ref, lo_ref):
    z = at_ref[0]
    c = at_ref[1]
    lane = lax.broadcasted_iota(jnp.int32, (256, 512), 1)
    src = lax.broadcasted_iota(jnp.int32, (256, 512), 0)
    block = lane >> 5
    home = (((z - block) & 7) << 1) + (c ^ (block >> 3))
    cell = (home << 4) + (lane & 15)
    pick = jnp.where(src == cell, 1.0, 0.0).astype(bf16)
    vec = jnp.dot(rv_ref[...].astype(f32).astype(bf16), pick, preferred_element_type=f32)
    kp = kp_ref[...]
    arg = two_pi * (
        kp[:, 0:1] * vec[0:1, :] + kp[:, 1:2] * vec[1:2, :] + kp[:, 2:3] * vec[2:3, :]
    )
    inverse = 1.0 / vec[3:4, :]
    co = jnp.cos(arg) * inverse
    si = jnp.sin(arg) * inverse
    first = (lax.broadcasted_iota(jnp.int32, (KPTS, 512), 1) & 16) == 0
    ph_ref[0:KPTS, :] = jnp.where(first, co, -si).astype(bf16)
    ph_ref[KPTS:2 * KPTS, :] = jnp.where(first, si, co).astype(bf16)
    row = lax.broadcasted_iota(jnp.int32, (KPTS, 128), 0)
    col = lax.broadcasted_iota(jnp.int32, (KPTS, 128), 1)
    spread = jnp.where((col >> 1) == row, 1.0, 0.0).astype(bf16)
    row2 = lax.broadcasted_iota(jnp.int32, (128, 128), 0)
    col2 = lax.broadcasted_iota(jnp.int32, (128, 128), 1)
    place = jnp.where((((col2 & 1) << 6) + (col2 >> 1)) == row2, 1.0, 0.0).astype(bf16)
    dims = (((0,), (0,)), ((), ()))
    mk = lax.dot_general(mk_ref[...].astype(f32).astype(bf16), spread, dims, preferred_element_type=f32)
    mq = lax.dot_general(mq_ref[...].astype(f32).astype(bf16), place, dims, preferred_element_type=f32)
    ur, ui = (
        lax.dot_general(u_ref[part], spread, dims, preferred_element_type=f32) for part in range(2)
    )
    lr, li = (
        lax.dot_general(uq_ref[part], place, dims, preferred_element_type=f32) for part in range(2)
    )
    for i, (u, left) in enumerate(((ur, lr), (ui - ur, -(li + lr)), (ur + ui, lr - li))):
        for b in range(BANDS):
            uo_ref[i, b] = u[b * 16:(b + 1) * 16] * mk
            lo_ref[i, b] = left[b * 16:(b + 1) * 16] * mq


def pack_body(own_ref, back_ref, ahead_ref, three_ref, two_ref):
    for i, ref in enumerate((own_ref, back_ref, ahead_ref)):
        value = ref[...]
        three_ref[i * ROWS:(i + 1) * ROWS, :] = value
        if i > 0:
            two_ref[(i - 1) * ROWS:i * ROWS, :] = value


PLACE = ((0, 0), (1, 0), (2, 0), (0, 1), (1, 1), (2, 1), (0, 2), (1, 2))


def couple_body(*refs):
    ph_ref, u_ref, l_ref, out_ref, y_ref, bl_ref, h_ref, r_ref = refs[6:]
    ph = ph_ref[...]
    for q in range(NQ):
        x = jnp.concatenate(
            [
                refs[side * 3 + i][j * ROWS + q * 32:j * ROWS + (q + 1) * 32, :]
                for side in range(2)
                for i, j in PLACE
            ],
            axis=0,
        )
        t = jnp.dot(ph, x, preferred_element_type=f32)
        for part in range(2):
            for v in range(2 * PER):
                y_ref[part, v, pl.ds(q, KPTS, stride=2), :] = t[
                    part * KPTS:(part + 1) * KPTS, v * 128:(v + 1) * 128
                ]
    for v in range(2 * PER):
        rows = slice(v * 128, (v + 1) * 128)
        xr, xi = (y_ref[part, v].T.astype(bf16).astype(f32) for part in range(2))
        bl_ref[0, rows, :] = xr + xi
        bl_ref[1, rows, :] = xr
        bl_ref[2, rows, :] = xi

    group = 4

    def first(i, _):
        base = i * group * BANDS
        acc = [[jnp.zeros((16, 128), f32) for _ in range(3)] for _ in range(group)]
        for b in range(BANDS):
            us = [u_ref[t, b] for t in range(3)]
            for s in range(group):
                for t in range(3):
                    acc[s][t] = acc[s][t] + bl_ref[t, pl.ds(base + s * BANDS + b, 1), :] * us[t]
        for s in range(group):
            hr = (acc[s][0] - acc[s][2]).astype(bf16).astype(f32)
            hi = (acc[s][0] + acc[s][1]).astype(bf16).astype(f32)
            h_ref[0, i * group + s] = hr + hi
            h_ref[1, i * group + s] = hr
            h_ref[2, i * group + s] = hi
        return 0

    lax.fori_loop(0, PER * BANDS // group, first, 0)

    per = BANDS // group

    def second(i, _):
        n = i // per
        c0 = (i - n * per) * group
        acc = [[jnp.zeros((16, 128), f32) for _ in range(3)] for _ in range(group)]
        for a in range(BANDS):
            hs = [h_ref[t, n * BANDS + a] for t in range(3)]
            for s in range(group):
                for t in range(3):
                    acc[s][t] = acc[s][t] + l_ref[t, a, pl.ds(c0 + s, 1), :] * hs[t]
        for s in range(group):
            r_ref[0, i * group + s] = acc[s][0] - acc[s][2]
            r_ref[1, i * group + s] = acc[s][0] + acc[s][1]
        return 0

    lax.fori_loop(0, PER * per, second, 0)
    for part in range(2):
        for v in range(2 * PER):
            tile = r_ref[part, v * 8:(v + 1) * 8].reshape(128, 128).T
            out_ref[part, :, :, v * 128:(v + 1) * 128] = tile.reshape(KPTS, NQ, 128).astype(bf16)


def vmem():
    return pl.BlockSpec(memory_space=pltpu.VMEM)


def hbm():
    return pl.BlockSpec(memory_space=pltpu.HBM)


def smem():
    return pl.BlockSpec(memory_space=pltpu.SMEM)


def params():
    return pltpu.CompilerParams(vmem_limit_bytes=40 << 20)


def per_device(
    coarse,
    rp_vectors,
    rp_weights,
    re_vectors,
    re_weights,
    q_points,
    k_points,
    modes_rot,
    u_k,
    u_kq,
    mask_k,
    mask_kq,
):
    rotated = pl.pallas_call(
        rotate_body,
        out_shape=jax.ShapeDtypeStruct((LAT, ROWS, LANES), bf16),
        in_specs=[hbm()] * 5,
        out_specs=vmem(),
        scratch_shapes=[
            pltpu.SMEM((NQ, 3), f32),
            pltpu.SMEM((1, 3), jnp.int32),
            pltpu.SMEM((1, 1), jnp.int32),
            pltpu.VMEM((2, NQ, MODES, MODES), bf16),
            pltpu.VMEM((2, CELLS, MODES * BANDS * BANDS), bf16),
            pltpu.VMEM((192, 128), f32),
            pltpu.VMEM((2, CELLS * STRIDE_S, 128), f32),
            pltpu.VMEM((2 * PER, LAT * STRIDE_O, 128), f32),
            pltpu.SemaphoreType.DMA((4 + 2 * CHUNKS,)),
        ],
        compiler_params=pltpu.CompilerParams(vmem_limit_bytes=40 << 20),
        name="rotate",
    )(
        pltpu.with_memory_space_constraint(q_points, pltpu.HBM),
        pltpu.with_memory_space_constraint(rp_vectors, pltpu.HBM),
        rp_weights[None, :],
        pltpu.with_memory_space_constraint(modes_rot, pltpu.HBM),
        pltpu.with_memory_space_constraint(coarse, pltpu.HBM),
    )
    parts = lax.all_to_all(rotated, "lat", 0, 0, tiled=True)

    index = lax.axis_index("kpt")
    at = jnp.stack([index // 2, index % 2]).astype(jnp.int32)
    lattice = jnp.concatenate(
        [re_vectors.T, re_weights[None, :], jnp.zeros((4, re_weights.shape[0]), jnp.int32)], axis=0
    )
    phase, right, left = pl.pallas_call(
        prep_body,
        out_shape=(
            jax.ShapeDtypeStruct((2 * KPTS, 512), bf16),
            jax.ShapeDtypeStruct((3, BANDS, BANDS, 128), f32),
            jax.ShapeDtypeStruct((3, BANDS, BANDS, 128), f32),
        ),
        in_specs=[smem()] + [vmem()] * 6,
        out_specs=(vmem(),) * 3,
        compiler_params=params(),
        name="prep",
    )(
        at,
        k_points,
        lattice,
        u_k.reshape(2, KPTS, BANDS * BANDS),
        u_kq.reshape(2, NQ * KPTS, BANDS * BANDS),
        mask_k,
        mask_kq.reshape(NQ * KPTS, BANDS),
    )

    own = pl.pallas_call(
        sum_body,
        out_shape=jax.ShapeDtypeStruct((ROWS, LANES), bf16),
        in_specs=[vmem()],
        out_specs=vmem(),
        compiler_params=params(),
        name="add_up",
    )(parts)

    def shift(x, step):
        return lax.ppermute(x, "kpt", [(i, (i + 2 * step) % 16) for i in range(16)])

    def swap(x):
        return lax.ppermute(x, "kpt", [(i, i ^ 1) for i in range(16)])

    back = shift(own, 3)
    ahead = shift(own, -2)
    packed, pair = pl.pallas_call(
        pack_body,
        out_shape=(
            jax.ShapeDtypeStruct((3 * ROWS, LANES), bf16),
            jax.ShapeDtypeStruct((2 * ROWS, LANES), bf16),
        ),
        in_specs=[vmem()] * 3,
        out_specs=(vmem(), vmem()),
        compiler_params=params(),
        name="pack",
    )(own, back, ahead)
    plus = shift(packed, 1)
    minus = shift(pair, -1)
    near = [packed, plus, minus]
    far = [swap(x) for x in near]

    result = pl.pallas_call(
        couple_body,
        out_shape=jax.ShapeDtypeStruct((2, KPTS, NQ, LANES), bf16),
        in_specs=[vmem()] * 9,
        out_specs=vmem(),
        scratch_shapes=[
            pltpu.VMEM((2, 2 * PER, 128, 128), f32),
            pltpu.VMEM((3, LANES, 128), f32),
            pltpu.VMEM((3, PER * BANDS, BANDS, 128), f32),
            pltpu.VMEM((2, PER * BANDS, BANDS, 128), f32),
        ],
        compiler_params=params(),
        name="couple",
    )(*near, *far, phase, right, left)
    return result


def solution(mesh):
    placed = (
        P(None, "lat", "kpt", None),
        P("lat", None),
        P("lat"),
        P(),
        P(),
        P(),
        P("kpt", None),
        P(),
        P(None, "kpt", None, None),
        P(None, None, "kpt", None, None),
        P("kpt", None),
        P(None, "kpt", None),
    )
    return jax.shard_map(
        per_device,
        mesh=mesh,
        in_specs=placed,
        out_specs=P(None, "kpt", None, "lat"),
        check_vma=False,
    )
```

```python
import jax
import jax.numpy as jnp
from jax import lax
from jax.experimental import pallas as pl
from jax.experimental.pallas import tpu as pltpu
from jax.sharding import PartitionSpec as P

two_pi = 6.283185307179586
f32 = jnp.float32
bf16 = jnp.bfloat16

MODES = 48
BANDS = 16
CELLS = 16
LAT = 16
NQ = 2
KPTS = 64
PER = MODES // LAT
LANES = PER * BANDS * BANDS
STRIDE_S = 2 * MODES + 1
ROWS = NQ * 2 * CELLS
STRIDE_O = ROWS + 1
CHUNKS = 4
CHUNK = MODES * BANDS * BANDS // CHUNKS


def rotate_body(
    qp_hbm, rv_hbm, rw_hbm, rot_hbm, coarse_hbm, out_ref,
    qp_ref, rv_ref, rw_ref, rot_ref, coarse_ref, mat_ref, s_ref, o_ref, sems,
):
    small = [
        pltpu.make_async_copy(src, dst, sems.at[i])
        for i, (src, dst) in enumerate(
            [(qp_hbm, qp_ref), (rv_hbm, rv_ref), (rw_hbm, rw_ref), (rot_hbm, rot_ref)]
        )
    ]
    large = []
    for part in range(2):
        for i in range(CHUNKS):
            lanes = pl.ds(i * CHUNK, CHUNK)
            large.append(
                pltpu.make_async_copy(
                    coarse_hbm.at[part, 0, :, lanes],
                    coarse_ref.at[part, :, lanes],
                    sems.at[4 + part * CHUNKS + i],
                )
            )
    for copy in small + large:
        copy.start()
    for copy in small:
        copy.wait()
    weight = 1.0 / jnp.full((8, 128), rw_ref[0, 0], jnp.int32).astype(f32)
    for q in range(NQ):
        arg = two_pi * (
            qp_ref[q, 0] * rv_ref[0, 0].astype(f32)
            + qp_ref[q, 1] * rv_ref[0, 1].astype(f32)
            + qp_ref[q, 2] * rv_ref[0, 2].astype(f32)
        )
        angle = jnp.full((8, 128), arg, f32)
        pr = (jnp.cos(angle) * weight).astype(bf16).astype(f32)[0:1, 0:1]
        pi = (jnp.sin(angle) * weight).astype(bf16).astype(f32)[0:1, 0:1]
        rr = rot_ref[0, q].astype(f32)
        ri = rot_ref[1, q].astype(f32)
        cr = rr * pr - ri * pi
        ci = rr * pi + ri * pr
        top = jnp.concatenate([cr, -ci], axis=0)
        low = jnp.concatenate([ci, cr], axis=0)
        mat_ref[q * 96:q * 96 + 48, 0:96] = top.T
        mat_ref[q * 96 + 48:q * 96 + 96, 0:96] = low.T
    rows = []
    for g in range(2 * NQ):
        for j in range(PER):
            rows.append(mat_ref[pl.ds(g * 48 + j, LAT, stride=PER), :])
    mat = jnp.concatenate(rows, axis=0)[:, 0:96].astype(bf16)
    for part in range(2):
        for m in range(MODES):
            if m * 256 % CHUNK == 0:
                large[part * CHUNKS + m * 256 // CHUNK].wait()
            for h in range(2):
                at = (2 * m + h) * 128
                tile = coarse_ref[part, :, at:at + 128].astype(f32)
                s_ref[h, pl.ds(part * MODES + m, CELLS, stride=STRIDE_S), :] = tile
    for e in range(CELLS):
        block = jnp.concatenate(
            [s_ref[h, e * STRIDE_S:e * STRIDE_S + 96, :].astype(bf16) for h in range(2)], axis=1
        )
        both = jnp.dot(mat, block, preferred_element_type=f32)
        for h in range(2):
            res = both[:, h * 128:(h + 1) * 128]
            for g in range(2 * NQ):
                for j in range(PER):
                    at = (g * PER + j) * LAT
                    o_ref[2 * j + h, pl.ds(g * CELLS + e, LAT, stride=STRIDE_O), :] = res[at:at + LAT]
    for l in range(LAT):
        for t in range(2 * PER):
            out_ref[l, :, t * 128:(t + 1) * 128] = o_ref[t, l * STRIDE_O:l * STRIDE_O + ROWS, :].astype(bf16)


def sum_body(x_ref, out_ref):
    for r in range(0, ROWS, 16):
        acc = x_ref[0, r:r + 16, :].astype(f32)
        for p in range(1, LAT):
            acc = acc + x_ref[p, r:r + 16, :].astype(f32)
        out_ref[r:r + 16, :] = acc.astype(bf16)


def prep_body(at_ref, kp_ref, rv_ref, u_ref, uq_ref, mk_ref, mq_ref, ph_ref, uo_ref, lo_ref):
    z = at_ref[0]
    c = at_ref[1]
    lane = lax.broadcasted_iota(jnp.int32, (256, 512), 1)
    src = lax.broadcasted_iota(jnp.int32, (256, 512), 0)
    block = lane >> 5
    home = (((z - block) & 7) << 1) + (c ^ (block >> 3))
    cell = (home << 4) + (lane & 15)
    pick = jnp.where(src == cell, 1.0, 0.0).astype(bf16)
    vec = jnp.dot(rv_ref[...].astype(f32).astype(bf16), pick, preferred_element_type=f32)
    kp = kp_ref[...]
    arg = two_pi * (
        kp[:, 0:1] * vec[0:1, :] + kp[:, 1:2] * vec[1:2, :] + kp[:, 2:3] * vec[2:3, :]
    )
    inverse = 1.0 / vec[3:4, :]
    co = jnp.cos(arg) * inverse
    si = jnp.sin(arg) * inverse
    first = (lax.broadcasted_iota(jnp.int32, (KPTS, 512), 1) & 16) == 0
    ph_ref[0:KPTS, :] = jnp.where(first, co, -si).astype(bf16)
    ph_ref[KPTS:2 * KPTS, :] = jnp.where(first, si, co).astype(bf16)
    row = lax.broadcasted_iota(jnp.int32, (KPTS, 128), 0)
    col = lax.broadcasted_iota(jnp.int32, (KPTS, 128), 1)
    spread = jnp.where((col >> 1) == row, 1.0, 0.0).astype(bf16)
    row2 = lax.broadcasted_iota(jnp.int32, (128, 128), 0)
    col2 = lax.broadcasted_iota(jnp.int32, (128, 128), 1)
    place = jnp.where((((col2 & 1) << 6) + (col2 >> 1)) == row2, 1.0, 0.0).astype(bf16)
    dims = (((0,), (0,)), ((), ()))
    mk = lax.dot_general(mk_ref[...].astype(f32).astype(bf16), spread, dims, preferred_element_type=f32)
    mq = lax.dot_general(mq_ref[...].astype(f32).astype(bf16), place, dims, preferred_element_type=f32)
    ur, ui = (
        lax.dot_general(u_ref[part], spread, dims, preferred_element_type=f32) for part in range(2)
    )
    lr, li = (
        lax.dot_general(uq_ref[part], place, dims, preferred_element_type=f32) for part in range(2)
    )
    for i, (u, left) in enumerate(((ur, lr), (ui - ur, -(li + lr)), (ur + ui, lr - li))):
        for b in range(BANDS):
            uo_ref[i, b] = u[b * 16:(b + 1) * 16] * mk
            lo_ref[i, b] = left[b * 16:(b + 1) * 16] * mq


def pack_body(own_ref, back_ref, ahead_ref, prev_ref, next_ref, all_ref, two_ref):
    for i, ref in enumerate((own_ref, back_ref, ahead_ref, prev_ref, next_ref)):
        value = ref[...]
        all_ref[i * ROWS:(i + 1) * ROWS, :] = value
        if i in (1, 2):
            two_ref[(i - 1) * ROWS:i * ROWS, :] = value


PLACE = ((0, 0), (0, 3), (1, 0), (0, 1), (2, 0), (1, 1), (0, 2), (0, 4))


def couple_body(*refs):
    ph_ref, u_ref, l_ref, out_ref, y_ref, bl_ref, h_ref, r_ref = refs[6:]
    ph = ph_ref[...]
    for q in range(NQ):
        x = jnp.concatenate(
            [
                refs[side * 3 + i][j * ROWS + q * 32:j * ROWS + (q + 1) * 32, :]
                for side in range(2)
                for i, j in PLACE
            ],
            axis=0,
        )
        t = jnp.dot(ph, x, preferred_element_type=f32)
        for part in range(2):
            for v in range(2 * PER):
                y_ref[part, v, pl.ds(q, KPTS, stride=2), :] = t[
                    part * KPTS:(part + 1) * KPTS, v * 128:(v + 1) * 128
                ]
    for v in range(2 * PER):
        rows = slice(v * 128, (v + 1) * 128)
        xr, xi = (y_ref[part, v].T.astype(bf16).astype(f32) for part in range(2))
        bl_ref[0, rows, :] = xr + xi
        bl_ref[1, rows, :] = xr
        bl_ref[2, rows, :] = xi

    group = 4

    def first(i, _):
        base = i * group * BANDS
        acc = [[jnp.zeros((16, 128), f32) for _ in range(3)] for _ in range(group)]
        for b in range(BANDS):
            us = [u_ref[t, b] for t in range(3)]
            for s in range(group):
                for t in range(3):
                    acc[s][t] = acc[s][t] + bl_ref[t, pl.ds(base + s * BANDS + b, 1), :] * us[t]
        for s in range(group):
            hr = (acc[s][0] - acc[s][2]).astype(bf16).astype(f32)
            hi = (acc[s][0] + acc[s][1]).astype(bf16).astype(f32)
            h_ref[0, i * group + s] = hr + hi
            h_ref[1, i * group + s] = hr
            h_ref[2, i * group + s] = hi
        return 0

    lax.fori_loop(0, PER * BANDS // group, first, 0)

    per = BANDS // group

    def second(i, _):
        n = i // per
        c0 = (i - n * per) * group
        acc = [[jnp.zeros((16, 128), f32) for _ in range(3)] for _ in range(group)]
        for a in range(BANDS):
            hs = [h_ref[t, n * BANDS + a] for t in range(3)]
            for s in range(group):
                for t in range(3):
                    acc[s][t] = acc[s][t] + l_ref[t, a, pl.ds(c0 + s, 1), :] * hs[t]
        for s in range(group):
            r_ref[0, i * group + s] = acc[s][0] - acc[s][2]
            r_ref[1, i * group + s] = acc[s][0] + acc[s][1]
        return 0

    lax.fori_loop(0, PER * per, second, 0)
    for part in range(2):
        for v in range(2 * PER):
            tile = r_ref[part, v * 8:(v + 1) * 8].reshape(128, 128).T
            out_ref[part, :, :, v * 128:(v + 1) * 128] = tile.reshape(KPTS, NQ, 128).astype(bf16)


def vmem():
    return pl.BlockSpec(memory_space=pltpu.VMEM)


def hbm():
    return pl.BlockSpec(memory_space=pltpu.HBM)


def smem():
    return pl.BlockSpec(memory_space=pltpu.SMEM)


def params():
    return pltpu.CompilerParams(vmem_limit_bytes=40 << 20)


def per_device(
    coarse,
    rp_vectors,
    rp_weights,
    re_vectors,
    re_weights,
    q_points,
    k_points,
    modes_rot,
    u_k,
    u_kq,
    mask_k,
    mask_kq,
):
    rotated = pl.pallas_call(
        rotate_body,
        out_shape=jax.ShapeDtypeStruct((LAT, ROWS, LANES), bf16),
        in_specs=[hbm()] * 5,
        out_specs=vmem(),
        scratch_shapes=[
            pltpu.SMEM((NQ, 3), f32),
            pltpu.SMEM((1, 3), jnp.int32),
            pltpu.SMEM((1, 1), jnp.int32),
            pltpu.VMEM((2, NQ, MODES, MODES), bf16),
            pltpu.VMEM((2, CELLS, MODES * BANDS * BANDS), bf16),
            pltpu.VMEM((192, 128), f32),
            pltpu.VMEM((2, CELLS * STRIDE_S, 128), f32),
            pltpu.VMEM((2 * PER, LAT * STRIDE_O, 128), f32),
            pltpu.SemaphoreType.DMA((4 + 2 * CHUNKS,)),
        ],
        compiler_params=pltpu.CompilerParams(vmem_limit_bytes=40 << 20),
        name="rotate",
    )(
        pltpu.with_memory_space_constraint(q_points, pltpu.HBM),
        pltpu.with_memory_space_constraint(rp_vectors, pltpu.HBM),
        rp_weights[None, :],
        pltpu.with_memory_space_constraint(modes_rot, pltpu.HBM),
        pltpu.with_memory_space_constraint(coarse, pltpu.HBM),
    )
    parts = lax.all_to_all(rotated, "lat", 0, 0, tiled=True)

    index = lax.axis_index("kpt")
    at = jnp.stack([index // 2, index % 2]).astype(jnp.int32)
    lattice = jnp.concatenate(
        [re_vectors.T, re_weights[None, :], jnp.zeros((4, re_weights.shape[0]), jnp.int32)], axis=0
    )
    phase, right, left = pl.pallas_call(
        prep_body,
        out_shape=(
            jax.ShapeDtypeStruct((2 * KPTS, 512), bf16),
            jax.ShapeDtypeStruct((3, BANDS, BANDS, 128), f32),
            jax.ShapeDtypeStruct((3, BANDS, BANDS, 128), f32),
        ),
        in_specs=[smem()] + [vmem()] * 6,
        out_specs=(vmem(),) * 3,
        compiler_params=params(),
        name="prep",
    )(
        at,
        k_points,
        lattice,
        u_k.reshape(2, KPTS, BANDS * BANDS),
        u_kq.reshape(2, NQ * KPTS, BANDS * BANDS),
        mask_k,
        mask_kq.reshape(NQ * KPTS, BANDS),
    )

    own = pl.pallas_call(
        sum_body,
        out_shape=jax.ShapeDtypeStruct((ROWS, LANES), bf16),
        in_specs=[vmem()],
        out_specs=vmem(),
        compiler_params=params(),
        name="add_up",
    )(parts)

    def shift(x, step):
        return lax.ppermute(x, "kpt", [(i, (i + 2 * step) % 16) for i in range(16)])

    def swap(x):
        return lax.ppermute(x, "kpt", [(i, i ^ 1) for i in range(16)])

    back = shift(own, 3)
    ahead = shift(own, -2)
    packed, pair = pl.pallas_call(
        pack_body,
        out_shape=(
            jax.ShapeDtypeStruct((5 * ROWS, LANES), bf16),
            jax.ShapeDtypeStruct((2 * ROWS, LANES), bf16),
        ),
        in_specs=[vmem()] * 5,
        out_specs=(vmem(), vmem()),
        compiler_params=params(),
        name="pack",
    )(own, back, ahead, shift(own, 1), shift(own, -1))
    near = [packed, shift(pair, -1), shift(back, 1)]
    far = [swap(x) for x in near]

    result = pl.pallas_call(
        couple_body,
        out_shape=jax.ShapeDtypeStruct((2, KPTS, NQ, LANES), bf16),
        in_specs=[vmem()] * 9,
        out_specs=vmem(),
        scratch_shapes=[
            pltpu.VMEM((2, 2 * PER, 128, 128), f32),
            pltpu.VMEM((3, LANES, 128), f32),
            pltpu.VMEM((3, PER * BANDS, BANDS, 128), f32),
            pltpu.VMEM((2, PER * BANDS, BANDS, 128), f32),
        ],
        compiler_params=params(),
        name="couple",
    )(*near, *far, phase, right, left)
    return result


def solution(mesh):
    placed = (
        P(None, "lat", "kpt", None),
        P("lat", None),
        P("lat"),
        P(),
        P(),
        P(),
        P("kpt", None),
        P(),
        P(None, "kpt", None, None),
        P(None, None, "kpt", None, None),
        P("kpt", None),
        P(None, "kpt", None),
    )
    return jax.shard_map(
        per_device,
        mesh=mesh,
        in_specs=placed,
        out_specs=P(None, "kpt", None, "lat"),
        check_vma=False,
    )
```

```python
import jax
import jax.numpy as jnp
from jax import lax
from jax.experimental import pallas as pl
from jax.experimental.pallas import tpu as pltpu
from jax.sharding import PartitionSpec as P

two_pi = 6.283185307179586
f32 = jnp.float32
bf16 = jnp.bfloat16

MODES = 48
BANDS = 16
CELLS = 16
LAT = 16
NQ = 2
KPTS = 64
PER = MODES // LAT
LANES = PER * BANDS * BANDS
STRIDE_S = 2 * MODES + 1
ROWS = NQ * 2 * CELLS
STRIDE_O = ROWS + 1
CHUNKS = 4
CHUNK = MODES * BANDS * BANDS // CHUNKS


def rotate_body(
    qp_hbm, rv_hbm, rw_hbm, rot_hbm, coarse_hbm, out_ref,
    qp_ref, rv_ref, rw_ref, rot_ref, coarse_ref, mat_ref, s_ref, o_ref, sems,
):
    small = [
        pltpu.make_async_copy(src, dst, sems.at[i])
        for i, (src, dst) in enumerate(
            [(qp_hbm, qp_ref), (rv_hbm, rv_ref), (rw_hbm, rw_ref), (rot_hbm, rot_ref)]
        )
    ]
    large = []
    for part in range(2):
        for i in range(CHUNKS):
            lanes = pl.ds(i * CHUNK, CHUNK)
            large.append(
                pltpu.make_async_copy(
                    coarse_hbm.at[part, 0, :, lanes],
                    coarse_ref.at[part, :, lanes],
                    sems.at[4 + part * CHUNKS + i],
                )
            )
    for copy in small + large:
        copy.start()
    for copy in small:
        copy.wait()
    weight = 1.0 / jnp.full((8, 128), rw_ref[0, 0], jnp.int32).astype(f32)
    for q in range(NQ):
        arg = two_pi * (
            qp_ref[q, 0] * rv_ref[0, 0].astype(f32)
            + qp_ref[q, 1] * rv_ref[0, 1].astype(f32)
            + qp_ref[q, 2] * rv_ref[0, 2].astype(f32)
        )
        angle = jnp.full((8, 128), arg, f32)
        pr = (jnp.cos(angle) * weight).astype(bf16).astype(f32)[0:1, 0:1]
        pi = (jnp.sin(angle) * weight).astype(bf16).astype(f32)[0:1, 0:1]
        rr = rot_ref[0, q].astype(f32)
        ri = rot_ref[1, q].astype(f32)
        cr = rr * pr - ri * pi
        ci = rr * pi + ri * pr
        top = jnp.concatenate([cr, -ci], axis=0)
        low = jnp.concatenate([ci, cr], axis=0)
        mat_ref[q * 96:q * 96 + 48, 0:96] = top.T
        mat_ref[q * 96 + 48:q * 96 + 96, 0:96] = low.T
    rows = []
    for g in range(2 * NQ):
        for j in range(PER):
            rows.append(mat_ref[pl.ds(g * 48 + j, LAT, stride=PER), :])
    mat = jnp.concatenate(rows, axis=0)[:, 0:96].astype(bf16)
    for part in range(2):
        for m in range(MODES):
            if m * 256 % CHUNK == 0:
                large[part * CHUNKS + m * 256 // CHUNK].wait()
            for h in range(2):
                at = (2 * m + h) * 128
                tile = coarse_ref[part, :, at:at + 128].astype(f32)
                s_ref[h, pl.ds(part * MODES + m, CELLS, stride=STRIDE_S), :] = tile
    for e in range(CELLS):
        block = jnp.concatenate(
            [s_ref[h, e * STRIDE_S:e * STRIDE_S + 96, :].astype(bf16) for h in range(2)], axis=1
        )
        both = jnp.dot(mat, block, preferred_element_type=f32)
        for h in range(2):
            res = both[:, h * 128:(h + 1) * 128]
            for g in range(2 * NQ):
                for j in range(PER):
                    at = (g * PER + j) * LAT
                    o_ref[2 * j + h, pl.ds(g * CELLS + e, LAT, stride=STRIDE_O), :] = res[at:at + LAT]
    for l in range(LAT):
        for t in range(2 * PER):
            out_ref[l, :, t * 128:(t + 1) * 128] = o_ref[t, l * STRIDE_O:l * STRIDE_O + ROWS, :].astype(bf16)


def sum_body(x_ref, out_ref):
    for r in range(0, ROWS, 16):
        acc = x_ref[0, r:r + 16, :].astype(f32)
        for p in range(1, LAT):
            acc = acc + x_ref[p, r:r + 16, :].astype(f32)
        out_ref[r:r + 16, :] = acc.astype(bf16)


def prep_body(*refs):
    ph_ref, uo_ref, lo_ref = refs[7:10]
    kp_ref, rv_ref, rw_ref, u_ref, uq_ref, mk_ref, mq_ref = refs[10:17]
    sems = refs[17]
    loads = [
        pltpu.make_async_copy(src, dst, sems.at[i])
        for i, (src, dst) in enumerate(zip(refs[:7], refs[10:17]))
    ]
    for load in loads:
        load.start()
    for load in loads:
        load.wait()
    place_k = lax.axis_index("kpt")
    z = place_k >> 1
    c = place_k & 1
    lane = lax.broadcasted_iota(jnp.int32, (256, 512), 1)
    src = lax.broadcasted_iota(jnp.int32, (256, 512), 0)
    block = lane >> 5
    home = (((z - block) & 7) << 1) + (c ^ (block >> 3))
    cell = (home << 4) + (lane & 15)
    pick = jnp.where(src == cell, 1.0, 0.0).astype(bf16)
    vec = jnp.dot(rv_ref[...].astype(f32).astype(bf16), pick, preferred_element_type=f32)
    weight = jnp.dot(rw_ref[...].astype(f32).astype(bf16), pick, preferred_element_type=f32)
    kp = kp_ref[...].T
    arg = two_pi * (
        kp[:, 0:1] * vec[0:1, :] + kp[:, 1:2] * vec[1:2, :] + kp[:, 2:3] * vec[2:3, :]
    )
    inverse = 1.0 / weight
    co = jnp.cos(arg) * inverse
    si = jnp.sin(arg) * inverse
    first = (lax.broadcasted_iota(jnp.int32, (KPTS, 512), 1) & 16) == 0
    ph_ref[0:KPTS, :] = jnp.where(first, co, -si).astype(bf16)
    ph_ref[KPTS:2 * KPTS, :] = jnp.where(first, si, co).astype(bf16)
    row = lax.broadcasted_iota(jnp.int32, (KPTS, 128), 0)
    col = lax.broadcasted_iota(jnp.int32, (KPTS, 128), 1)
    spread = jnp.where((col >> 1) == row, 1.0, 0.0).astype(bf16)
    place = [jnp.where(col == 2 * row + q, 1.0, 0.0).astype(bf16) for q in range(NQ)]

    def by_q(values):
        return sum(
            jnp.dot(values[q], place[q], preferred_element_type=f32) for q in range(NQ)
        )

    mk = jnp.dot(mk_ref[...].astype(f32).astype(bf16), spread, preferred_element_type=f32)
    mq = by_q([mq_ref[q].astype(f32).astype(bf16) for q in range(NQ)])
    ur, ui = (jnp.dot(u_ref[part], spread, preferred_element_type=f32) for part in range(2))
    lr, li = (by_q([uq_ref[part, q] for q in range(NQ)]) for part in range(2))
    for i, (u, left) in enumerate(((ur, lr), (ui - ur, -(li + lr)), (ur + ui, lr - li))):
        for b in range(BANDS):
            uo_ref[i, b] = u[b * 16:(b + 1) * 16] * mk
            lo_ref[i, b] = left[b * 16:(b + 1) * 16] * mq


def pack_body(own_ref, back_ref, ahead_ref, prev_ref, next_ref, order_ref, rest_ref, two_ref):
    for out_ref, group in ((rest_ref, (own_ref, prev_ref, next_ref)), (two_ref, (back_ref, ahead_ref))):
        for i, ref in enumerate(group):
            out_ref[i * ROWS:(i + 1) * ROWS, :] = ref[...]


PLACE = ((0, 0), (0, 1), (2, 0), (1, 0), (3, 0), (2, 1), (1, 1), (0, 2))


def couple_body(*refs):
    ph_ref, u_ref, l_ref, out_ref, y_ref, bl_ref, h_ref, r_ref = refs[8:]
    ph = ph_ref[...]
    for q in range(NQ):
        x = jnp.concatenate(
            [
                refs[side * 4 + i][j * ROWS + q * 32:j * ROWS + (q + 1) * 32, :]
                for side in range(2)
                for i, j in PLACE
            ],
            axis=0,
        )
        t = jnp.dot(ph, x, preferred_element_type=f32)
        for part in range(2):
            for v in range(2 * PER):
                y_ref[part, v, pl.ds(q, KPTS, stride=2), :] = t[
                    part * KPTS:(part + 1) * KPTS, v * 128:(v + 1) * 128
                ]
    for v in range(2 * PER):
        rows = slice(v * 128, (v + 1) * 128)
        xr, xi = (y_ref[part, v].T.astype(bf16).astype(f32) for part in range(2))
        bl_ref[0, rows, :] = xr + xi
        bl_ref[1, rows, :] = xr
        bl_ref[2, rows, :] = xi

    group = 4

    def first(i, _):
        base = i * group * BANDS
        acc = [[jnp.zeros((16, 128), f32) for _ in range(3)] for _ in range(group)]
        for b in range(BANDS):
            us = [u_ref[t, b] for t in range(3)]
            for s in range(group):
                for t in range(3):
                    acc[s][t] = acc[s][t] + bl_ref[t, pl.ds(base + s * BANDS + b, 1), :] * us[t]
        for s in range(group):
            hr = (acc[s][0] - acc[s][2]).astype(bf16).astype(f32)
            hi = (acc[s][0] + acc[s][1]).astype(bf16).astype(f32)
            h_ref[0, i * group + s] = hr + hi
            h_ref[1, i * group + s] = hr
            h_ref[2, i * group + s] = hi
        return 0

    lax.fori_loop(0, PER * BANDS // group, first, 0)

    per = BANDS // group

    def second(i, _):
        n = i // per
        c0 = (i - n * per) * group
        acc = [[jnp.zeros((16, 128), f32) for _ in range(3)] for _ in range(group)]
        for a in range(BANDS):
            hs = [h_ref[t, n * BANDS + a] for t in range(3)]
            for s in range(group):
                for t in range(3):
                    acc[s][t] = acc[s][t] + l_ref[t, a, pl.ds(c0 + s, 1), :] * hs[t]
        for s in range(group):
            r_ref[0, i * group + s] = acc[s][0] - acc[s][2]
            r_ref[1, i * group + s] = acc[s][0] + acc[s][1]
        return 0

    lax.fori_loop(0, PER * per, second, 0)
    for part in range(2):
        for v in range(2 * PER):
            tile = r_ref[part, v * 8:(v + 1) * 8].reshape(128, 128).T
            out_ref[part, :, :, v * 128:(v + 1) * 128] = tile.reshape(KPTS, NQ, 128).astype(bf16)


def vmem():
    return pl.BlockSpec(memory_space=pltpu.VMEM)


def hbm():
    return pl.BlockSpec(memory_space=pltpu.HBM)


def smem():
    return pl.BlockSpec(memory_space=pltpu.SMEM)


def params():
    return pltpu.CompilerParams(vmem_limit_bytes=40 << 20)


def per_device(
    coarse,
    rp_vectors,
    rp_weights,
    re_vectors,
    re_weights,
    q_points,
    k_points,
    modes_rot,
    u_k,
    u_kq,
    mask_k,
    mask_kq,
):
    rotated = pl.pallas_call(
        rotate_body,
        out_shape=jax.ShapeDtypeStruct((LAT, ROWS, LANES), bf16),
        in_specs=[hbm()] * 5,
        out_specs=vmem(),
        scratch_shapes=[
            pltpu.SMEM((NQ, 3), f32),
            pltpu.SMEM((1, 3), jnp.int32),
            pltpu.SMEM((1, 1), jnp.int32),
            pltpu.VMEM((2, NQ, MODES, MODES), bf16),
            pltpu.VMEM((2, CELLS, MODES * BANDS * BANDS), bf16),
            pltpu.VMEM((192, 128), f32),
            pltpu.VMEM((2, CELLS * STRIDE_S, 128), f32),
            pltpu.VMEM((2 * PER, LAT * STRIDE_O, 128), f32),
            pltpu.SemaphoreType.DMA((4 + 2 * CHUNKS,)),
        ],
        compiler_params=pltpu.CompilerParams(vmem_limit_bytes=40 << 20),
        name="rotate",
    )(
        pltpu.with_memory_space_constraint(q_points, pltpu.HBM),
        pltpu.with_memory_space_constraint(rp_vectors, pltpu.HBM),
        rp_weights[None, :],
        pltpu.with_memory_space_constraint(modes_rot, pltpu.HBM),
        pltpu.with_memory_space_constraint(coarse, pltpu.HBM),
    )
    parts = lax.all_to_all(rotated, "lat", 0, 0, tiled=True)

    given = (
        k_points.T,
        re_vectors.T,
        re_weights[None, :],
        jnp.transpose(u_k, (0, 2, 3, 1)).reshape(2, BANDS * BANDS, KPTS),
        jnp.transpose(u_kq, (0, 1, 3, 4, 2)).reshape(2, NQ, BANDS * BANDS, KPTS),
        mask_k.T,
        jnp.transpose(mask_kq, (0, 2, 1)),
    )
    phase, right, left = pl.pallas_call(
        prep_body,
        out_shape=(
            jax.ShapeDtypeStruct((2 * KPTS, 512), bf16),
            jax.ShapeDtypeStruct((3, BANDS, BANDS, 128), f32),
            jax.ShapeDtypeStruct((3, BANDS, BANDS, 128), f32),
        ),
        in_specs=[hbm()] * 7,
        out_specs=(vmem(),) * 3,
        scratch_shapes=[pltpu.VMEM(x.shape, x.dtype) for x in given]
        + [pltpu.SemaphoreType.DMA((len(given),))],
        compiler_params=params(),
        name="prep",
    )(*(pltpu.with_memory_space_constraint(x, pltpu.HBM) for x in given))

    own = pl.pallas_call(
        sum_body,
        out_shape=jax.ShapeDtypeStruct((ROWS, LANES), bf16),
        in_specs=[vmem()],
        out_specs=vmem(),
        compiler_params=params(),
        name="add_up",
    )(parts)

    def shift(x, step):
        return lax.ppermute(x, "kpt", [(i, (i + 2 * step) % 16) for i in range(16)])

    def swap(x):
        return lax.ppermute(x, "kpt", [(i, i ^ 1) for i in range(16)])

    back = shift(own, 3)
    ahead = shift(own, -2)
    rest, pair = pl.pallas_call(
        pack_body,
        out_shape=(
            jax.ShapeDtypeStruct((3 * ROWS, LANES), bf16),
            jax.ShapeDtypeStruct((2 * ROWS, LANES), bf16),
        ),
        in_specs=[vmem()] * 5 + [pl.BlockSpec(memory_space=pl.ANY)],
        out_specs=(vmem(), vmem()),
        compiler_params=params(),
        name="pack",
    )(own, back, ahead, shift(own, 1), shift(own, -1), phase)
    near = [rest, pair, shift(pair, -1), shift(back, 1)]
    far = [swap(x) for x in near]

    result = pl.pallas_call(
        couple_body,
        out_shape=jax.ShapeDtypeStruct((2, KPTS, NQ, LANES), bf16),
        in_specs=[vmem()] * 11,
        out_specs=vmem(),
        scratch_shapes=[
            pltpu.VMEM((2, 2 * PER, 128, 128), f32),
            pltpu.VMEM((3, LANES, 128), f32),
            pltpu.VMEM((3, PER * BANDS, BANDS, 128), f32),
            pltpu.VMEM((2, PER * BANDS, BANDS, 128), f32),
        ],
        compiler_params=params(),
        name="couple",
    )(*near, *far, phase, right, left)
    return result


def solution(mesh):
    placed = (
        P(None, "lat", "kpt", None),
        P("lat", None),
        P("lat"),
        P(),
        P(),
        P(),
        P("kpt", None),
        P(),
        P(None, "kpt", None, None),
        P(None, None, "kpt", None, None),
        P("kpt", None),
        P(None, "kpt", None),
    )
    return jax.shard_map(
        per_device,
        mesh=mesh,
        in_specs=placed,
        out_specs=P(None, "kpt", None, "lat"),
        check_vma=False,
    )
```

```python
import jax
import jax.numpy as jnp
from jax import lax
from jax.experimental import pallas as pl
from jax.experimental.pallas import tpu as pltpu
from jax.sharding import PartitionSpec as P

two_pi = 6.283185307179586
f32 = jnp.float32
bf16 = jnp.bfloat16

MODES = 48
BANDS = 16
CELLS = 16
LAT = 16
NQ = 2
KPTS = 64
PER = MODES // LAT
LANES = PER * BANDS * BANDS
STRIDE_S = 2 * MODES + 1
ROWS = NQ * 2 * CELLS
STRIDE_O = ROWS + 1
CHUNKS = 4
CHUNK = MODES * BANDS * BANDS // CHUNKS


def rotate_body(
    qp_hbm, rv_hbm, rw_hbm, rot_hbm, coarse_hbm, out_ref,
    qp_ref, rv_ref, rw_ref, rot_ref, coarse_ref, mat_ref, s_ref, o_ref, sems,
):
    small = [
        pltpu.make_async_copy(src, dst, sems.at[i])
        for i, (src, dst) in enumerate(
            [(qp_hbm, qp_ref), (rv_hbm, rv_ref), (rw_hbm, rw_ref), (rot_hbm, rot_ref)]
        )
    ]
    large = []
    for part in range(2):
        for i in range(CHUNKS):
            lanes = pl.ds(i * CHUNK, CHUNK)
            large.append(
                pltpu.make_async_copy(
                    coarse_hbm.at[part, 0, :, lanes],
                    coarse_ref.at[part, :, lanes],
                    sems.at[4 + part * CHUNKS + i],
                )
            )
    for copy in small + large:
        copy.start()
    for copy in small:
        copy.wait()
    weight = 1.0 / jnp.full((8, 128), rw_ref[0, 0], jnp.int32).astype(f32)
    for q in range(NQ):
        arg = two_pi * (
            qp_ref[q, 0] * rv_ref[0, 0].astype(f32)
            + qp_ref[q, 1] * rv_ref[0, 1].astype(f32)
            + qp_ref[q, 2] * rv_ref[0, 2].astype(f32)
        )
        angle = jnp.full((8, 128), arg, f32)
        pr = (jnp.cos(angle) * weight).astype(bf16).astype(f32)[0:1, 0:1]
        pi = (jnp.sin(angle) * weight).astype(bf16).astype(f32)[0:1, 0:1]
        rr = rot_ref[0, q].astype(f32)
        ri = rot_ref[1, q].astype(f32)
        cr = rr * pr - ri * pi
        ci = rr * pi + ri * pr
        top = jnp.concatenate([cr, -ci], axis=0)
        low = jnp.concatenate([ci, cr], axis=0)
        mat_ref[q * 96:q * 96 + 48, 0:96] = top.T
        mat_ref[q * 96 + 48:q * 96 + 96, 0:96] = low.T
    rows = []
    for g in range(2 * NQ):
        for j in range(PER):
            rows.append(mat_ref[pl.ds(g * 48 + j, LAT, stride=PER), :])
    mat = jnp.concatenate(rows, axis=0)[:, 0:96].astype(bf16)
    for part in range(2):
        for m in range(MODES):
            if m * 256 % CHUNK == 0:
                large[part * CHUNKS + m * 256 // CHUNK].wait()
            for h in range(2):
                at = (2 * m + h) * 128
                tile = coarse_ref[part, :, at:at + 128].astype(f32)
                s_ref[h, pl.ds(part * MODES + m, CELLS, stride=STRIDE_S), :] = tile
    for e in range(CELLS):
        block = jnp.concatenate(
            [s_ref[h, e * STRIDE_S:e * STRIDE_S + 96, :].astype(bf16) for h in range(2)], axis=1
        )
        both = jnp.dot(mat, block, preferred_element_type=f32)
        for h in range(2):
            res = both[:, h * 128:(h + 1) * 128]
            for g in range(2 * NQ):
                for j in range(PER):
                    at = (g * PER + j) * LAT
                    o_ref[2 * j + h, pl.ds(g * CELLS + e, LAT, stride=STRIDE_O), :] = res[at:at + LAT]
    for l in range(LAT):
        for t in range(2 * PER):
            out_ref[l, :, t * 128:(t + 1) * 128] = o_ref[t, l * STRIDE_O:l * STRIDE_O + ROWS, :].astype(bf16)


def sum_body(x_ref, out_ref):
    for r in range(0, ROWS, 16):
        acc = x_ref[0, r:r + 16, :].astype(f32)
        for p in range(1, LAT):
            acc = acc + x_ref[p, r:r + 16, :].astype(f32)
        out_ref[r:r + 16, :] = acc.astype(bf16)


def prep_body(*refs):
    ph_ref, uo_ref, lo_ref = refs[7:10]
    kp_ref, rv_ref, rw_ref, u_ref, uq_ref, mk_ref, mq_ref = refs[10:17]
    sems = refs[17]
    loads = [
        pltpu.make_async_copy(src, dst, sems.at[i])
        for i, (src, dst) in enumerate(zip(refs[:7], refs[10:17]))
    ]
    for load in loads:
        load.start()
    for load in loads:
        load.wait()
    place_k = lax.axis_index("kpt")
    z = place_k >> 1
    c = place_k & 1
    lane = lax.broadcasted_iota(jnp.int32, (256, 512), 1)
    src = lax.broadcasted_iota(jnp.int32, (256, 512), 0)
    block = lane >> 5
    home = (((z - block) & 7) << 1) + (c ^ (block >> 3))
    cell = (home << 4) + (lane & 15)
    pick = jnp.where(src == cell, 1.0, 0.0).astype(bf16)
    vec = jnp.dot(rv_ref[...].astype(f32).astype(bf16), pick, preferred_element_type=f32)
    weight = jnp.dot(rw_ref[...].astype(f32).astype(bf16), pick, preferred_element_type=f32)
    kp = kp_ref[...].T
    arg = two_pi * (
        kp[:, 0:1] * vec[0:1, :] + kp[:, 1:2] * vec[1:2, :] + kp[:, 2:3] * vec[2:3, :]
    )
    inverse = 1.0 / weight
    co = jnp.cos(arg) * inverse
    si = jnp.sin(arg) * inverse
    first = (lax.broadcasted_iota(jnp.int32, (KPTS, 512), 1) & 16) == 0
    ph_ref[0:KPTS, :] = jnp.where(first, co, -si).astype(bf16)
    ph_ref[KPTS:2 * KPTS, :] = jnp.where(first, si, co).astype(bf16)
    row = lax.broadcasted_iota(jnp.int32, (KPTS, 128), 0)
    col = lax.broadcasted_iota(jnp.int32, (KPTS, 128), 1)
    spread = jnp.where((col >> 1) == row, 1.0, 0.0).astype(bf16)
    place = [jnp.where(col == 2 * row + q, 1.0, 0.0).astype(bf16) for q in range(NQ)]

    def by_q(values):
        return sum(
            jnp.dot(values[q], place[q], preferred_element_type=f32) for q in range(NQ)
        )

    mk = jnp.dot(mk_ref[...].astype(f32).astype(bf16), spread, preferred_element_type=f32)
    mq = by_q([mq_ref[q].astype(f32).astype(bf16) for q in range(NQ)])
    ur, ui = (jnp.dot(u_ref[part], spread, preferred_element_type=f32) for part in range(2))
    lr, li = (by_q([uq_ref[part, q] for q in range(NQ)]) for part in range(2))
    for i, (u, left) in enumerate(((ur, lr), (ui - ur, -(li + lr)), (ur + ui, lr - li))):
        for b in range(BANDS):
            uo_ref[i, b] = u[b * 16:(b + 1) * 16] * mk
            lo_ref[i, b] = left[b * 16:(b + 1) * 16] * mq


def pack_body(own_ref, back_ref, ahead_ref, order_ref, three_ref, two_ref):
    for i, ref in enumerate((own_ref, back_ref, ahead_ref)):
        value = ref[...]
        three_ref[i * ROWS:(i + 1) * ROWS, :] = value
        if i > 0:
            two_ref[(i - 1) * ROWS:i * ROWS, :] = value


PLACE = ((0, 0), (1, 0), (2, 0), (0, 1), (1, 1), (2, 1), (0, 2), (1, 2))


def couple_body(*refs):
    ph_ref, u_ref, l_ref, out_ref, y_ref, bl_ref, h_ref, r_ref = refs[6:]
    ph = ph_ref[...]
    for q in range(NQ):
        x = jnp.concatenate(
            [
                refs[side * 3 + i][j * ROWS + q * 32:j * ROWS + (q + 1) * 32, :]
                for side in range(2)
                for i, j in PLACE
            ],
            axis=0,
        )
        t = jnp.dot(ph, x, preferred_element_type=f32)
        for part in range(2):
            for v in range(2 * PER):
                y_ref[part, v, pl.ds(q, KPTS, stride=2), :] = t[
                    part * KPTS:(part + 1) * KPTS, v * 128:(v + 1) * 128
                ]
    for v in range(2 * PER):
        rows = slice(v * 128, (v + 1) * 128)
        xr, xi = (y_ref[part, v].T.astype(bf16).astype(f32) for part in range(2))
        bl_ref[0, rows, :] = xr + xi
        bl_ref[1, rows, :] = xr
        bl_ref[2, rows, :] = xi

    group = 4

    def first(i, _):
        base = i * group * BANDS
        acc = [[jnp.zeros((16, 128), f32) for _ in range(3)] for _ in range(group)]
        for b in range(BANDS):
            us = [u_ref[t, b] for t in range(3)]
            for s in range(group):
                for t in range(3):
                    acc[s][t] = acc[s][t] + bl_ref[t, pl.ds(base + s * BANDS + b, 1), :] * us[t]
        for s in range(group):
            hr = (acc[s][0] - acc[s][2]).astype(bf16).astype(f32)
            hi = (acc[s][0] + acc[s][1]).astype(bf16).astype(f32)
            h_ref[0, i * group + s] = hr + hi
            h_ref[1, i * group + s] = hr
            h_ref[2, i * group + s] = hi
        return 0

    lax.fori_loop(0, PER * BANDS // group, first, 0)

    per = BANDS // group

    def second(i, _):
        n = i // per
        c0 = (i - n * per) * group
        acc = [[jnp.zeros((16, 128), f32) for _ in range(3)] for _ in range(group)]
        for a in range(BANDS):
            hs = [h_ref[t, n * BANDS + a] for t in range(3)]
            for s in range(group):
                for t in range(3):
                    acc[s][t] = acc[s][t] + l_ref[t, a, pl.ds(c0 + s, 1), :] * hs[t]
        for s in range(group):
            r_ref[0, i * group + s] = acc[s][0] - acc[s][2]
            r_ref[1, i * group + s] = acc[s][0] + acc[s][1]
        return 0

    lax.fori_loop(0, PER * per, second, 0)
    for part in range(2):
        for v in range(2 * PER):
            tile = r_ref[part, v * 8:(v + 1) * 8].reshape(128, 128).T
            out_ref[part, :, :, v * 128:(v + 1) * 128] = tile.reshape(KPTS, NQ, 128).astype(bf16)


def vmem():
    return pl.BlockSpec(memory_space=pltpu.VMEM)


def hbm():
    return pl.BlockSpec(memory_space=pltpu.HBM)


def smem():
    return pl.BlockSpec(memory_space=pltpu.SMEM)


def params():
    return pltpu.CompilerParams(vmem_limit_bytes=40 << 20)


def per_device(
    coarse,
    rp_vectors,
    rp_weights,
    re_vectors,
    re_weights,
    q_points,
    k_points,
    modes_rot,
    u_k,
    u_kq,
    mask_k,
    mask_kq,
):
    rotated = pl.pallas_call(
        rotate_body,
        out_shape=jax.ShapeDtypeStruct((LAT, ROWS, LANES), bf16),
        in_specs=[hbm()] * 5,
        out_specs=vmem(),
        scratch_shapes=[
            pltpu.SMEM((NQ, 3), f32),
            pltpu.SMEM((1, 3), jnp.int32),
            pltpu.SMEM((1, 1), jnp.int32),
            pltpu.VMEM((2, NQ, MODES, MODES), bf16),
            pltpu.VMEM((2, CELLS, MODES * BANDS * BANDS), bf16),
            pltpu.VMEM((192, 128), f32),
            pltpu.VMEM((2, CELLS * STRIDE_S, 128), f32),
            pltpu.VMEM((2 * PER, LAT * STRIDE_O, 128), f32),
            pltpu.SemaphoreType.DMA((4 + 2 * CHUNKS,)),
        ],
        compiler_params=pltpu.CompilerParams(vmem_limit_bytes=40 << 20),
        name="rotate",
    )(
        pltpu.with_memory_space_constraint(q_points, pltpu.HBM),
        pltpu.with_memory_space_constraint(rp_vectors, pltpu.HBM),
        rp_weights[None, :],
        pltpu.with_memory_space_constraint(modes_rot, pltpu.HBM),
        pltpu.with_memory_space_constraint(coarse, pltpu.HBM),
    )
    parts = lax.all_to_all(rotated, "lat", 0, 0, tiled=True)

    given = (
        k_points.T,
        re_vectors.T,
        re_weights[None, :],
        jnp.transpose(u_k, (0, 2, 3, 1)).reshape(2, BANDS * BANDS, KPTS),
        jnp.transpose(u_kq, (0, 1, 3, 4, 2)).reshape(2, NQ, BANDS * BANDS, KPTS),
        mask_k.T,
        jnp.transpose(mask_kq, (0, 2, 1)),
    )
    phase, right, left = pl.pallas_call(
        prep_body,
        out_shape=(
            jax.ShapeDtypeStruct((2 * KPTS, 512), bf16),
            jax.ShapeDtypeStruct((3, BANDS, BANDS, 128), f32),
            jax.ShapeDtypeStruct((3, BANDS, BANDS, 128), f32),
        ),
        in_specs=[hbm()] * 7,
        out_specs=(vmem(),) * 3,
        scratch_shapes=[pltpu.VMEM(x.shape, x.dtype) for x in given]
        + [pltpu.SemaphoreType.DMA((len(given),))],
        compiler_params=params(),
        name="prep",
    )(*(pltpu.with_memory_space_constraint(x, pltpu.HBM) for x in given))

    own = pl.pallas_call(
        sum_body,
        out_shape=jax.ShapeDtypeStruct((ROWS, LANES), bf16),
        in_specs=[vmem()],
        out_specs=vmem(),
        compiler_params=params(),
        name="add_up",
    )(parts)

    def shift(x, step):
        return lax.ppermute(x, "kpt", [(i, (i + 2 * step) % 16) for i in range(16)])

    def swap(x):
        return lax.ppermute(x, "kpt", [(i, i ^ 1) for i in range(16)])

    back = shift(own, 3)
    ahead = shift(own, -2)
    packed, pair = pl.pallas_call(
        pack_body,
        out_shape=(
            jax.ShapeDtypeStruct((3 * ROWS, LANES), bf16),
            jax.ShapeDtypeStruct((2 * ROWS, LANES), bf16),
        ),
        in_specs=[vmem()] * 3 + [pl.BlockSpec(memory_space=pl.ANY)],
        out_specs=(vmem(), vmem()),
        compiler_params=params(),
        name="pack",
    )(own, back, ahead, phase)
    plus = shift(packed, 1)
    minus = shift(pair, -1)
    near = [packed, plus, minus]
    far = [swap(x) for x in near]

    result = pl.pallas_call(
        couple_body,
        out_shape=jax.ShapeDtypeStruct((2, KPTS, NQ, LANES), bf16),
        in_specs=[vmem()] * 9,
        out_specs=vmem(),
        scratch_shapes=[
            pltpu.VMEM((2, 2 * PER, 128, 128), f32),
            pltpu.VMEM((3, LANES, 128), f32),
            pltpu.VMEM((3, PER * BANDS, BANDS, 128), f32),
            pltpu.VMEM((2, PER * BANDS, BANDS, 128), f32),
        ],
        compiler_params=params(),
        name="couple",
    )(*near, *far, phase, right, left)
    return result


def solution(mesh):
    placed = (
        P(None, "lat", "kpt", None),
        P("lat", None),
        P("lat"),
        P(),
        P(),
        P(),
        P("kpt", None),
        P(),
        P(None, "kpt", None, None),
        P(None, None, "kpt", None, None),
        P("kpt", None),
        P(None, "kpt", None),
    )
    return jax.shard_map(
        per_device,
        mesh=mesh,
        in_specs=placed,
        out_specs=P(None, "kpt", None, "lat"),
        check_vma=False,
    )
```

```python
import jax
import jax.numpy as jnp
from jax import lax
from jax.experimental import pallas as pl
from jax.experimental.pallas import tpu as pltpu
from jax.sharding import PartitionSpec as P

two_pi = 6.283185307179586
f32 = jnp.float32
bf16 = jnp.bfloat16

MODES = 48
BANDS = 16
CELLS = 16
LAT = 16
NQ = 2
KPTS = 64
PER = MODES // LAT
LANES = PER * BANDS * BANDS
STRIDE_S = 2 * MODES + 1
ROWS = NQ * 2 * CELLS
STRIDE_O = ROWS + 1
CHUNKS = 4
CHUNK = MODES * BANDS * BANDS // CHUNKS


def rotate_body(
    qp_hbm, rv_hbm, rw_hbm, rot_hbm, coarse_hbm, out_ref,
    qp_ref, rv_ref, rw_ref, rot_ref, coarse_ref, mat_ref, s_ref, o_ref, sems,
):
    small = [
        pltpu.make_async_copy(src, dst, sems.at[i])
        for i, (src, dst) in enumerate(
            [(qp_hbm, qp_ref), (rv_hbm, rv_ref), (rw_hbm, rw_ref), (rot_hbm, rot_ref)]
        )
    ]
    large = []
    for part in range(2):
        for i in range(CHUNKS):
            lanes = pl.ds(i * CHUNK, CHUNK)
            large.append(
                pltpu.make_async_copy(
                    coarse_hbm.at[part, 0, :, lanes],
                    coarse_ref.at[part, :, lanes],
                    sems.at[4 + part * CHUNKS + i],
                )
            )
    for copy in small + large:
        copy.start()
    for copy in small:
        copy.wait()
    weight = 1.0 / jnp.full((8, 128), rw_ref[0, 0], jnp.int32).astype(f32)
    for q in range(NQ):
        arg = two_pi * (
            qp_ref[q, 0] * rv_ref[0, 0].astype(f32)
            + qp_ref[q, 1] * rv_ref[0, 1].astype(f32)
            + qp_ref[q, 2] * rv_ref[0, 2].astype(f32)
        )
        angle = jnp.full((8, 128), arg, f32)
        pr = (jnp.cos(angle) * weight).astype(bf16).astype(f32)[0:1, 0:1]
        pi = (jnp.sin(angle) * weight).astype(bf16).astype(f32)[0:1, 0:1]
        rr = rot_ref[0, q].astype(f32)
        ri = rot_ref[1, q].astype(f32)
        cr = rr * pr - ri * pi
        ci = rr * pi + ri * pr
        top = jnp.concatenate([cr, -ci], axis=0)
        low = jnp.concatenate([ci, cr], axis=0)
        mat_ref[q * 96:q * 96 + 48, 0:96] = top.T
        mat_ref[q * 96 + 48:q * 96 + 96, 0:96] = low.T
    rows = []
    for g in range(2 * NQ):
        for j in range(PER):
            rows.append(mat_ref[pl.ds(g * 48 + j, LAT, stride=PER), :])
    mat = jnp.concatenate(rows, axis=0)[:, 0:96].astype(bf16)
    for part in range(2):
        for m in range(MODES):
            if m * 256 % CHUNK == 0:
                large[part * CHUNKS + m * 256 // CHUNK].wait()
            for h in range(2):
                at = (2 * m + h) * 128
                tile = coarse_ref[part, :, at:at + 128].astype(f32)
                s_ref[h, pl.ds(part * MODES + m, CELLS, stride=STRIDE_S), :] = tile
    for e in range(CELLS):
        block = jnp.concatenate(
            [s_ref[h, e * STRIDE_S:e * STRIDE_S + 96, :].astype(bf16) for h in range(2)], axis=1
        )
        both = jnp.dot(mat, block, preferred_element_type=f32)
        for h in range(2):
            res = both[:, h * 128:(h + 1) * 128]
            for g in range(2 * NQ):
                for j in range(PER):
                    at = (g * PER + j) * LAT
                    o_ref[2 * j + h, pl.ds(g * CELLS + e, LAT, stride=STRIDE_O), :] = res[at:at + LAT]
    for l in range(LAT):
        for t in range(2 * PER):
            out_ref[l, :, t * 128:(t + 1) * 128] = o_ref[t, l * STRIDE_O:l * STRIDE_O + ROWS, :].astype(bf16)


def sum_body(x_ref, out_ref):
    for r in range(0, ROWS, 16):
        acc = x_ref[0, r:r + 16, :].astype(f32)
        for p in range(1, LAT):
            acc = acc + x_ref[p, r:r + 16, :].astype(f32)
        out_ref[r:r + 16, :] = acc.astype(bf16)


def prep_body(*refs):
    ph_ref, uo_ref, lo_ref = refs[7:10]
    kp_ref, rv_ref, rw_ref, u_ref, uq_ref, mk_ref, mq_ref = refs[10:17]
    sems = refs[17]
    loads = [
        pltpu.make_async_copy(src, dst, sems.at[i])
        for i, (src, dst) in enumerate(zip(refs[:7], refs[10:17]))
    ]
    for load in loads:
        load.start()
    for load in loads:
        load.wait()
    place_k = lax.axis_index("kpt")
    z = place_k >> 1
    c = place_k & 1
    lane = lax.broadcasted_iota(jnp.int32, (256, 512), 1)
    src = lax.broadcasted_iota(jnp.int32, (256, 512), 0)
    block = lane >> 5
    home = (((z - block) & 7) << 1) + (c ^ (block >> 3))
    cell = (home << 4) + (lane & 15)
    pick = jnp.where(src == cell, 1.0, 0.0).astype(bf16)
    vec = jnp.dot(rv_ref[...].astype(f32).astype(bf16), pick, preferred_element_type=f32)
    weight = jnp.dot(rw_ref[...].astype(f32).astype(bf16), pick, preferred_element_type=f32)
    kp = kp_ref[...].T
    arg = two_pi * (
        kp[:, 0:1] * vec[0:1, :] + kp[:, 1:2] * vec[1:2, :] + kp[:, 2:3] * vec[2:3, :]
    )
    inverse = 1.0 / weight
    co = jnp.cos(arg) * inverse
    si = jnp.sin(arg) * inverse
    first = (lax.broadcasted_iota(jnp.int32, (KPTS, 512), 1) & 16) == 0
    ph_ref[0:KPTS, :] = jnp.where(first, co, -si).astype(bf16)
    ph_ref[KPTS:2 * KPTS, :] = jnp.where(first, si, co).astype(bf16)
    row = lax.broadcasted_iota(jnp.int32, (KPTS, 128), 0)
    col = lax.broadcasted_iota(jnp.int32, (KPTS, 128), 1)
    spread = jnp.where((col >> 1) == row, 1.0, 0.0).astype(bf16)
    place = [jnp.where(col == 2 * row + q, 1.0, 0.0).astype(bf16) for q in range(NQ)]

    def by_q(values):
        return sum(
            jnp.dot(values[q], place[q], preferred_element_type=f32) for q in range(NQ)
        )

    mk = jnp.dot(mk_ref[...].astype(f32).astype(bf16), spread, preferred_element_type=f32)
    mq = by_q([mq_ref[q].astype(f32).astype(bf16) for q in range(NQ)])
    ur, ui = (jnp.dot(u_ref[part], spread, preferred_element_type=f32) for part in range(2))
    lr, li = (by_q([uq_ref[part, q] for q in range(NQ)]) for part in range(2))
    for i, (u, left) in enumerate(((ur, lr), (ui - ur, -(li + lr)), (ur + ui, lr - li))):
        for b in range(BANDS):
            uo_ref[i, b] = u[b * 16:(b + 1) * 16] * mk
            lo_ref[i, b] = left[b * 16:(b + 1) * 16] * mq


def pack_body(own_ref, back_ref, ahead_ref, order_ref, all_ref, plus_ref, minus_ref):
    half = ROWS // 2
    own = own_ref[...]
    back = back_ref[...]
    ahead = ahead_ref[...]
    for i, value in enumerate((own, back, ahead)):
        all_ref[i * ROWS:(i + 1) * ROWS, :] = value
    plus_ref[0:ROWS, :] = own
    plus_ref[ROWS:2 * ROWS, :] = back
    plus_ref[2 * ROWS:, :] = ahead[0:half]
    minus_ref[0:ROWS, :] = back
    minus_ref[ROWS:2 * ROWS, :] = ahead
    minus_ref[2 * ROWS:, :] = own[half:]


PLACE = ((0, 0), (1, 0), (2, 0), (0, 1), (1, 1), (2, 1), (0, 2))


def couple_body(*refs):
    ph_ref, u_ref, l_ref, out_ref, y_ref, bl_ref, h_ref, r_ref = refs[6:]
    ph = ph_ref[...]
    for q in range(NQ):
        pieces = []
        for side in range(2):
            for i, j in PLACE:
                at = j * ROWS + q * 32
                pieces.append(refs[side * 3 + i][at:at + 32, :])
            pieces.append(refs[side * 3 + 1 + q][2 * ROWS:2 * ROWS + 32, :])
        x = jnp.concatenate(pieces, axis=0)
        t = jnp.dot(ph, x, preferred_element_type=f32)
        for part in range(2):
            for v in range(2 * PER):
                y_ref[part, v, pl.ds(q, KPTS, stride=2), :] = t[
                    part * KPTS:(part + 1) * KPTS, v * 128:(v + 1) * 128
                ]
    for v in range(2 * PER):
        rows = slice(v * 128, (v + 1) * 128)
        xr, xi = (y_ref[part, v].T.astype(bf16).astype(f32) for part in range(2))
        bl_ref[0, rows, :] = xr + xi
        bl_ref[1, rows, :] = xr
        bl_ref[2, rows, :] = xi

    group = 4

    def first(i, _):
        base = i * group * BANDS
        acc = [[jnp.zeros((16, 128), f32) for _ in range(3)] for _ in range(group)]
        for b in range(BANDS):
            us = [u_ref[t, b] for t in range(3)]
            for s in range(group):
                for t in range(3):
                    acc[s][t] = acc[s][t] + bl_ref[t, pl.ds(base + s * BANDS + b, 1), :] * us[t]
        for s in range(group):
            hr = (acc[s][0] - acc[s][2]).astype(bf16).astype(f32)
            hi = (acc[s][0] + acc[s][1]).astype(bf16).astype(f32)
            h_ref[0, i * group + s] = hr + hi
            h_ref[1, i * group + s] = hr
            h_ref[2, i * group + s] = hi
        return 0

    lax.fori_loop(0, PER * BANDS // group, first, 0)

    per = BANDS // group

    def second(i, _):
        n = i // per
        c0 = (i - n * per) * group
        acc = [[jnp.zeros((16, 128), f32) for _ in range(3)] for _ in range(group)]
        for a in range(BANDS):
            hs = [h_ref[t, n * BANDS + a] for t in range(3)]
            for s in range(group):
                for t in range(3):
                    acc[s][t] = acc[s][t] + l_ref[t, a, pl.ds(c0 + s, 1), :] * hs[t]
        for s in range(group):
            r_ref[0, i * group + s] = acc[s][0] - acc[s][2]
            r_ref[1, i * group + s] = acc[s][0] + acc[s][1]
        return 0

    lax.fori_loop(0, PER * per, second, 0)
    for part in range(2):
        for v in range(2 * PER):
            tile = r_ref[part, v * 8:(v + 1) * 8].reshape(128, 128).T
            out_ref[part, :, :, v * 128:(v + 1) * 128] = tile.reshape(KPTS, NQ, 128).astype(bf16)


def vmem():
    return pl.BlockSpec(memory_space=pltpu.VMEM)


def hbm():
    return pl.BlockSpec(memory_space=pltpu.HBM)


def smem():
    return pl.BlockSpec(memory_space=pltpu.SMEM)


def params():
    return pltpu.CompilerParams(vmem_limit_bytes=40 << 20)


def per_device(
    coarse,
    rp_vectors,
    rp_weights,
    re_vectors,
    re_weights,
    q_points,
    k_points,
    modes_rot,
    u_k,
    u_kq,
    mask_k,
    mask_kq,
):
    rotated = pl.pallas_call(
        rotate_body,
        out_shape=jax.ShapeDtypeStruct((LAT, ROWS, LANES), bf16),
        in_specs=[hbm()] * 5,
        out_specs=vmem(),
        scratch_shapes=[
            pltpu.SMEM((NQ, 3), f32),
            pltpu.SMEM((1, 3), jnp.int32),
            pltpu.SMEM((1, 1), jnp.int32),
            pltpu.VMEM((2, NQ, MODES, MODES), bf16),
            pltpu.VMEM((2, CELLS, MODES * BANDS * BANDS), bf16),
            pltpu.VMEM((192, 128), f32),
            pltpu.VMEM((2, CELLS * STRIDE_S, 128), f32),
            pltpu.VMEM((2 * PER, LAT * STRIDE_O, 128), f32),
            pltpu.SemaphoreType.DMA((4 + 2 * CHUNKS,)),
        ],
        compiler_params=pltpu.CompilerParams(vmem_limit_bytes=40 << 20),
        name="rotate",
    )(
        pltpu.with_memory_space_constraint(q_points, pltpu.HBM),
        pltpu.with_memory_space_constraint(rp_vectors, pltpu.HBM),
        rp_weights[None, :],
        pltpu.with_memory_space_constraint(modes_rot, pltpu.HBM),
        pltpu.with_memory_space_constraint(coarse, pltpu.HBM),
    )
    parts = lax.all_to_all(rotated, "lat", 0, 0, tiled=True)

    given = (
        k_points.T,
        re_vectors.T,
        re_weights[None, :],
        jnp.transpose(u_k, (0, 2, 3, 1)).reshape(2, BANDS * BANDS, KPTS),
        jnp.transpose(u_kq, (0, 1, 3, 4, 2)).reshape(2, NQ, BANDS * BANDS, KPTS),
        mask_k.T,
        jnp.transpose(mask_kq, (0, 2, 1)),
    )
    phase, right, left = pl.pallas_call(
        prep_body,
        out_shape=(
            jax.ShapeDtypeStruct((2 * KPTS, 512), bf16),
            jax.ShapeDtypeStruct((3, BANDS, BANDS, 128), f32),
            jax.ShapeDtypeStruct((3, BANDS, BANDS, 128), f32),
        ),
        in_specs=[hbm()] * 7,
        out_specs=(vmem(),) * 3,
        scratch_shapes=[pltpu.VMEM(x.shape, x.dtype) for x in given]
        + [pltpu.SemaphoreType.DMA((len(given),))],
        compiler_params=params(),
        name="prep",
    )(*(pltpu.with_memory_space_constraint(x, pltpu.HBM) for x in given))

    own = pl.pallas_call(
        sum_body,
        out_shape=jax.ShapeDtypeStruct((ROWS, LANES), bf16),
        in_specs=[vmem()],
        out_specs=vmem(),
        compiler_params=params(),
        name="add_up",
    )(parts)

    def shift(x, step):
        return lax.ppermute(x, "kpt", [(i, (i + 2 * step) % 16) for i in range(16)])

    def swap(x):
        return lax.ppermute(x, "kpt", [(i, i ^ 1) for i in range(16)])

    back = shift(own, 3)
    ahead = shift(own, -2)
    packed, forth, behind = pl.pallas_call(
        pack_body,
        out_shape=(
            jax.ShapeDtypeStruct((3 * ROWS, LANES), bf16),
            jax.ShapeDtypeStruct((5 * ROWS // 2, LANES), bf16),
            jax.ShapeDtypeStruct((5 * ROWS // 2, LANES), bf16),
        ),
        in_specs=[vmem()] * 3 + [pl.BlockSpec(memory_space=pl.ANY)],
        out_specs=(vmem(),) * 3,
        compiler_params=params(),
        name="pack",
    )(own, back, ahead, phase)
    near = [packed, shift(forth, 1), shift(behind, -1)]
    far = [swap(x) for x in near]

    result = pl.pallas_call(
        couple_body,
        out_shape=jax.ShapeDtypeStruct((2, KPTS, NQ, LANES), bf16),
        in_specs=[vmem()] * 9,
        out_specs=vmem(),
        scratch_shapes=[
            pltpu.VMEM((2, 2 * PER, 128, 128), f32),
            pltpu.VMEM((3, LANES, 128), f32),
            pltpu.VMEM((3, PER * BANDS, BANDS, 128), f32),
            pltpu.VMEM((2, PER * BANDS, BANDS, 128), f32),
        ],
        compiler_params=params(),
        name="couple",
    )(*near, *far, phase, right, left)
    return result


def solution(mesh):
    placed = (
        P(None, "lat", "kpt", None),
        P("lat", None),
        P("lat"),
        P(),
        P(),
        P(),
        P("kpt", None),
        P(),
        P(None, "kpt", None, None),
        P(None, None, "kpt", None, None),
        P("kpt", None),
        P(None, "kpt", None),
    )
    return jax.shard_map(
        per_device,
        mesh=mesh,
        in_specs=placed,
        out_specs=P(None, "kpt", None, "lat"),
        check_vma=False,
    )
```

```python
import jax
import jax.numpy as jnp
from jax import lax
from jax.experimental import pallas as pl
from jax.experimental.pallas import tpu as pltpu
from jax.sharding import PartitionSpec as P

two_pi = 6.283185307179586
f32 = jnp.float32
bf16 = jnp.bfloat16

MODES = 48
BANDS = 16
CELLS = 16
LAT = 16
NQ = 2
KPTS = 64
PER = MODES // LAT
LANES = PER * BANDS * BANDS
STRIDE_S = 2 * MODES + 1
ROWS = NQ * 2 * CELLS
STRIDE_O = ROWS + 1
CHUNKS = 4
CHUNK = MODES * BANDS * BANDS // CHUNKS


def rotate_body(
    qp_hbm, rv_hbm, rw_hbm, rot_hbm, coarse_hbm, out_ref,
    qp_ref, rv_ref, rw_ref, rot_ref, coarse_ref, mat_ref, s_ref, o_ref, sems,
):
    small = [
        pltpu.make_async_copy(src, dst, sems.at[i])
        for i, (src, dst) in enumerate(
            [(qp_hbm, qp_ref), (rv_hbm, rv_ref), (rw_hbm, rw_ref), (rot_hbm, rot_ref)]
        )
    ]
    large = []
    for part in range(2):
        for i in range(CHUNKS):
            lanes = pl.ds(i * CHUNK, CHUNK)
            large.append(
                pltpu.make_async_copy(
                    coarse_hbm.at[part, 0, :, lanes],
                    coarse_ref.at[part, :, lanes],
                    sems.at[4 + part * CHUNKS + i],
                )
            )
    for copy in small + large:
        copy.start()
    for copy in small:
        copy.wait()
    weight = 1.0 / jnp.full((8, 128), rw_ref[0, 0], jnp.int32).astype(f32)
    for q in range(NQ):
        arg = two_pi * (
            qp_ref[q, 0] * rv_ref[0, 0].astype(f32)
            + qp_ref[q, 1] * rv_ref[0, 1].astype(f32)
            + qp_ref[q, 2] * rv_ref[0, 2].astype(f32)
        )
        angle = jnp.full((8, 128), arg, f32)
        pr = (jnp.cos(angle) * weight).astype(bf16).astype(f32)[0:1, 0:1]
        pi = (jnp.sin(angle) * weight).astype(bf16).astype(f32)[0:1, 0:1]
        rr = rot_ref[0, q].astype(f32)
        ri = rot_ref[1, q].astype(f32)
        cr = rr * pr - ri * pi
        ci = rr * pi + ri * pr
        top = jnp.concatenate([cr, -ci], axis=0)
        low = jnp.concatenate([ci, cr], axis=0)
        mat_ref[q * 96:q * 96 + 48, 0:96] = top.T
        mat_ref[q * 96 + 48:q * 96 + 96, 0:96] = low.T
    rows = []
    for g in range(2 * NQ):
        for j in range(PER):
            rows.append(mat_ref[pl.ds(g * 48 + j, LAT, stride=PER), :])
    mat = jnp.concatenate(rows, axis=0)[:, 0:96].astype(bf16)
    for part in range(2):
        for m in range(MODES):
            if m * 256 % CHUNK == 0:
                large[part * CHUNKS + m * 256 // CHUNK].wait()
            for h in range(2):
                at = (2 * m + h) * 128
                tile = coarse_ref[part, :, at:at + 128].astype(f32)
                s_ref[h, pl.ds(part * MODES + m, CELLS, stride=STRIDE_S), :] = tile
    for e in range(CELLS):
        block = jnp.concatenate(
            [s_ref[h, e * STRIDE_S:e * STRIDE_S + 96, :].astype(bf16) for h in range(2)], axis=1
        )
        both = jnp.dot(mat, block, preferred_element_type=f32)
        for h in range(2):
            res = both[:, h * 128:(h + 1) * 128]
            for g in range(2 * NQ):
                for j in range(PER):
                    at = (g * PER + j) * LAT
                    o_ref[2 * j + h, pl.ds(g * CELLS + e, LAT, stride=STRIDE_O), :] = res[at:at + LAT]
    for l in range(LAT):
        for t in range(2 * PER):
            out_ref[l, :, t * 128:(t + 1) * 128] = o_ref[t, l * STRIDE_O:l * STRIDE_O + ROWS, :].astype(bf16)


def sum_body(x_ref, out_ref):
    for r in range(0, ROWS, 16):
        acc = x_ref[0, r:r + 16, :].astype(f32)
        for p in range(1, LAT):
            acc = acc + x_ref[p, r:r + 16, :].astype(f32)
        out_ref[r:r + 16, :] = acc.astype(bf16)


def prep_body(*refs):
    ph_ref, uo_ref, lo_ref = refs[7:10]
    kp_ref, rv_ref, rw_ref, u_ref, uq_ref, mk_ref, mq_ref = refs[10:17]
    sems = refs[17]
    loads = [
        pltpu.make_async_copy(src, dst, sems.at[i])
        for i, (src, dst) in enumerate(zip(refs[:7], refs[10:17]))
    ]
    for load in loads:
        load.start()
    for load in loads:
        load.wait()
    place_k = lax.axis_index("kpt")
    z = place_k >> 1
    c = place_k & 1
    lane = lax.broadcasted_iota(jnp.int32, (256, 512), 1)
    src = lax.broadcasted_iota(jnp.int32, (256, 512), 0)
    block = lane >> 5
    home = (((z - block) & 7) << 1) + (c ^ (block >> 3))
    cell = (home << 4) + (lane & 15)
    pick = jnp.where(src == cell, 1.0, 0.0).astype(bf16)
    vec = jnp.dot(rv_ref[...].astype(f32).astype(bf16), pick, preferred_element_type=f32)
    weight = jnp.dot(rw_ref[...].astype(f32).astype(bf16), pick, preferred_element_type=f32)
    kp = kp_ref[...].T
    arg = two_pi * (
        kp[:, 0:1] * vec[0:1, :] + kp[:, 1:2] * vec[1:2, :] + kp[:, 2:3] * vec[2:3, :]
    )
    inverse = 1.0 / weight
    co = jnp.cos(arg) * inverse
    si = jnp.sin(arg) * inverse
    first = (lax.broadcasted_iota(jnp.int32, (KPTS, 512), 1) & 16) == 0
    ph_ref[0:KPTS, :] = jnp.where(first, co, -si).astype(bf16)
    ph_ref[KPTS:2 * KPTS, :] = jnp.where(first, si, co).astype(bf16)
    row = lax.broadcasted_iota(jnp.int32, (KPTS, 128), 0)
    col = lax.broadcasted_iota(jnp.int32, (KPTS, 128), 1)
    spread = jnp.where((col >> 1) == row, 1.0, 0.0).astype(bf16)
    place = [jnp.where(col == 2 * row + q, 1.0, 0.0).astype(bf16) for q in range(NQ)]

    def by_q(values):
        return sum(
            jnp.dot(values[q], place[q], preferred_element_type=f32) for q in range(NQ)
        )

    mk = jnp.dot(mk_ref[...].astype(f32).astype(bf16), spread, preferred_element_type=f32)
    mq = by_q([mq_ref[q].astype(f32).astype(bf16) for q in range(NQ)])
    ur, ui = (jnp.dot(u_ref[part], spread, preferred_element_type=f32) for part in range(2))
    lr, li = (by_q([uq_ref[part, q] for q in range(NQ)]) for part in range(2))
    for i, (u, left) in enumerate(((ur, lr), (ui - ur, -(li + lr)), (ur + ui, lr - li))):
        for b in range(BANDS):
            uo_ref[i, b] = u[b * 16:(b + 1) * 16] * mk
            lo_ref[i, b] = left[b * 16:(b + 1) * 16] * mq


def pack_body(own_ref, back_ref, ahead_ref, order_ref, three_ref, two_ref):
    for i, ref in enumerate((own_ref, back_ref, ahead_ref)):
        value = ref[...]
        three_ref[i * ROWS:(i + 1) * ROWS, :] = value
        if i > 0:
            two_ref[(i - 1) * ROWS:i * ROWS, :] = value


PLACE = ((0, 0), (1, 0), (2, 0), (0, 1), (1, 1), (2, 1), (0, 2), (1, 2))


def couple_body(*refs):
    ph_ref, u_ref, l_ref, out_ref, y_ref, bl_ref, h_ref, r_ref = refs[6:]
    ph = ph_ref[...]
    for q in range(NQ):
        x = jnp.concatenate(
            [
                refs[side * 3 + i][j * ROWS + q * 32:j * ROWS + (q + 1) * 32, :]
                for side in range(2)
                for i, j in PLACE
            ],
            axis=0,
        )
        t = jnp.dot(ph, x, preferred_element_type=f32)
        for part in range(2):
            for v in range(2 * PER):
                y_ref[part, v, pl.ds(q, KPTS, stride=2), :] = t[
                    part * KPTS:(part + 1) * KPTS, v * 128:(v + 1) * 128
                ]
    for v in range(2 * PER):
        rows = slice(v * 128, (v + 1) * 128)
        xr, xi = (y_ref[part, v].T.astype(bf16).astype(f32) for part in range(2))
        bl_ref[0, rows, :] = xr + xi
        bl_ref[1, rows, :] = xr
        bl_ref[2, rows, :] = xi

    group = 8

    def first(i, _):
        base = i * group * BANDS
        acc = [[jnp.zeros((16, 128), f32) for _ in range(3)] for _ in range(group)]
        for b in range(BANDS):
            us = [u_ref[t, b] for t in range(3)]
            for s in range(group):
                for t in range(3):
                    acc[s][t] = acc[s][t] + bl_ref[t, pl.ds(base + s * BANDS + b, 1), :] * us[t]
        for s in range(group):
            hr = (acc[s][0] - acc[s][2]).astype(bf16).astype(f32)
            hi = (acc[s][0] + acc[s][1]).astype(bf16).astype(f32)
            h_ref[0, i * group + s] = hr + hi
            h_ref[1, i * group + s] = hr
            h_ref[2, i * group + s] = hi
        return 0

    lax.fori_loop(0, PER * BANDS // group, first, 0)

    per = BANDS // group

    def second(i, _):
        n = i // per
        c0 = (i - n * per) * group
        acc = [[jnp.zeros((16, 128), f32) for _ in range(3)] for _ in range(group)]
        for a in range(BANDS):
            hs = [h_ref[t, n * BANDS + a] for t in range(3)]
            for s in range(group):
                for t in range(3):
                    acc[s][t] = acc[s][t] + l_ref[t, a, pl.ds(c0 + s, 1), :] * hs[t]
        for s in range(group):
            r_ref[0, i * group + s] = acc[s][0] - acc[s][2]
            r_ref[1, i * group + s] = acc[s][0] + acc[s][1]
        return 0

    lax.fori_loop(0, PER * per, second, 0)
    for part in range(2):
        for v in range(2 * PER):
            tile = r_ref[part, v * 8:(v + 1) * 8].reshape(128, 128).T
            out_ref[part, :, :, v * 128:(v + 1) * 128] = tile.reshape(KPTS, NQ, 128).astype(bf16)


def vmem():
    return pl.BlockSpec(memory_space=pltpu.VMEM)


def hbm():
    return pl.BlockSpec(memory_space=pltpu.HBM)


def smem():
    return pl.BlockSpec(memory_space=pltpu.SMEM)


def params():
    return pltpu.CompilerParams(vmem_limit_bytes=40 << 20)


def per_device(
    coarse,
    rp_vectors,
    rp_weights,
    re_vectors,
    re_weights,
    q_points,
    k_points,
    modes_rot,
    u_k,
    u_kq,
    mask_k,
    mask_kq,
):
    rotated = pl.pallas_call(
        rotate_body,
        out_shape=jax.ShapeDtypeStruct((LAT, ROWS, LANES), bf16),
        in_specs=[hbm()] * 5,
        out_specs=vmem(),
        scratch_shapes=[
            pltpu.SMEM((NQ, 3), f32),
            pltpu.SMEM((1, 3), jnp.int32),
            pltpu.SMEM((1, 1), jnp.int32),
            pltpu.VMEM((2, NQ, MODES, MODES), bf16),
            pltpu.VMEM((2, CELLS, MODES * BANDS * BANDS), bf16),
            pltpu.VMEM((192, 128), f32),
            pltpu.VMEM((2, CELLS * STRIDE_S, 128), f32),
            pltpu.VMEM((2 * PER, LAT * STRIDE_O, 128), f32),
            pltpu.SemaphoreType.DMA((4 + 2 * CHUNKS,)),
        ],
        compiler_params=pltpu.CompilerParams(vmem_limit_bytes=40 << 20),
        name="rotate",
    )(
        pltpu.with_memory_space_constraint(q_points, pltpu.HBM),
        pltpu.with_memory_space_constraint(rp_vectors, pltpu.HBM),
        rp_weights[None, :],
        pltpu.with_memory_space_constraint(modes_rot, pltpu.HBM),
        pltpu.with_memory_space_constraint(coarse, pltpu.HBM),
    )
    parts = lax.all_to_all(rotated, "lat", 0, 0, tiled=True)

    given = (
        k_points.T,
        re_vectors.T,
        re_weights[None, :],
        jnp.transpose(u_k, (0, 2, 3, 1)).reshape(2, BANDS * BANDS, KPTS),
        jnp.transpose(u_kq, (0, 1, 3, 4, 2)).reshape(2, NQ, BANDS * BANDS, KPTS),
        mask_k.T,
        jnp.transpose(mask_kq, (0, 2, 1)),
    )
    phase, right, left = pl.pallas_call(
        prep_body,
        out_shape=(
            jax.ShapeDtypeStruct((2 * KPTS, 512), bf16),
            jax.ShapeDtypeStruct((3, BANDS, BANDS, 128), f32),
            jax.ShapeDtypeStruct((3, BANDS, BANDS, 128), f32),
        ),
        in_specs=[hbm()] * 7,
        out_specs=(vmem(),) * 3,
        scratch_shapes=[pltpu.VMEM(x.shape, x.dtype) for x in given]
        + [pltpu.SemaphoreType.DMA((len(given),))],
        compiler_params=params(),
        name="prep",
    )(*(pltpu.with_memory_space_constraint(x, pltpu.HBM) for x in given))

    own = pl.pallas_call(
        sum_body,
        out_shape=jax.ShapeDtypeStruct((ROWS, LANES), bf16),
        in_specs=[vmem()],
        out_specs=vmem(),
        compiler_params=params(),
        name="add_up",
    )(parts)

    def shift(x, step):
        return lax.ppermute(x, "kpt", [(i, (i + 2 * step) % 16) for i in range(16)])

    def swap(x):
        return lax.ppermute(x, "kpt", [(i, i ^ 1) for i in range(16)])

    back = shift(own, 3)
    ahead = shift(own, -2)
    packed, pair = pl.pallas_call(
        pack_body,
        out_shape=(
            jax.ShapeDtypeStruct((3 * ROWS, LANES), bf16),
            jax.ShapeDtypeStruct((2 * ROWS, LANES), bf16),
        ),
        in_specs=[vmem()] * 3 + [pl.BlockSpec(memory_space=pl.ANY)],
        out_specs=(vmem(), vmem()),
        compiler_params=params(),
        name="pack",
    )(own, back, ahead, phase)
    plus = shift(packed, 1)
    minus = shift(pair, -1)
    near = [packed, plus, minus]
    far = [swap(x) for x in near]

    result = pl.pallas_call(
        couple_body,
        out_shape=jax.ShapeDtypeStruct((2, KPTS, NQ, LANES), bf16),
        in_specs=[vmem()] * 9,
        out_specs=vmem(),
        scratch_shapes=[
            pltpu.VMEM((2, 2 * PER, 128, 128), f32),
            pltpu.VMEM((3, LANES, 128), f32),
            pltpu.VMEM((3, PER * BANDS, BANDS, 128), f32),
            pltpu.VMEM((2, PER * BANDS, BANDS, 128), f32),
        ],
        compiler_params=params(),
        name="couple",
    )(*near, *far, phase, right, left)
    return result


def solution(mesh):
    placed = (
        P(None, "lat", "kpt", None),
        P("lat", None),
        P("lat"),
        P(),
        P(),
        P(),
        P("kpt", None),
        P(),
        P(None, "kpt", None, None),
        P(None, None, "kpt", None, None),
        P("kpt", None),
        P(None, "kpt", None),
    )
    return jax.shard_map(
        per_device,
        mesh=mesh,
        in_specs=placed,
        out_specs=P(None, "kpt", None, "lat"),
        check_vma=False,
    )
```
